32 devices in a mesh: tm: 8 (over z, y), space: 4 (over x, core).
Axes of the slice: x: 2, y: 2, z: 4, core: 2. Of those that a mesh axis runs over, the one named last changes fastest.
Arguments:
- controls: bfloat16 [32, 64, 2048], P('tm', None, 'space'), may hold values from -4 to 4
- target: bfloat16 [64, 2048], P(None, 'space'), may hold values from -4 to 4
- state_in: float32 [8, 64, 2048], P('tm', None, 'space'), may hold values from -2.5 to 2.5
- adjoint_in: float32 [8, 64, 2048], P('tm', None, 'space'), may hold values from -5 to 5
- block_inverse: bfloat16 [64, 64, 2048], P(None, None, 'space'), may hold values from -1 to 1
- numbering: int32 [4, 512], P('space'), may hold values from 0 to 511, each once within a row
Outputs:
- new_controls: bfloat16 [32, 64, 2048], P('tm', None, 'space')
- next_state: float32 [8, 64, 2048], P('tm', None, 'space')
- next_adjoint: float32 [8, 64, 2048], P('tm', None, 'space')
- objective: float32 [], replicated
The draws below stay inside these ranges and needn't reach their ends.
Inputs may be any that keep to these rules, and one draw needn't show every extreme that they name: `numbering`: each row names every structural element of its slab exactly once.
All inputs are finite; a program needn't handle non-finite values.
Results may differ from the reference program's by a relative error of at most 0.0085.
Values may be sent and summed in bfloat16 or wider, within the bound.
A program may use at most 128 MiB of HBM per device.

```python
import math
import jax
import jax.numpy as jnp
from jax import lax

NSIDE = 4
NODES = 64
EXY = 16
ELAYERS = 2
STEP_DEV = 4
E_DEV = 512
ELEMENTS = 2048
SLABS = 4
TSLICES = 8
STEPS = 32


def draw_block_inverse(key, part):
    first_key, second_key = jax.random.split(key)
    dims = (NODES, NODES, ELEMENTS)
    spread = jax.random.truncated_normal(first_key, -4.0, 4.0, dims, jnp.float32) * (0.15 / NODES ** 0.5)
    diagonal = jnp.exp(jax.random.uniform(second_key, (NODES, ELEMENTS), jnp.float32, math.log(0.55), 0.0))
    row_index = lax.broadcasted_iota(jnp.int32, (NODES, NODES), 0)
    column_index = lax.broadcasted_iota(jnp.int32, (NODES, NODES), 1)
    unit_mask = (row_index == column_index).astype(jnp.float32)[:, :, None]
    return (spread * (1.0 - unit_mask) + unit_mask * diagonal[None, :, :]).astype(jnp.bfloat16)


def block_scale(stream_key, extent, pieces, smallest, top_value):
    level, own = 1.0, jax.random.fold_in(stream_key, 6)
    for dim, shards_of in pieces:
        heights = jnp.exp(jax.random.uniform(jax.random.fold_in(own, dim), (shards_of,), jnp.float32, smallest / len(pieces), top_value / len(pieces)))
        level = level * jnp.repeat(heights, extent[dim] // shards_of).reshape([-1 if axis == dim else 1 for axis in range(len(extent))])
    return level


def normal_values(own_key, extent, deviation, bound, cuts=(), held_as=jnp.bfloat16):
    level = block_scale(own_key, extent, cuts, -0.22, 0.18) if cuts else 1.0
    values = jax.random.normal(own_key, extent, jnp.float32) * deviation * level
    return jnp.minimum(jnp.maximum(values, -bound), bound).astype(held_as)


def setup_inputs(seed: int = 0) -> dict:
    splits = jax.random.split(jax.random.key(seed), 7)
    controls = normal_values(splits[0], (STEPS, NODES, ELEMENTS), 1.0, 4.0, ((0, 8), (2, 4)))
    target = normal_values(splits[1], (NODES, ELEMENTS), 1.0, 4.0, ((1, 4),))
    state_in = normal_values(splits[2], (TSLICES, NODES, ELEMENTS), 0.5, 2.5, ((0, 8), (2, 4)), jnp.float32)
    adjoint_in = normal_values(splits[3], (TSLICES, NODES, ELEMENTS), 1.0, 5.0, ((0, 8), (2, 4)), jnp.float32)
    block_inverse = draw_block_inverse(jax.random.fold_in(splits[6], 71), 0)
    numbering = jax.vmap(lambda own: jax.random.permutation(own, E_DEV))(jax.random.split(splits[5], SLABS)).reshape((SLABS, E_DEV)).astype(jnp.int32)
    return {"controls": controls, "target": target, "state_in": state_in, "adjoint_in": adjoint_in, "block_inverse": block_inverse, "numbering": numbering}


TIME_STEP = 0.1
PENALTY = 0.5
REGULAR = 0.1


def shift_layers(traces, upward):
    empty = jnp.zeros_like(traces[:, :, :, :1])
    if upward:
        return jnp.concatenate([empty, traces[:, :, :, :-1]], axis=3)
    return jnp.concatenate([traces[:, :, :, 1:], empty], axis=3)


def face_jumps(values, node_side, layers_all, width):
    leading = values.shape[0]
    tensor = values.reshape(leading, node_side, node_side, node_side, layers_all, width, width)
    last = node_side - 1
    west = jnp.roll(tensor[:, :, :, last], 1, axis=-1) - tensor[:, :, :, 0]
    east = jnp.roll(tensor[:, :, :, 0], -1, axis=-1) - tensor[:, :, :, last]
    south = jnp.roll(tensor[:, :, last], 1, axis=-2) - tensor[:, :, 0]
    north = jnp.roll(tensor[:, :, 0], -1, axis=-2) - tensor[:, :, last]
    lower = shift_layers(tensor[:, last], True) - tensor[:, 0]
    upper = shift_layers(tensor[:, 0], False) - tensor[:, last]
    total = jnp.zeros_like(tensor)
    total = total.at[:, :, :, 0].add(west)
    total = total.at[:, :, :, last].add(east)
    total = total.at[:, :, 0].add(south)
    total = total.at[:, :, last].add(north)
    total = total.at[:, 0].add(lower)
    total = total.at[:, last].add(upper)
    return total.reshape(values.shape)


def reference(controls, target, state_in, adjoint_in, block_inverse, numbering):
    slabs, per_slab = numbering.shape
    rows = jnp.broadcast_to(jnp.arange(slabs, dtype=jnp.int32)[:, None], (slabs, per_slab))
    columns = jnp.broadcast_to(jnp.arange(per_slab, dtype=jnp.int32)[None, :], (slabs, per_slab))
    inverse = jnp.zeros((slabs, per_slab), jnp.int32).at[rows, numbering].set(columns)
    to_struct = (rows * per_slab + inverse).reshape(-1).astype(jnp.int32)
    to_store = (rows * per_slab + numbering).reshape(-1).astype(jnp.int32)
    layers_all = slabs * ELAYERS
    slices = state_in.shape[0]
    blocks = jnp.take(block_inverse, to_struct, axis=-1).astype(jnp.float32)
    goal = jnp.take(target, to_struct, axis=-1).astype(jnp.float32)
    control_all = jnp.take(controls, to_struct, axis=-1).astype(jnp.float32)
    control_all = control_all.reshape(slices, STEP_DEV, NODES, ELEMENTS)
    state = jnp.take(state_in, to_struct, axis=-1)
    start_adjoint = jnp.take(adjoint_in, to_struct, axis=-1)
    first_steps = (jnp.arange(slices, dtype=jnp.int32) * STEP_DEV).astype(jnp.float32)[:, None, None]

    def jumps(values):
        return face_jumps(values, NSIDE, layers_all, EXY)

    def forward_apply(right_side):
        return jnp.einsum("ije,tje->tie", blocks, right_side.astype(jnp.float32), precision=lax.Precision.HIGHEST)

    def backward_apply(vector):
        return jnp.einsum("ije,tie->tje", blocks, vector.astype(jnp.float32), precision=lax.Precision.HIGHEST)

    history = [state]
    misfit = jnp.float32(0.0)
    for index_k in range(STEP_DEV):
        control_now = control_all[:, index_k]
        right_side = (state + TIME_STEP * (state - state * state * state) + TIME_STEP * PENALTY * jumps(state)
                      + TIME_STEP * control_now).astype(jnp.bfloat16)
        state = forward_apply(right_side)
        history.append(state)
        weight = (first_steps + (index_k + 1)) / STEPS
        misfit = misfit + jnp.sum(weight * (state - goal) ** 2)
    regular_sum = jnp.sum(control_all * control_all)
    objective = (0.5 * misfit + 0.5 * REGULAR * regular_sum) / (STEPS * NODES * ELEMENTS)

    adjoint = (first_steps + STEP_DEV) / STEPS * (history[-1] - goal) + start_adjoint
    updated = [None] * STEP_DEV
    carried = adjoint
    for index_k in reversed(range(STEP_DEV)):
        pulled = backward_apply(adjoint.astype(jnp.bfloat16))
        control_now = control_all[:, index_k]
        updated[index_k] = (control_now - (TIME_STEP * pulled + REGULAR * control_now)).astype(jnp.bfloat16)
        before = history[index_k]
        carried = pulled + TIME_STEP * (1.0 - 3.0 * before * before) * pulled + TIME_STEP * PENALTY * jumps(pulled)
        if index_k > 0:
            weight = (first_steps + index_k) / STEPS
            adjoint = weight * (before - goal) + carried
    new_controls = jnp.stack(updated, axis=1).reshape(STEPS, NODES, ELEMENTS)
    new_controls = jnp.take(new_controls, to_store, axis=-1)
    next_state = jnp.concatenate([history[0][:1], history[-1][:-1]], axis=0)
    next_state = jnp.take(next_state, to_store, axis=-1)
    next_adjoint = jnp.concatenate([carried[1:], jnp.zeros_like(carried[:1])], axis=0)
    next_adjoint = jnp.take(next_adjoint, to_store, axis=-1)
    return new_controls, next_state, next_adjoint, objective
```

```python
import functools

import jax
import jax.numpy as jnp
from jax import lax
from jax.experimental import pallas as pl
from jax.experimental.pallas import tpu as pltpu
from jax.sharding import PartitionSpec as P

NSIDE = 4
EXY = 16
BLOCK = NSIDE * NSIDE
HALF = 2 * BLOCK
LAYER = EXY * EXY
TIME_STEP = 0.1
PENALTY = 0.5
REGULAR = 0.1
F32 = jnp.float32
BF16 = jnp.bfloat16
RIM, MID = 0, 1
WIDE = 256


def dot(a, b):
    return jnp.dot(a, b, preferred_element_type=F32)


def rows_of(half):
    if half == RIM:
        return ((0, BLOCK), (3 * BLOCK, BLOCK))
    return ((BLOCK, BLOCK), (2 * BLOCK, BLOCK))


def take(ref, half, *lead):
    return jnp.concatenate([ref[lead + (slice(s, s + n),)] for s, n in rows_of(half)], axis=0)


def put(ref, half, value, *lead):
    at = 0
    for s, n in rows_of(half):
        ref[lead + (slice(s, s + n),)] = value[at : at + n]
        at += n


def fold(x):
    total = None
    for i in range(0, x.shape[0], 8):
        for j in range(0, x.shape[1], 128):
            piece = x[i : i + 8, j : j + 128]
            total = piece if total is None else total + piece
    return total


def lateral(x):
    rows, lanes = x.shape
    q = lax.broadcasted_iota(jnp.int32, x.shape, 0)
    s = lax.broadcasted_iota(jnp.int32, x.shape, 1)
    a, b = q % NSIDE, (q // NSIDE) % NSIDE
    col, row = s % EXY, (s // EXY) % EXY
    last = NSIDE - 1

    def along(which, node_step, place, lane_step):
        back = (EXY - 1) * lane_step
        low = which == 0
        z = jnp.where(low, pltpu.roll(x, rows - last * node_step, 0), pltpu.roll(x, last * node_step, 0))
        down = jnp.where(place == 0, pltpu.roll(z, lanes - back, 1), pltpu.roll(z, lane_step, 1))
        up = jnp.where(place == EXY - 1, pltpu.roll(z, back, 1), pltpu.roll(z, lanes - lane_step, 1))
        return jnp.where(low, down, jnp.where(which == last, up, 0.0))

    return along(a, 1, col, 1) + along(b, NSIDE, row, EXY)


def faces(half, shape):
    q = lax.broadcasted_iota(jnp.int32, shape, 0)
    a, b = q % NSIDE, (q // NSIDE) % NSIDE
    last = NSIDE - 1
    count = jnp.where((a == 0) | (a == last), 1.0, 0.0) + jnp.where((b == 0) | (b == last), 1.0, 0.0)
    return count + (1.0 if half == RIM else 0.0)


def kernel(
    n_space, n_tm,
    num_ref, ctl_hbm, tgt_hbm, st_hbm, adj_hbm, a_hbm,
    newc_ref, nst_ref, nadj_ref, obj_ref,
    a_ref, ctl, tgt, adj, st, hist, goal, r_ref, gf, pulled, part, xr, pa, pt,
    cost, rim_out, rim_in, st_out, st_in, adj_out, adj_in, slot_s, tree_out, tree_in,
    in_sem, a_sem, rim_send, rim_recv, st_sem, adj_send_sem, adj_recv_sem,
    ss_send, ss_recv, tt_send, tt_recv,
):
    steps = ctl.shape[0]
    elements = ctl.shape[2]
    nodes = ctl.shape[1]
    me = lax.axis_index("space")
    t = lax.axis_index("tm")
    first = t * steps
    total_steps = steps * n_tm

    def weight(k):
        return (first + k).astype(F32) / total_steps

    loads = [
        pltpu.make_async_copy(src, dst, in_sem.at[i])
        for i, (src, dst) in enumerate(
            ((st_hbm.at[0], st), (ctl_hbm, ctl), (tgt_hbm, tgt), (adj_hbm.at[0], adj))
        )
    ]
    for c in loads:
        c.start()
    parts = a_sem.shape[0]
    chunk = nodes // parts
    a_loads = [
        pltpu.make_async_copy(a_hbm.at[pl.ds(i * chunk, chunk)], a_ref.at[pl.ds(i * chunk, chunk)], a_sem.at[i])
        for i in range(parts)
    ]
    for c in a_loads:
        c.start()

    rim_in[...] = jnp.zeros_like(rim_in)
    barrier = pltpu.get_barrier_semaphore()
    for d in range(1, n_space):
        pl.semaphore_signal(barrier, inc=1, device_id={"space": lax.rem(me + d, n_space)},
                            device_id_type=pl.DeviceIdType.MESH)
    bits = (n_tm - 1).bit_length()

    def partner(j):
        size = 2**j
        return t + size - 2 * size * ((t // size) % 2)

    def greet(peer):
        pl.semaphore_signal(barrier, inc=1, device_id={"tm": peer}, device_id_type=pl.DeviceIdType.MESH)

    for j in range(bits):
        greet(partner(j))

    @pl.when(t > 0)
    def _():
        greet(t - 1)

    @pl.when(t < n_tm - 1)
    def _():
        greet(t + 1)

    beside = jnp.where(t > 0, 1, 0) + jnp.where(t < n_tm - 1, 1, 0)

    for i in range(0, elements, WIDE):
        place = lax.broadcasted_iota(jnp.int32, (WIDE, elements), 0) + i
        hot = jnp.where(num_ref[...] == place, 1.0, 0.0)
        pt[i : i + WIDE, :] = hot.astype(BF16)
        pa[:, i : i + WIDE] = hot.T.astype(BF16)

    cost[...] = jnp.zeros_like(cost)

    def arrange(x):
        return dot(x.astype(BF16), pa[...])

    def restore(x):
        return dot(x.astype(BF16), pt[...])

    def rim_copy(rnd, side):
        peer = me - 1 if side == 0 else me + 1
        return pltpu.make_async_remote_copy(
            src_ref=rim_out.at[rnd, side], dst_ref=rim_in.at[rnd, 1 - side],
            send_sem=rim_send.at[rnd, side], recv_sem=rim_recv.at[rnd, 1 - side],
            device_id={"space": peer}, device_id_type=pl.DeviceIdType.MESH,
        )

    def send_rims(rnd, x):
        rim_out[rnd, 0] = x[:BLOCK, :LAYER].astype(BF16)
        rim_out[rnd, 1] = x[BLOCK:, elements - LAYER :].astype(BF16)

        @pl.when(me > 0)
        def _():
            rim_copy(rnd, 0).start()

        @pl.when(me < n_space - 1)
        def _():
            rim_copy(rnd, 1).start()

    def arrival(rnd, side):
        peer = me - 1 if side == 0 else me + 1
        return pltpu.make_async_remote_copy(
            src_ref=rim_out.at[rnd, side], dst_ref=rim_in.at[rnd, side],
            send_sem=rim_send.at[rnd, side], recv_sem=rim_recv.at[rnd, side],
            device_id={"space": peer}, device_id_type=pl.DeviceIdType.MESH,
        )

    def wait_rims(rnd):
        @pl.when(me > 0)
        def _():
            arrival(rnd, 0).wait()

        @pl.when(me < n_space - 1)
        def _():
            arrival(rnd, 1).wait()

    def rim_neighbours(rnd, x, lat):
        below = jnp.concatenate([rim_in[rnd, 0].astype(F32), x[BLOCK:, : elements - LAYER]], axis=1)
        above = jnp.concatenate([x[:BLOCK, LAYER:], rim_in[rnd, 1].astype(F32)], axis=1)
        return restore(lat + jnp.concatenate([below, above], axis=0))

    depth = BLOCK * BLOCK
    place_k = lax.broadcasted_iota(jnp.int32, (BLOCK, depth), 1)
    place_r = lax.broadcasted_iota(jnp.int32, (BLOCK, depth), 0)
    sum_rows = jnp.where(place_k // BLOCK == place_r, 1.0, 0.0).astype(BF16)
    sum_groups = jnp.where(place_k % BLOCK == place_r, 1.0, 0.0).astype(BF16)

    def apply(out_half, in_half, write):
        (s0, _), (s1, _) = rows_of(in_half)
        for n0 in range(0, elements, WIDE):
            lanes = slice(n0, n0 + WIDE)
            r0, r1 = r_ref[in_half, :BLOCK, lanes], r_ref[in_half, BLOCK:, lanes]
            for at, (i0, _) in enumerate(rows_of(out_half)):
                q = (
                    a_ref[i0 : i0 + BLOCK, s0 : s0 + BLOCK, lanes] * r0[None]
                    + a_ref[i0 : i0 + BLOCK, s1 : s1 + BLOCK, lanes] * r1[None]
                )
                write(slice(at * BLOCK, (at + 1) * BLOCK), lanes, dot(sum_rows, q.reshape(depth, WIDE)))

    def apply_t(out_half, in_half, write):
        nodes_in = [s + i for s, n in rows_of(in_half) for i in range(n)]
        for n0 in range(0, elements, WIDE):
            lanes = slice(n0, n0 + WIDE)
            spread = [
                jnp.broadcast_to(gf[in_half, i : i + 1, lanes], (BLOCK, WIDE)).astype(BF16) for i in range(HALF)
            ]
            for at, (s, _) in enumerate(rows_of(out_half)):
                pieces = [
                    a_ref[nodes_in[i], s : s + BLOCK, lanes] * spread[i]
                    + a_ref[nodes_in[i + 1], s : s + BLOCK, lanes] * spread[i + 1]
                    for i in range(0, HALF, 2)
                ]
                write(slice(at * BLOCK, (at + 1) * BLOCK), lanes, dot(sum_groups, jnp.concatenate(pieces, axis=0)))

    shape = (HALF, elements)

    def rhs(half, u, n, control):
        return (
            u + TIME_STEP * (u - u * u * u)
            + TIME_STEP * PENALTY * (n - faces(half, shape) * u)
            + TIME_STEP * control
        ).astype(BF16)

    loads[0].wait()
    for half in (RIM, MID):
        hist[0, half] = take(st, half)
    x0 = arrange(hist[0, RIM])
    xr[...] = x0
    pl.semaphore_wait(barrier, n_space - 1 + bits + beside)
    send_rims(0, x0)
    for c in loads[1:]:
        c.wait()
    for half in (RIM, MID):
        goal[half] = take(tgt, half).astype(F32)

    def forward(k, carry):
        um = hist[k, MID]
        nm = restore(lateral(arrange(um)))
        cm = take(ctl, MID, k).astype(F32)
        cr = take(ctl, RIM, k).astype(F32)
        r_ref[MID] = rhs(MID, um, nm, cm)
        x = xr[...]
        lat = lateral(x)

        @pl.when(k == 0)
        def _():
            for c in a_loads:
                c.wait()

        for out in (RIM, MID):
            def write(rows, lanes, v, out=out):
                hist[k + 1, out, rows, lanes] = v
            apply(out, MID, write)
        ur = hist[k, RIM]
        w = jnp.where(k > 0, weight(k), 0.0)
        dm, dr = um - goal[MID], ur - goal[RIM]
        cost[...] += 0.5 * w * fold(dm * dm + dr * dr) + 0.5 * REGULAR * fold(cm * cm + cr * cr)

        wait_rims(k)
        nr = rim_neighbours(k, x, lat)
        r_ref[RIM] = rhs(RIM, ur, nr, cr)

        def add(out):
            def write(rows, lanes, v):
                hist[k + 1, out, rows, lanes] += v
            return write

        apply(RIM, RIM, add(RIM))

        @pl.when(k < steps - 1)
        def _():
            y = arrange(hist[k + 1, RIM])
            xr[...] = y
            send_rims(k + 1, y)

        apply(MID, RIM, add(MID))
        return carry

    lax.fori_loop(0, steps, forward, 0)

    w_end = weight(steps)
    for half in (MID, RIM):
        u = hist[steps, half]
        d = u - goal[half]
        cost[...] += 0.5 * w_end * fold(d * d)
        gf[half] = w_end * d + take(adj, half)
        st_out[half] = u.astype(BF16)

    def st_copy(dst):
        return pltpu.make_async_remote_copy(
            src_ref=st_out, dst_ref=st_in, send_sem=st_sem.at[0], recv_sem=st_sem.at[1],
            device_id={"tm": dst}, device_id_type=pl.DeviceIdType.MESH)

    @pl.when(t < n_tm - 1)
    def _():
        st_copy(t + 1).start()

    slot_s[me] = cost[...]

    def gather_copy(slots, send, recv, axis, index, count, d):
        return pltpu.make_async_remote_copy(
            src_ref=slots.at[index], dst_ref=slots.at[index], send_sem=send.at[d], recv_sem=recv.at[index],
            device_id={axis: lax.rem(index + d, count)}, device_id_type=pl.DeviceIdType.MESH)

    def gather_wait(slots, send, recv, axis, index, count, d):
        gather_copy(slots, send, recv, axis, index, count, d).wait_send()
        origin = lax.rem(index + d, count)
        pltpu.make_async_remote_copy(
            src_ref=slots.at[origin], dst_ref=slots.at[origin], send_sem=send.at[d], recv_sem=recv.at[origin],
            device_id={axis: origin}, device_id_type=pl.DeviceIdType.MESH).wait_recv()

    over_s = (slot_s, ss_send, ss_recv, "space", me, n_space)

    def tree_copy(j):
        return pltpu.make_async_remote_copy(
            src_ref=tree_out.at[j], dst_ref=tree_in.at[j], send_sem=tt_send.at[j], recv_sem=tt_recv.at[j],
            device_id={"tm": partner(j)}, device_id_type=pl.DeviceIdType.MESH)

    def tree_sum(j):
        if j == 0:
            for d in range(1, n_space):
                gather_wait(*over_s, d)
            total = slot_s[0]
            for i in range(1, n_space):
                total = total + slot_s[i]
            return total
        tree_copy(j - 1).wait()
        return tree_out[j - 1] + tree_in[j - 1]

    def tree_stage(j):
        tree_out[j] = tree_sum(j)
        tree_copy(j).start()

    early = min(bits, steps - 1)
    for d in range(1, n_space):
        gather_copy(*over_s, d).start()

    def part_write(out):
        def write(rows, lanes, v):
            part[out, rows, lanes] = v
        return write

    def pulled_write(out):
        def write(rows, lanes, v):
            pulled[out, rows, lanes] = part[out, rows, lanes] + v
        return write

    def finish(rnd):
        apply_t(RIM, RIM, pulled_write(RIM))
        y = arrange(pulled[RIM])
        xr[...] = y
        send_rims(rnd, y)
        apply_t(MID, RIM, pulled_write(MID))

    def carry_back(half, k, p, n):
        before = hist[k, half]
        carried = (
            p + TIME_STEP * (1.0 - 3.0 * before * before) * p
            + TIME_STEP * PENALTY * (n - faces(half, shape) * p)
        )
        return before, carried

    def update(half, k, p):
        control = take(ctl, half, k).astype(F32)
        put(newc_ref, half, (control - (TIME_STEP * p + REGULAR * control)).astype(BF16), k)

    apply_t(RIM, MID, part_write(RIM))
    apply_t(MID, MID, part_write(MID))
    finish(steps)

    def backward(i, carry):
        k = steps - 1 - i
        rnd = steps + i
        pm = pulled[MID]
        nm = restore(lateral(arrange(pm)))
        before, carried = carry_back(MID, k, pm, nm)
        gf[MID] = weight(k) * (before - goal[MID]) + carried
        x = xr[...]
        lat = lateral(x)
        apply_t(RIM, MID, part_write(RIM))
        apply_t(MID, MID, part_write(MID))
        pr = pulled[RIM]
        update(MID, k, pm)
        update(RIM, k, pr)

        for j in range(early):
            pl.when(i == j)(functools.partial(tree_stage, j))

        wait_rims(rnd)
        nr = rim_neighbours(rnd, x, lat)
        before_r, carried_r = carry_back(RIM, k, pr, nr)
        gf[RIM] = weight(k) * (before_r - goal[RIM]) + carried_r
        finish(rnd + 1)
        return carry

    lax.fori_loop(0, steps - 1, backward, 0)

    def adj_copy(dst, half):
        return pltpu.make_async_remote_copy(
            src_ref=adj_out.at[half], dst_ref=adj_in.at[half], send_sem=adj_send_sem.at[half],
            recv_sem=adj_recv_sem.at[half], device_id={"tm": dst}, device_id_type=pl.DeviceIdType.MESH)

    def send_adj(half, carried):
        adj_out[half] = carried.astype(adj_out.dtype)

        @pl.when(t > 0)
        def _():
            adj_copy(t - 1, half).start()

    rnd = 2 * steps - 1
    pm, pr = pulled[MID], pulled[RIM]
    nm = restore(lateral(arrange(pm)))
    send_adj(MID, carry_back(MID, 0, pm, nm)[1])
    x = xr[...]
    lat = lateral(x)
    wait_rims(rnd)
    nr = rim_neighbours(rnd, x, lat)
    send_adj(RIM, carry_back(RIM, 0, pr, nr)[1])
    update(MID, 0, pm)
    update(RIM, 0, pr)

    @pl.when(t == 0)
    def _():
        nst_ref[0] = st[...]

    @pl.when(t > 0)
    def _():
        st_copy(t - 1).wait_recv()
        for half in (RIM, MID):
            put(nst_ref, half, st_in[half].astype(F32), 0)

    @pl.when(t < n_tm - 1)
    def _():
        st_copy(t + 1).wait_send()

    for j in range(early, bits):
        tree_stage(j)
    total = tree_sum(bits)
    obj_ref[0, 0] = jnp.sum(total) * (1.0 / (total_steps * nodes * elements * n_space))

    @pl.when(t == n_tm - 1)
    def _():
        nadj_ref[...] = jnp.zeros_like(nadj_ref)

    @pl.when(t < n_tm - 1)
    def _():
        for half in (MID, RIM):
            adj_copy(t + 1, half).wait_recv()
            put(nadj_ref, half, adj_in[half].astype(F32), 0)

    @pl.when(t > 0)
    def _():
        for half in (MID, RIM):
            adj_copy(t - 1, half).wait_send()


def store_kernel(count, *refs):
    outs = refs[count + 1 : 2 * count + 1]
    held = refs[2 * count + 2 : 3 * count + 2]
    sems = refs[-1]
    takes = [pltpu.make_async_copy(refs[i], held[i], sems.at[0, i]) for i in range(count)]
    gives = [pltpu.make_async_copy(held[i], outs[i], sems.at[1, i]) for i in range(count)]
    for c in takes:
        c.start()
    refs[2 * count + 1][0, 0] = refs[count][0, 0]
    for take_one, give in zip(takes, gives):
        take_one.wait()
        give.start()
    for c in gives:
        c.wait()


def store(values, scalar):
    count = len(values)
    smem = pl.BlockSpec(memory_space=pltpu.SMEM)
    return pl.pallas_call(
        functools.partial(store_kernel, count),
        out_shape=tuple(jax.ShapeDtypeStruct(v.shape, v.dtype) for v in values + (scalar,)),
        in_specs=[pl.BlockSpec(memory_space=pltpu.HBM)] * count + [smem],
        out_specs=(pl.BlockSpec(memory_space=pltpu.HBM),) * count + (smem,),
        scratch_shapes=[pltpu.VMEM(v.shape, v.dtype) for v in values] + [pltpu.SemaphoreType.DMA((2, count))],
        compiler_params=pltpu.CompilerParams(vmem_limit_bytes=67043328),
    )(*values, scalar)


def solution(mesh):
    n_space, n_tm = mesh.shape["space"], mesh.shape["tm"]

    def per_device(controls, target, state_in, adjoint_in, block_inverse, numbering):
        steps, nodes, elements = controls.shape
        vm = pl.BlockSpec(memory_space=pltpu.VMEM)
        hbm = pl.BlockSpec(memory_space=pltpu.HBM)
        halves = (2, HALF, elements)
        rounds = 2 * steps
        bits = (n_tm - 1).bit_length()
        dma = pltpu.SemaphoreType.DMA
        new_controls, next_state, next_adjoint, objective = pl.pallas_call(
            functools.partial(kernel, n_space, n_tm),
            out_shape=(
                jax.ShapeDtypeStruct(controls.shape, BF16),
                jax.ShapeDtypeStruct(state_in.shape, F32),
                jax.ShapeDtypeStruct(adjoint_in.shape, F32),
                jax.ShapeDtypeStruct((1, 1), F32),
            ),
            in_specs=[vm, hbm, hbm, hbm, hbm, hbm],
            out_specs=(vm, vm, vm, pl.BlockSpec(memory_space=pltpu.SMEM)),
            scratch_shapes=[
                pltpu.VMEM(block_inverse.shape, BF16),
                pltpu.VMEM(controls.shape, BF16),
                pltpu.VMEM(target.shape, BF16),
                pltpu.VMEM(adjoint_in.shape[1:], F32),
                pltpu.VMEM(state_in.shape[1:], F32),
                pltpu.VMEM((steps + 1,) + halves, F32),
                pltpu.VMEM(halves, F32),
                pltpu.VMEM(halves, BF16),
                pltpu.VMEM(halves, F32),
                pltpu.VMEM(halves, F32),
                pltpu.VMEM(halves, F32),
                pltpu.VMEM(halves[1:], F32),
                pltpu.VMEM((elements, elements), BF16),
                pltpu.VMEM((elements, elements), BF16),
                pltpu.VMEM((8, 128), F32),
                pltpu.VMEM((rounds, 2, BLOCK, LAYER), BF16),
                pltpu.VMEM((rounds, 2, BLOCK, LAYER), BF16),
                pltpu.VMEM(halves, BF16),
                pltpu.VMEM(halves, BF16),
                pltpu.VMEM(halves, BF16),
                pltpu.VMEM(halves, BF16),
                pltpu.VMEM((n_space, 8, 128), F32),
                pltpu.VMEM((bits, 8, 128), F32),
                pltpu.VMEM((bits, 8, 128), F32),
                dma((4,)),
                dma((4,)),
                dma((rounds, 2)),
                dma((rounds, 2)),
                dma((2,)),
                dma((2,)),
                dma((2,)),
                dma((n_space,)),
                dma((n_space,)),
                dma((bits,)),
                dma((bits,)),
            ],
            compiler_params=pltpu.CompilerParams(
                collective_id=0, has_side_effects=True, vmem_limit_bytes=67043328
            ),
        )(numbering, controls, target, state_in, adjoint_in, block_inverse)
        out = store((new_controls, next_state, next_adjoint), objective)
        return out[:3] + (out[3].reshape(()),)

    return jax.shard_map(
        per_device,
        mesh=mesh,
        in_specs=(
            P("tm", None, "space"),
            P(None, "space"),
            P("tm", None, "space"),
            P("tm", None, "space"),
            P(None, None, "space"),
            P("space", None),
        ),
        out_specs=(P("tm", None, "space"), P("tm", None, "space"), P("tm", None, "space"), P()),
        check_vma=False,
    )
```

```python
import functools

import jax
import jax.numpy as jnp
from jax import lax
from jax.experimental import pallas as pl
from jax.experimental.pallas import tpu as pltpu
from jax.sharding import PartitionSpec as P

NSIDE = 4
EXY = 16
BLOCK = NSIDE * NSIDE
LAYER = EXY * EXY
TIME_STEP = 0.1
PENALTY = 0.5
REGULAR = 0.1
F32 = jnp.float32
BF16 = jnp.bfloat16


def dot(a, b):
    return jnp.dot(a, b, preferred_element_type=F32)


def fold(x):
    total = None
    for i in range(0, x.shape[0], 8):
        for j in range(0, x.shape[1], 128):
            piece = x[i : i + 8, j : j + 128]
            total = piece if total is None else total + piece
    return total


def lateral(x):
    rows, lanes = x.shape
    q = lax.broadcasted_iota(jnp.int32, x.shape, 0)
    s = lax.broadcasted_iota(jnp.int32, x.shape, 1)
    a, b = q % NSIDE, (q // NSIDE) % NSIDE
    col, row = s % EXY, (s // EXY) % EXY
    last = NSIDE - 1

    def along(which, node_step, place, lane_step):
        back = (EXY - 1) * lane_step
        low = which == 0
        z = jnp.where(low, pltpu.roll(x, rows - last * node_step, 0), pltpu.roll(x, last * node_step, 0))
        down = jnp.where(place == 0, pltpu.roll(z, lanes - back, 1), pltpu.roll(z, lane_step, 1))
        up = jnp.where(place == EXY - 1, pltpu.roll(z, back, 1), pltpu.roll(z, lanes - lane_step, 1))
        return jnp.where(low, down, jnp.where(which == last, up, 0.0))

    return along(a, 1, col, 1) + along(b, NSIDE, row, EXY)


def face_count(shape):
    q = lax.broadcasted_iota(jnp.int32, shape, 0)
    count = jnp.zeros(shape, F32)
    for step in (1, NSIDE, BLOCK):
        at = (q // step) % NSIDE
        count += jnp.where((at == 0) | (at == NSIDE - 1), 1.0, 0.0)
    return count


def jumps_inside(x):
    nodes, elements = x.shape
    low, high = slice(0, BLOCK), slice(nodes - BLOCK, nodes)
    empty = jnp.zeros((BLOCK, LAYER), F32)
    below = jnp.concatenate([empty, x[high, : elements - LAYER]], axis=1)
    above = jnp.concatenate([x[low, LAYER:], empty], axis=1)
    middle = jnp.zeros((nodes - 2 * BLOCK, elements), F32)
    return lateral(x) + jnp.concatenate([below, middle, above], axis=0) - face_count(x.shape) * x


def kernel(
    n_space, n_tm,
    num_hbm, ctl_hbm, tgt_hbm, st_hbm, adj_hbm, a_hbm,
    newc_ref, nst_ref, nadj_ref, obj_ref,
    a_raw, a_ref, num, ctl_raw, ctl, tgt_raw, goal, adj_raw, adj, st, hist, r_ref, edge, gf, pulled, pa, pt,
    cost, rim_out, rim_in, st_out, st_in, adj_out, adj_in, slot_s, tree_out, tree_in,
    in_sem, a_sem, rim_send, rim_recv, st_sem, adj_sem,
    ss_send, ss_recv, tt_send, tt_recv,
):
    steps, nodes, elements = ctl.shape
    me = lax.axis_index("space")
    t = lax.axis_index("tm")
    first = t * steps
    total_steps = steps * n_tm
    rounds = 2 * steps
    final = rounds - 1
    last_block = nodes - BLOCK
    blocks = [slice(s, s + BLOCK) for s in range(0, nodes, BLOCK)]
    edge_rows = (slice(0, BLOCK), slice(last_block, nodes))
    edge_lanes = (slice(0, LAYER), slice(elements - LAYER, elements))

    def weight(k):
        return (first + k).astype(F32) / total_steps

    loads = [
        pltpu.make_async_copy(src, dst, in_sem.at[i])
        for i, (src, dst) in enumerate(
            ((num_hbm, num), (st_hbm.at[0], st), (tgt_hbm, tgt_raw), (ctl_hbm, ctl_raw), (adj_hbm.at[0], adj_raw))
        )
    ]
    for c in loads[:2]:
        c.start()
    rim_in[...] = jnp.zeros_like(rim_in)
    barrier = pltpu.get_barrier_semaphore()
    for d in range(1, n_space):
        pl.semaphore_signal(barrier, inc=1, device_id={"space": lax.rem(me + d, n_space)},
                            device_id_type=pl.DeviceIdType.MESH)
    bits = (n_tm - 1).bit_length()

    def partner(j):
        size = 2**j
        return t + size - 2 * size * ((t // size) % 2)

    def greet(peer):
        pl.semaphore_signal(barrier, inc=1, device_id={"tm": peer}, device_id_type=pl.DeviceIdType.MESH)

    for j in range(bits):
        greet(partner(j))

    @pl.when(t > 0)
    def _():
        greet(t - 1)

    @pl.when(t < n_tm - 1)
    def _():
        greet(t + 1)

    beside = jnp.where(t > 0, 1, 0) + jnp.where(t < n_tm - 1, 1, 0)

    parts = a_sem.shape[0]
    chunk = nodes // parts
    a_loads = [
        pltpu.make_async_copy(a_hbm.at[pl.ds(i * chunk, chunk)], a_raw.at[pl.ds(i * chunk, chunk)], a_sem.at[i])
        for i in range(parts)
    ]
    for c in a_loads:
        c.start()
    for c in loads[2:]:
        c.start()
    cost[...] = jnp.zeros_like(cost)

    loads[0].wait()
    own = num[...]
    for i in range(0, elements, LAYER):
        place = lax.broadcasted_iota(jnp.int32, (LAYER, elements), 0) + i
        pt[i : i + LAYER, :] = jnp.where(own == place, 1.0, 0.0).astype(BF16)
    down = jnp.broadcast_to(own.astype(F32), (128, elements)).T
    for i in range(0, elements, 128):
        place = lax.broadcasted_iota(jnp.int32, (elements, 128), 1) + i
        pa[:, i : i + 128] = jnp.where(down == place.astype(F32), 1.0, 0.0).astype(BF16)

    def split(x):
        high = x.astype(BF16)
        return jnp.concatenate([high, (x - high.astype(F32)).astype(BF16)], axis=0)

    def joined(x):
        return x[:nodes] + x[nodes:]

    def rim_peer(rnd, side):
        return {"tm": t - jnp.where(rnd == final, 1, 0), "space": me - 1 if side == 0 else me + 1}

    def rim_copy(rnd, side, slot):
        return pltpu.make_async_remote_copy(
            src_ref=rim_out.at[rnd, side], dst_ref=rim_in.at[rnd, slot],
            send_sem=rim_send.at[rnd, side], recv_sem=rim_recv.at[rnd, slot],
            device_id=rim_peer(rnd, side), device_id_type=pl.DeviceIdType.MESH,
        )

    def at_side(side):
        return me > 0 if side == 0 else me < n_space - 1

    def start_rims(rnd):
        for side in (0, 1):
            @pl.when(at_side(side) & ((rnd < final) | (t > 0)))
            def _():
                rim_copy(rnd, side, 1 - side).start()

    def wait_rims(rnd):
        for side in (0, 1):
            @pl.when(at_side(side))
            def _():
                rim_copy(rnd, side, side).wait()

    def wait_final_rims():
        for side in (0, 1):
            @pl.when(at_side(side) & (t < n_tm - 1))
            def _():
                rim_copy(final, side, side).wait_recv()

            @pl.when(at_side(side) & (t > 0))
            def _():
                rim_copy(final, side, side).wait_send()

    depth = BLOCK * BLOCK
    place_k = lax.broadcasted_iota(jnp.int32, (BLOCK, depth), 1)
    place_r = lax.broadcasted_iota(jnp.int32, (BLOCK, depth), 0)
    sum_rows = jnp.where(place_k // BLOCK == place_r, 1.0, 0.0).astype(BF16)
    sum_groups = jnp.where(place_k % BLOCK == place_r, 1.0, 0.0).astype(BF16)
    sum_rows2 = jnp.concatenate([sum_rows, sum_rows], axis=1)

    def groups(n):
        place_c = lax.broadcasted_iota(jnp.int32, (BLOCK, n), 1) % BLOCK
        return jnp.where(place_c == lax.broadcasted_iota(jnp.int32, (BLOCK, n), 0), 1.0, 0.0).astype(BF16)

    def product(out, into, lanes, right):
        return (a_ref[out, into, lanes] * right[None]).reshape(depth, LAYER)

    def product_pair(out, into, lanes, right):
        (i0, i1), (r0, r1) = into, right
        return (a_ref[out, i0, lanes] * r0[None] + a_ref[out, i1, lanes] * r1[None]).reshape(depth, LAYER)

    def inner_blocks(side):
        return [b for b in blocks if b != edge_rows[side]]

    def apply_inner(write):
        for side, lanes in enumerate(edge_lanes):
            b0, b1, b2 = inner_blocks(side)
            if side == 0:
                pair, single = (b0, b1), b2
            else:
                pair, single = (b1, b2), b0
            rp = (r_ref[pair[0], lanes], r_ref[pair[1], lanes])
            rs = r_ref[single, lanes]
            for out in blocks:
                q = jnp.concatenate(
                    [product_pair(out, pair, lanes, rp), product(out, single, lanes, rs)], axis=0
                )
                write(out, lanes, dot(sum_rows2, q))

    def transposed(out, into, lanes):
        rows = [i for b in into for i in range(b.start, b.stop)]

        def term(i):
            row = jnp.broadcast_to(gf[i : i + 1, lanes], (BLOCK, LAYER)).astype(BF16)
            return a_ref[i, out, lanes] * row

        pieces = [term(rows[i]) + term(rows[i + 1]) for i in range(0, len(rows), 2)]
        return dot(groups(BLOCK * len(pieces)), jnp.concatenate(pieces, axis=0))

    loads[1].wait()
    hist[0] = joined(dot(split(st[...]), pa[...]))
    for side in (0, 1):
        rim_out[0, side] = hist[0, edge_rows[side], edge_lanes[side]].astype(BF16)
    pl.semaphore_wait(barrier, n_space - 1 + bits + beside)
    start_rims(0)

    for c in loads[2:]:
        c.wait()
    goal[...] = dot(tgt_raw[...], pa[...])
    adj[...] = joined(dot(split(adj_raw[...]), pa[...]))
    for k in range(steps):
        ctl[k] = dot(ctl_raw[k], pa[...]).astype(BF16)
    piece = depth // nodes
    for i in range(0, nodes, piece):
        if i % chunk == 0:
            a_loads[i // chunk].wait()
        rows = a_raw[i : i + piece].reshape(depth, elements)
        a_ref[i : i + piece] = dot(rows, pa[...]).astype(BF16).reshape(piece, nodes, elements)

    def forward(k, carry):
        u = hist[k]
        c = ctl[k].astype(F32)
        base = u + TIME_STEP * (u - u * u * u) + TIME_STEP * PENALTY * jumps_inside(u) + TIME_STEP * c
        r_ref[...] = base.astype(BF16)
        for side in (0, 1):
            edge[side] = base[edge_rows[side], edge_lanes[side]]

        def write(rows, lanes, v):
            hist[k + 1, rows, lanes] = v

        apply_inner(write)
        w = jnp.where(k > 0, weight(k), 0.0)
        d = u - goal[...]
        cost[...] += 0.5 * w * fold(d * d) + 0.5 * REGULAR * fold(c * c)

        wait_rims(k)
        right = [
            (edge[side] + TIME_STEP * PENALTY * rim_in[k, side].astype(F32)).astype(BF16) for side in (0, 1)
        ]
        for side, (rows, lanes) in enumerate(zip(edge_rows, edge_lanes)):
            v = hist[k + 1, rows, lanes] + dot(sum_rows, product(rows, rows, lanes, right[side]))
            hist[k + 1, rows, lanes] = v
            rim_out[k + 1, side] = v.astype(BF16)

        @pl.when(k < steps - 1)
        def _():
            start_rims(k + 1)

        for side, (rows, lanes) in enumerate(zip(edge_rows, edge_lanes)):
            for out in inner_blocks(side):
                hist[k + 1, out, lanes] += dot(sum_rows, product(out, rows, lanes, right[side]))
        return carry

    lax.fori_loop(0, steps, forward, 0)

    w_end = weight(steps)
    u = hist[steps]
    d = u - goal[...]
    cost[...] += 0.5 * w_end * fold(d * d)
    gf[...] = w_end * d + adj[...]

    for side, (rows, lanes) in enumerate(zip(edge_rows, edge_lanes)):
        v = transposed(rows, blocks, lanes)
        pulled[rows, lanes] = v
        rim_out[steps, side] = v.astype(BF16)
    start_rims(steps)

    st_out[...] = hist[steps].astype(BF16)

    def st_copy(dst):
        return pltpu.make_async_remote_copy(
            src_ref=st_out, dst_ref=st_in, send_sem=st_sem.at[0], recv_sem=st_sem.at[1],
            device_id={"tm": dst}, device_id_type=pl.DeviceIdType.MESH)

    slot_s[me] = cost[...]

    def gather_copy(slots, send, recv, axis, index, count, d):
        return pltpu.make_async_remote_copy(
            src_ref=slots.at[index], dst_ref=slots.at[index], send_sem=send.at[d], recv_sem=recv.at[index],
            device_id={axis: lax.rem(index + d, count)}, device_id_type=pl.DeviceIdType.MESH)

    def gather_wait(slots, send, recv, axis, index, count, d):
        gather_copy(slots, send, recv, axis, index, count, d).wait_send()
        origin = lax.rem(index + d, count)
        pltpu.make_async_remote_copy(
            src_ref=slots.at[origin], dst_ref=slots.at[origin], send_sem=send.at[d], recv_sem=recv.at[origin],
            device_id={axis: origin}, device_id_type=pl.DeviceIdType.MESH).wait_recv()

    over_s = (slot_s, ss_send, ss_recv, "space", me, n_space)

    def tree_copy(j):
        return pltpu.make_async_remote_copy(
            src_ref=tree_out.at[j], dst_ref=tree_in.at[j], send_sem=tt_send.at[j], recv_sem=tt_recv.at[j],
            device_id={"tm": partner(j)}, device_id_type=pl.DeviceIdType.MESH)

    def tree_sum(j):
        if j == 0:
            for d in range(1, n_space):
                gather_wait(*over_s, d)
            total = slot_s[0]
            for i in range(1, n_space):
                total = total + slot_s[i]
            return total
        tree_copy(j - 1).wait()
        return tree_out[j - 1] + tree_in[j - 1]

    def tree_stage(j):
        tree_out[j] = tree_sum(j)
        tree_copy(j).start()

    early = min(bits, steps - 1)
    for d in range(1, n_space):
        gather_copy(*over_s, d).start()

    @pl.when(t < n_tm - 1)
    def _():
        st_copy(t + 1).start()

    for side, lanes in enumerate(edge_lanes):
        for out in inner_blocks(side):
            pulled[out, lanes] = transposed(out, blocks, lanes)

    def carry_back(k, p):
        before = hist[k]
        carried = p + TIME_STEP * (1.0 - 3.0 * before * before) * p + TIME_STEP * PENALTY * jumps_inside(p)
        return before, carried

    def update(k, p):
        control = ctl[k].astype(F32)
        fresh = (control - (TIME_STEP * p + REGULAR * control)).astype(BF16)
        newc_ref[k] = dot(fresh, pt[...]).astype(BF16)

    def backward(i, carry):
        k = steps - 1 - i
        rnd = steps + i
        p = pulled[...]
        before, carried = carry_back(k, p)
        gf[...] = weight(k) * (before - goal[...]) + carried
        update(k, p)
        for side, lanes in enumerate(edge_lanes):
            for out in blocks:
                pulled[out, lanes] = transposed(out, inner_blocks(side), lanes)

        for j in range(early):
            pl.when(i == j)(functools.partial(tree_stage, j))

        wait_rims(rnd)
        for side, (rows, lanes) in enumerate(zip(edge_rows, edge_lanes)):
            gf[rows, lanes] += TIME_STEP * PENALTY * rim_in[rnd, side].astype(F32)
        for side, (rows, lanes) in enumerate(zip(edge_rows, edge_lanes)):
            v = pulled[rows, lanes] + transposed(rows, [rows], lanes)
            pulled[rows, lanes] = v
            rim_out[rnd + 1, side] = v.astype(BF16)
        start_rims(rnd + 1)
        for side, (rows, lanes) in enumerate(zip(edge_rows, edge_lanes)):
            for out in inner_blocks(side):
                pulled[out, lanes] += transposed(out, [rows], lanes)
        return carry

    lax.fori_loop(0, steps - 1, backward, 0)

    def adj_copy(dst):
        return pltpu.make_async_remote_copy(
            src_ref=adj_out, dst_ref=adj_in, send_sem=adj_sem.at[0], recv_sem=adj_sem.at[1],
            device_id={"tm": dst}, device_id_type=pl.DeviceIdType.MESH)

    p = pulled[...]
    adj_out[...] = carry_back(0, p)[1].astype(BF16)

    @pl.when(t > 0)
    def _():
        adj_copy(t - 1).start()

    update(0, p)

    @pl.when(t == 0)
    def _():
        nst_ref[0] = st[...]

    @pl.when(t > 0)
    def _():
        st_copy(t - 1).wait_recv()
        nst_ref[0] = dot(st_in[...], pt[...])

    @pl.when(t < n_tm - 1)
    def _():
        st_copy(t + 1).wait_send()

    for j in range(early, bits):
        tree_stage(j)
    total = tree_sum(bits)
    scaled = total * (1.0 / (total_steps * nodes * elements * n_space))
    obj_ref[...] = jnp.sum(jnp.sum(scaled, axis=0, keepdims=True), axis=1, keepdims=True)

    wait_final_rims()

    @pl.when(t == n_tm - 1)
    def _():
        nadj_ref[...] = jnp.zeros_like(nadj_ref)

    @pl.when(t < n_tm - 1)
    def _():
        adj_copy(t + 1).wait_recv()
        gf[...] = adj_in[...].astype(F32)
        for side, (rows, lanes) in enumerate(zip(edge_rows, edge_lanes)):
            gf[rows, lanes] += TIME_STEP * PENALTY * rim_in[final, side].astype(F32)
        nadj_ref[0] = joined(dot(split(gf[...]), pt[...]))

    @pl.when(t > 0)
    def _():
        adj_copy(t - 1).wait_send()


def store_kernel(count, *refs):
    held = refs[2 * count : 3 * count]
    sems = refs[-1]
    takes = [pltpu.make_async_copy(refs[i], held[i], sems.at[0, i]) for i in range(count)]
    gives = [pltpu.make_async_copy(held[i], refs[count + i], sems.at[1, i]) for i in range(count)]
    for c in takes:
        c.start()
    for take_one, give in zip(takes, gives):
        take_one.wait()
        give.start()
    for c in gives:
        c.wait()


def store(values):
    count = len(values)
    return pl.pallas_call(
        functools.partial(store_kernel, count),
        out_shape=tuple(jax.ShapeDtypeStruct(v.shape, v.dtype) for v in values),
        in_specs=[pl.BlockSpec(memory_space=pltpu.HBM)] * count,
        out_specs=(pl.BlockSpec(memory_space=pltpu.HBM),) * count,
        scratch_shapes=[pltpu.VMEM(v.shape, v.dtype) for v in values] + [pltpu.SemaphoreType.DMA((2, count))],
        compiler_params=pltpu.CompilerParams(vmem_limit_bytes=67043328),
    )(*values)


def solution(mesh):
    n_space, n_tm = mesh.shape["space"], mesh.shape["tm"]

    def per_device(controls, target, state_in, adjoint_in, block_inverse, numbering):
        steps, nodes, elements = controls.shape
        vm = pl.BlockSpec(memory_space=pltpu.VMEM)
        hbm = pl.BlockSpec(memory_space=pltpu.HBM)
        field = (nodes, elements)
        rounds = 2 * steps
        bits = (n_tm - 1).bit_length()
        dma = pltpu.SemaphoreType.DMA
        new_controls, next_state, next_adjoint, objective = pl.pallas_call(
            functools.partial(kernel, n_space, n_tm),
            out_shape=(
                jax.ShapeDtypeStruct(controls.shape, BF16),
                jax.ShapeDtypeStruct(state_in.shape, F32),
                jax.ShapeDtypeStruct(adjoint_in.shape, F32),
                jax.ShapeDtypeStruct((1, 1), F32),
            ),
            in_specs=[hbm] * 6,
            out_specs=(vm, vm, vm, vm),
            scratch_shapes=[
                pltpu.VMEM(block_inverse.shape, BF16),
                pltpu.VMEM(block_inverse.shape, BF16),
                pltpu.VMEM(numbering.shape, jnp.int32),
                pltpu.VMEM(controls.shape, BF16),
                pltpu.VMEM(controls.shape, BF16),
                pltpu.VMEM(field, BF16),
                pltpu.VMEM(field, F32),
                pltpu.VMEM(field, F32),
                pltpu.VMEM(field, F32),
                pltpu.VMEM(field, F32),
                pltpu.VMEM((steps + 1,) + field, F32),
                pltpu.VMEM(field, BF16),
                pltpu.VMEM((2, BLOCK, LAYER), F32),
                pltpu.VMEM(field, F32),
                pltpu.VMEM(field, F32),
                pltpu.VMEM((elements, elements), BF16),
                pltpu.VMEM((elements, elements), BF16),
                pltpu.VMEM((8, 128), F32),
                pltpu.VMEM((rounds, 2, BLOCK, LAYER), BF16),
                pltpu.VMEM((rounds, 2, BLOCK, LAYER), BF16),
                pltpu.VMEM(field, BF16),
                pltpu.VMEM(field, BF16),
                pltpu.VMEM(field, BF16),
                pltpu.VMEM(field, BF16),
                pltpu.VMEM((n_space, 8, 128), F32),
                pltpu.VMEM((bits, 8, 128), F32),
                pltpu.VMEM((bits, 8, 128), F32),
                dma((5,)),
                dma((4,)),
                dma((rounds, 2)),
                dma((rounds, 2)),
                dma((2,)),
                dma((2,)),
                dma((n_space,)),
                dma((n_space,)),
                dma((bits,)),
                dma((bits,)),
            ],
            compiler_params=pltpu.CompilerParams(
                collective_id=0, has_side_effects=True, vmem_limit_bytes=67043328
            ),
        )(numbering, controls, target, state_in, adjoint_in, block_inverse)
        out = store((new_controls, next_state, next_adjoint, objective))
        return out[:3] + (out[3].reshape(()),)

    return jax.shard_map(
        per_device,
        mesh=mesh,
        in_specs=(
            P("tm", None, "space"),
            P(None, "space"),
            P("tm", None, "space"),
            P("tm", None, "space"),
            P(None, None, "space"),
            P("space", None),
        ),
        out_specs=(P("tm", None, "space"), P("tm", None, "space"), P("tm", None, "space"), P()),
        check_vma=False,
    )
```

```python
import functools

import jax
import jax.numpy as jnp
from jax import lax
from jax.experimental import pallas as pl
from jax.experimental.pallas import tpu as pltpu
from jax.sharding import PartitionSpec as P

NSIDE = 4
EXY = 16
BLOCK = NSIDE * NSIDE
LAYER = EXY * EXY
TIME_STEP = 0.1
PENALTY = 0.5
REGULAR = 0.1
F32 = jnp.float32
BF16 = jnp.bfloat16


def dot(a, b):
    return jnp.dot(a, b, preferred_element_type=F32)


def fold(x):
    total = None
    for i in range(0, x.shape[0], 8):
        for j in range(0, x.shape[1], 128):
            piece = x[i : i + 8, j : j + 128]
            total = piece if total is None else total + piece
    return total


def lateral(x):
    rows, lanes = x.shape
    q = lax.broadcasted_iota(jnp.int32, x.shape, 0)
    s = lax.broadcasted_iota(jnp.int32, x.shape, 1)
    a, b = q % NSIDE, (q // NSIDE) % NSIDE
    col, row = s % EXY, (s // EXY) % EXY
    last = NSIDE - 1

    def along(which, node_step, place, lane_step):
        back = (EXY - 1) * lane_step
        low = which == 0
        z = jnp.where(low, pltpu.roll(x, rows - last * node_step, 0), pltpu.roll(x, last * node_step, 0))
        down = jnp.where(place == 0, pltpu.roll(z, lanes - back, 1), pltpu.roll(z, lane_step, 1))
        up = jnp.where(place == EXY - 1, pltpu.roll(z, back, 1), pltpu.roll(z, lanes - lane_step, 1))
        return jnp.where(low, down, jnp.where(which == last, up, 0.0))

    return along(a, 1, col, 1) + along(b, NSIDE, row, EXY)


def face_count(shape):
    q = lax.broadcasted_iota(jnp.int32, shape, 0)
    count = jnp.zeros(shape, F32)
    for step in (1, NSIDE, BLOCK):
        at = (q // step) % NSIDE
        count += jnp.where((at == 0) | (at == NSIDE - 1), 1.0, 0.0)
    return count


def jumps_inside(x):
    nodes, elements = x.shape
    low, high = slice(0, BLOCK), slice(nodes - BLOCK, nodes)
    empty = jnp.zeros((BLOCK, LAYER), F32)
    below = jnp.concatenate([empty, x[high, : elements - LAYER]], axis=1)
    above = jnp.concatenate([x[low, LAYER:], empty], axis=1)
    middle = jnp.zeros((nodes - 2 * BLOCK, elements), F32)
    return lateral(x) + jnp.concatenate([below, middle, above], axis=0) - face_count(x.shape) * x


def kernel(
    n_space, n_tm,
    num_hbm, ctl_hbm, tgt_hbm, st_hbm, adj_hbm, a_hbm,
    newc_ref, nst_ref, nadj_ref, obj_ref,
    a_raw, a_ref, num, ctl_raw, ctl, tgt_raw, goal, adj_raw, adj, st, hist, r_ref, edge, gf, pulled, pa, pt,
    cost, rim_out, rim_in, st_out, st_in, adj_out, adj_in, slot_s, tree_out, tree_in,
    in_sem, a_sem, rim_send, rim_recv, st_sem, adj_sem,
    ss_send, ss_recv, tt_send, tt_recv, ready,
):
    steps, nodes, elements = ctl.shape
    me = lax.axis_index("space")
    t = lax.axis_index("tm")
    first = t * steps
    total_steps = steps * n_tm
    rounds = 2 * steps
    final = rounds - 1
    last_block = nodes - BLOCK
    blocks = [slice(s, s + BLOCK) for s in range(0, nodes, BLOCK)]
    edge_rows = (slice(0, BLOCK), slice(last_block, nodes))
    edge_lanes = (slice(0, LAYER), slice(elements - LAYER, elements))

    def weight(k):
        return (first + k).astype(F32) / total_steps

    loads = [
        pltpu.make_async_copy(src, dst, in_sem.at[i])
        for i, (src, dst) in enumerate(
            ((num_hbm, num), (st_hbm.at[0], st), (tgt_hbm, tgt_raw), (ctl_hbm, ctl_raw), (adj_hbm.at[0], adj_raw))
        )
    ]
    for c in loads[:2]:
        c.start()
    rim_in[...] = jnp.zeros_like(rim_in)
    barrier = pltpu.get_barrier_semaphore()
    for d in range(1, n_space):
        pl.semaphore_signal(barrier, inc=1, device_id={"space": lax.rem(me + d, n_space)},
                            device_id_type=pl.DeviceIdType.MESH)
    bits = (n_tm - 1).bit_length()

    def partner(j):
        size = 2**j
        return t + size - 2 * size * ((t // size) % 2)

    def beside(far):
        return jnp.where(t >= far, 1, 0) + jnp.where(t + far < n_tm, 1, 0)

    def greet(sem, far):
        @pl.when(t >= far)
        def _():
            pl.semaphore_signal(sem, inc=1, device_id={"tm": t - far}, device_id_type=pl.DeviceIdType.MESH)

        @pl.when(t + far < n_tm)
        def _():
            pl.semaphore_signal(sem, inc=1, device_id={"tm": t + far}, device_id_type=pl.DeviceIdType.MESH)

    greet(barrier, 1)

    def tell(j):
        if 0 < j < bits:
            greet(ready.at[j], 2 ** (j - 1))

    def hear(j):
        if 0 < j < bits:
            pl.semaphore_wait(ready.at[j], beside(2 ** (j - 1)))

    parts = a_sem.shape[0]
    chunk = nodes // parts
    a_loads = [
        pltpu.make_async_copy(a_hbm.at[pl.ds(i * chunk, chunk)], a_raw.at[pl.ds(i * chunk, chunk)], a_sem.at[i])
        for i in range(parts)
    ]
    outer = [0, parts - 1]
    inner = list(range(1, parts - 1))
    for i in outer + inner:
        a_loads[i].start()
    for c in loads[2:]:
        c.start()
    cost[...] = jnp.zeros_like(cost)

    loads[0].wait()
    own = num[...]
    for i in range(0, elements, LAYER):
        place = lax.broadcasted_iota(jnp.int32, (LAYER, elements), 0) + i
        pt[i : i + LAYER, :] = jnp.where(own == place, 1.0, 0.0).astype(BF16)
    down = jnp.broadcast_to(own.astype(F32), (128, elements)).T
    for i in range(0, elements, 128):
        place = lax.broadcasted_iota(jnp.int32, (elements, 128), 1) + i
        pa[:, i : i + 128] = jnp.where(down == place.astype(F32), 1.0, 0.0).astype(BF16)

    def split(x):
        high = x.astype(BF16)
        return jnp.concatenate([high, (x - high.astype(F32)).astype(BF16)], axis=0)

    def joined(x):
        return x[:nodes] + x[nodes:]

    def rim_peer(rnd, side):
        return {"tm": t - jnp.where(rnd == final, 1, 0), "space": me - 1 if side == 0 else me + 1}

    def rim_copy(rnd, side, slot):
        return pltpu.make_async_remote_copy(
            src_ref=rim_out.at[rnd, side], dst_ref=rim_in.at[rnd, slot],
            send_sem=rim_send.at[rnd, side], recv_sem=rim_recv.at[rnd, slot],
            device_id=rim_peer(rnd, side), device_id_type=pl.DeviceIdType.MESH,
        )

    def at_side(side):
        return me > 0 if side == 0 else me < n_space - 1

    def start_rims(rnd):
        for side in (0, 1):
            @pl.when(at_side(side) & ((rnd < final) | (t > 0)))
            def _():
                rim_copy(rnd, side, 1 - side).start()

    def wait_rims(rnd):
        for side in (0, 1):
            @pl.when(at_side(side))
            def _():
                rim_copy(rnd, side, side).wait()

    def wait_final_rims():
        for side in (0, 1):
            @pl.when(at_side(side) & (t < n_tm - 1))
            def _():
                rim_copy(final, side, side).wait_recv()

            @pl.when(at_side(side) & (t > 0))
            def _():
                rim_copy(final, side, side).wait_send()

    depth = BLOCK * BLOCK
    place_k = lax.broadcasted_iota(jnp.int32, (BLOCK, depth), 1)
    place_r = lax.broadcasted_iota(jnp.int32, (BLOCK, depth), 0)
    sum_rows = jnp.where(place_k // BLOCK == place_r, 1.0, 0.0).astype(BF16)
    sum_groups = jnp.where(place_k % BLOCK == place_r, 1.0, 0.0).astype(BF16)
    sum_rows2 = jnp.concatenate([sum_rows, sum_rows], axis=1)

    def groups(n):
        place_c = lax.broadcasted_iota(jnp.int32, (BLOCK, n), 1) % BLOCK
        return jnp.where(place_c == lax.broadcasted_iota(jnp.int32, (BLOCK, n), 0), 1.0, 0.0).astype(BF16)

    def product(out, into, lanes, right):
        return (a_ref[out, into, lanes] * right[None]).reshape(depth, LAYER)

    def product_pair(out, into, lanes, right):
        (i0, i1), (r0, r1) = into, right
        return (a_ref[out, i0, lanes] * r0[None] + a_ref[out, i1, lanes] * r1[None]).reshape(depth, LAYER)

    def inner_blocks(side):
        return [b for b in blocks if b != edge_rows[side]]

    def apply_inner(side, outs, write):
        lanes = edge_lanes[side]
        b0, b1, b2 = inner_blocks(side)
        if side == 0:
            pair, single = (b0, b1), b2
        else:
            pair, single = (b1, b2), b0
        rp = (r_ref[pair[0], lanes], r_ref[pair[1], lanes])
        rs = r_ref[single, lanes]
        for out in outs:
            q = jnp.concatenate([product_pair(out, pair, lanes, rp), product(out, single, lanes, rs)], axis=0)
            write(out, lanes, dot(sum_rows2, q))

    def transposed(out, into, lanes):
        rows = [i for b in into for i in range(b.start, b.stop)]

        def term(i):
            row = jnp.broadcast_to(gf[i : i + 1, lanes], (BLOCK, LAYER)).astype(BF16)
            return a_ref[i, out, lanes] * row

        pieces = [term(rows[i]) + term(rows[i + 1]) for i in range(0, len(rows), 2)]
        return dot(groups(BLOCK * len(pieces)), jnp.concatenate(pieces, axis=0))

    loads[1].wait()
    hist[0] = joined(dot(split(st[...]), pa[...]))
    for side in (0, 1):
        rim_out[0, side] = hist[0, edge_rows[side], edge_lanes[side]].astype(BF16)
    pl.semaphore_wait(barrier, n_space - 1 + beside(1))
    start_rims(0)
    tell(1)

    for c in loads[2:]:
        c.wait()
    goal[...] = dot(tgt_raw[...], pa[...])
    adj[...] = joined(dot(split(adj_raw[...]), pa[...]))
    for k in range(steps):
        ctl[k] = dot(ctl_raw[k], pa[...]).astype(BF16)
    piece = depth // nodes

    def permute(part):
        a_loads[part].wait()
        for i in range(part * chunk, (part + 1) * chunk, piece):
            rows = a_raw[i : i + piece].reshape(depth, elements)
            a_ref[i : i + piece] = dot(rows, pa[...]).astype(BF16).reshape(piece, nodes, elements)

    def prepare(k):
        u = hist[k]
        c = ctl[k].astype(F32)
        base = u + TIME_STEP * (u - u * u * u) + TIME_STEP * PENALTY * jumps_inside(u) + TIME_STEP * c
        r_ref[...] = base.astype(BF16)
        for side in (0, 1):
            edge[side] = base[edge_rows[side], edge_lanes[side]]

    def keep(k):
        def write(rows, lanes, v):
            hist[k + 1, rows, lanes] = v

        return write

    def count_cost(k):
        c = ctl[k].astype(F32)
        w = jnp.where(k > 0, weight(k), 0.0)
        d = hist[k] - goal[...]
        cost[...] += 0.5 * w * fold(d * d) + 0.5 * REGULAR * fold(c * c)

    def right_edges(k):
        return [
            (edge[side] + TIME_STEP * PENALTY * rim_in[k, side].astype(F32)).astype(BF16) for side in (0, 1)
        ]

    def step_edges(k, right):
        for side, (rows, lanes) in enumerate(zip(edge_rows, edge_lanes)):
            v = hist[k + 1, rows, lanes] + dot(sum_rows, product(rows, rows, lanes, right[side]))
            hist[k + 1, rows, lanes] = v
            rim_out[k + 1, side] = v.astype(BF16)

    def step_rest(k, right):
        for side, (rows, lanes) in enumerate(zip(edge_rows, edge_lanes)):
            for out in inner_blocks(side):
                hist[k + 1, out, lanes] += dot(sum_rows, product(out, rows, lanes, right[side]))

    prepare(0)
    for part in outer:
        permute(part)
    for side in (0, 1):
        apply_inner(side, [edge_rows[side]], keep(0))
    wait_rims(0)
    first_right = right_edges(0)
    step_edges(0, first_right)
    if steps > 1:
        start_rims(1)
    for part in inner:
        permute(part)
    for side in (0, 1):
        apply_inner(side, inner_blocks(side), keep(0))
    step_rest(0, first_right)
    count_cost(0)
    hear(1)
    tell(2)

    def forward(k, carry):
        prepare(k)
        for side in (0, 1):
            apply_inner(side, blocks, keep(k))
        count_cost(k)
        wait_rims(k)
        right = right_edges(k)
        step_edges(k, right)

        @pl.when(k < steps - 1)
        def _():
            start_rims(k + 1)

        step_rest(k, right)
        return carry

    lax.fori_loop(1, steps, forward, 0)
    for j in range(2, bits):
        hear(j)
        tell(j + 1)

    w_end = weight(steps)
    u = hist[steps]
    d = u - goal[...]
    cost[...] += 0.5 * w_end * fold(d * d)
    gf[...] = w_end * d + adj[...]

    for side, (rows, lanes) in enumerate(zip(edge_rows, edge_lanes)):
        v = transposed(rows, blocks, lanes)
        pulled[rows, lanes] = v
        rim_out[steps, side] = v.astype(BF16)
    start_rims(steps)

    st_out[...] = hist[steps].astype(BF16)

    def st_copy(dst):
        return pltpu.make_async_remote_copy(
            src_ref=st_out, dst_ref=st_in, send_sem=st_sem.at[0], recv_sem=st_sem.at[1],
            device_id={"tm": dst}, device_id_type=pl.DeviceIdType.MESH)

    slot_s[me] = cost[...]

    def gather_copy(slots, send, recv, axis, index, count, d):
        return pltpu.make_async_remote_copy(
            src_ref=slots.at[index], dst_ref=slots.at[index], send_sem=send.at[d], recv_sem=recv.at[index],
            device_id={axis: lax.rem(index + d, count)}, device_id_type=pl.DeviceIdType.MESH)

    def gather_wait(slots, send, recv, axis, index, count, d):
        gather_copy(slots, send, recv, axis, index, count, d).wait_send()
        origin = lax.rem(index + d, count)
        pltpu.make_async_remote_copy(
            src_ref=slots.at[origin], dst_ref=slots.at[origin], send_sem=send.at[d], recv_sem=recv.at[origin],
            device_id={axis: origin}, device_id_type=pl.DeviceIdType.MESH).wait_recv()

    over_s = (slot_s, ss_send, ss_recv, "space", me, n_space)

    def tree_copy(j):
        return pltpu.make_async_remote_copy(
            src_ref=tree_out.at[j], dst_ref=tree_in.at[j], send_sem=tt_send.at[j], recv_sem=tt_recv.at[j],
            device_id={"tm": partner(j)}, device_id_type=pl.DeviceIdType.MESH)

    def tree_sum(j):
        if j == 0:
            for d in range(1, n_space):
                gather_wait(*over_s, d)
            total = slot_s[0]
            for i in range(1, n_space):
                total = total + slot_s[i]
            return total
        tree_copy(j - 1).wait()
        return tree_out[j - 1] + tree_in[j - 1]

    def tree_stage(j):
        tree_out[j] = tree_sum(j)
        tree_copy(j).start()

    early = min(bits, steps - 1)
    for d in range(1, n_space):
        gather_copy(*over_s, d).start()

    @pl.when(t < n_tm - 1)
    def _():
        st_copy(t + 1).start()

    for side, lanes in enumerate(edge_lanes):
        for out in inner_blocks(side):
            pulled[out, lanes] = transposed(out, blocks, lanes)

    def carry_back(k, p):
        before = hist[k]
        carried = p + TIME_STEP * (1.0 - 3.0 * before * before) * p + TIME_STEP * PENALTY * jumps_inside(p)
        return before, carried

    def update(k, p):
        control = ctl[k].astype(F32)
        fresh = (control - (TIME_STEP * p + REGULAR * control)).astype(BF16)
        newc_ref[k] = dot(fresh, pt[...]).astype(BF16)

    def backward(i, carry):
        k = steps - 1 - i
        rnd = steps + i
        p = pulled[...]
        before, carried = carry_back(k, p)
        gf[...] = weight(k) * (before - goal[...]) + carried
        update(k, p)
        for side, lanes in enumerate(edge_lanes):
            for out in blocks:
                pulled[out, lanes] = transposed(out, inner_blocks(side), lanes)

        for j in range(early):
            pl.when(i == j)(functools.partial(tree_stage, j))

        wait_rims(rnd)
        for side, (rows, lanes) in enumerate(zip(edge_rows, edge_lanes)):
            gf[rows, lanes] += TIME_STEP * PENALTY * rim_in[rnd, side].astype(F32)
        for side, (rows, lanes) in enumerate(zip(edge_rows, edge_lanes)):
            v = pulled[rows, lanes] + transposed(rows, [rows], lanes)
            pulled[rows, lanes] = v
            rim_out[rnd + 1, side] = v.astype(BF16)
        start_rims(rnd + 1)
        for side, (rows, lanes) in enumerate(zip(edge_rows, edge_lanes)):
            for out in inner_blocks(side):
                pulled[out, lanes] += transposed(out, [rows], lanes)
        return carry

    lax.fori_loop(0, steps - 1, backward, 0)

    def adj_copy(dst):
        return pltpu.make_async_remote_copy(
            src_ref=adj_out, dst_ref=adj_in, send_sem=adj_sem.at[0], recv_sem=adj_sem.at[1],
            device_id={"tm": dst}, device_id_type=pl.DeviceIdType.MESH)

    p = pulled[...]
    adj_out[...] = carry_back(0, p)[1].astype(BF16)

    @pl.when(t > 0)
    def _():
        adj_copy(t - 1).start()

    update(0, p)

    @pl.when(t == 0)
    def _():
        nst_ref[0] = st[...]

    @pl.when(t > 0)
    def _():
        st_copy(t - 1).wait_recv()
        nst_ref[0] = dot(st_in[...], pt[...])

    @pl.when(t < n_tm - 1)
    def _():
        st_copy(t + 1).wait_send()

    for j in range(early, bits):
        tree_stage(j)
    total = tree_sum(bits)
    scaled = total * (1.0 / (total_steps * nodes * elements * n_space))
    obj_ref[...] = jnp.sum(jnp.sum(scaled, axis=0, keepdims=True), axis=1, keepdims=True)

    wait_final_rims()

    @pl.when(t == n_tm - 1)
    def _():
        nadj_ref[...] = jnp.zeros_like(nadj_ref)

    @pl.when(t < n_tm - 1)
    def _():
        adj_copy(t + 1).wait_recv()
        gf[...] = adj_in[...].astype(F32)
        for side, (rows, lanes) in enumerate(zip(edge_rows, edge_lanes)):
            gf[rows, lanes] += TIME_STEP * PENALTY * rim_in[final, side].astype(F32)
        nadj_ref[0] = joined(dot(split(gf[...]), pt[...]))

    @pl.when(t > 0)
    def _():
        adj_copy(t - 1).wait_send()


def store_kernel(count, *refs):
    held = refs[2 * count : 3 * count]
    sems = refs[-1]
    takes = [pltpu.make_async_copy(refs[i], held[i], sems.at[0, i]) for i in range(count)]
    gives = [pltpu.make_async_copy(held[i], refs[count + i], sems.at[1, i]) for i in range(count)]
    for c in takes:
        c.start()
    for take_one, give in zip(takes, gives):
        take_one.wait()
        give.start()
    for c in gives:
        c.wait()


def store(values):
    count = len(values)
    return pl.pallas_call(
        functools.partial(store_kernel, count),
        out_shape=tuple(jax.ShapeDtypeStruct(v.shape, v.dtype) for v in values),
        in_specs=[pl.BlockSpec(memory_space=pltpu.HBM)] * count,
        out_specs=(pl.BlockSpec(memory_space=pltpu.HBM),) * count,
        scratch_shapes=[pltpu.VMEM(v.shape, v.dtype) for v in values] + [pltpu.SemaphoreType.DMA((2, count))],
        compiler_params=pltpu.CompilerParams(vmem_limit_bytes=67043328),
    )(*values)


def solution(mesh):
    n_space, n_tm = mesh.shape["space"], mesh.shape["tm"]

    def per_device(controls, target, state_in, adjoint_in, block_inverse, numbering):
        steps, nodes, elements = controls.shape
        vm = pl.BlockSpec(memory_space=pltpu.VMEM)
        hbm = pl.BlockSpec(memory_space=pltpu.HBM)
        field = (nodes, elements)
        rounds = 2 * steps
        bits = (n_tm - 1).bit_length()
        dma = pltpu.SemaphoreType.DMA
        new_controls, next_state, next_adjoint, objective = pl.pallas_call(
            functools.partial(kernel, n_space, n_tm),
            out_shape=(
                jax.ShapeDtypeStruct(controls.shape, BF16),
                jax.ShapeDtypeStruct(state_in.shape, F32),
                jax.ShapeDtypeStruct(adjoint_in.shape, F32),
                jax.ShapeDtypeStruct((1, 1), F32),
            ),
            in_specs=[hbm] * 6,
            out_specs=(vm, vm, vm, vm),
            scratch_shapes=[
                pltpu.VMEM(block_inverse.shape, BF16),
                pltpu.VMEM(block_inverse.shape, BF16),
                pltpu.VMEM(numbering.shape, jnp.int32),
                pltpu.VMEM(controls.shape, BF16),
                pltpu.VMEM(controls.shape, BF16),
                pltpu.VMEM(field, BF16),
                pltpu.VMEM(field, F32),
                pltpu.VMEM(field, F32),
                pltpu.VMEM(field, F32),
                pltpu.VMEM(field, F32),
                pltpu.VMEM((steps + 1,) + field, F32),
                pltpu.VMEM(field, BF16),
                pltpu.VMEM((2, BLOCK, LAYER), F32),
                pltpu.VMEM(field, F32),
                pltpu.VMEM(field, F32),
                pltpu.VMEM((elements, elements), BF16),
                pltpu.VMEM((elements, elements), BF16),
                pltpu.VMEM((8, 128), F32),
                pltpu.VMEM((rounds, 2, BLOCK, LAYER), BF16),
                pltpu.VMEM((rounds, 2, BLOCK, LAYER), BF16),
                pltpu.VMEM(field, BF16),
                pltpu.VMEM(field, BF16),
                pltpu.VMEM(field, BF16),
                pltpu.VMEM(field, BF16),
                pltpu.VMEM((n_space, 8, 128), F32),
                pltpu.VMEM((bits, 8, 128), F32),
                pltpu.VMEM((bits, 8, 128), F32),
                dma((5,)),
                dma((4,)),
                dma((rounds, 2)),
                dma((rounds, 2)),
                dma((2,)),
                dma((2,)),
                dma((n_space,)),
                dma((n_space,)),
                dma((bits,)),
                dma((bits,)),
                pltpu.SemaphoreType.REGULAR((bits,)),
            ],
            compiler_params=pltpu.CompilerParams(
                collective_id=0, has_side_effects=True, vmem_limit_bytes=67043328
            ),
        )(numbering, controls, target, state_in, adjoint_in, block_inverse)
        out = store((new_controls, next_state, next_adjoint, objective))
        return out[:3] + (out[3].reshape(()),)

    return jax.shard_map(
        per_device,
        mesh=mesh,
        in_specs=(
            P("tm", None, "space"),
            P(None, "space"),
            P("tm", None, "space"),
            P("tm", None, "space"),
            P(None, None, "space"),
            P("space", None),
        ),
        out_specs=(P("tm", None, "space"), P("tm", None, "space"), P("tm", None, "space"), P()),
        check_vma=False,
    )
```

```python
import functools

import jax
import jax.numpy as jnp
from jax import lax
from jax.experimental import pallas as pl
from jax.experimental.pallas import tpu as pltpu
from jax.sharding import PartitionSpec as P

NSIDE = 4
EXY = 16
BLOCK = NSIDE * NSIDE
LAYER = EXY * EXY
TIME_STEP = 0.1
PENALTY = 0.5
REGULAR = 0.1
F32 = jnp.float32
BF16 = jnp.bfloat16


def dot(a, b):
    return jnp.dot(a, b, preferred_element_type=F32)


def fold(x):
    total = None
    for i in range(0, x.shape[0], 8):
        for j in range(0, x.shape[1], 128):
            piece = x[i : i + 8, j : j + 128]
            total = piece if total is None else total + piece
    return total


def lateral(x):
    rows, lanes = x.shape
    q = lax.broadcasted_iota(jnp.int32, x.shape, 0)
    s = lax.broadcasted_iota(jnp.int32, x.shape, 1)
    a, b = q % NSIDE, (q // NSIDE) % NSIDE
    col, row = s % EXY, (s // EXY) % EXY
    last = NSIDE - 1

    def along(which, node_step, place, lane_step):
        back = (EXY - 1) * lane_step
        low = which == 0
        z = jnp.where(low, pltpu.roll(x, rows - last * node_step, 0), pltpu.roll(x, last * node_step, 0))
        down = jnp.where(place == 0, pltpu.roll(z, lanes - back, 1), pltpu.roll(z, lane_step, 1))
        up = jnp.where(place == EXY - 1, pltpu.roll(z, back, 1), pltpu.roll(z, lanes - lane_step, 1))
        return jnp.where(low, down, jnp.where(which == last, up, 0.0))

    return along(a, 1, col, 1) + along(b, NSIDE, row, EXY)


def face_count(shape):
    q = lax.broadcasted_iota(jnp.int32, shape, 0)
    count = jnp.zeros(shape, F32)
    for step in (1, NSIDE, BLOCK):
        at = (q // step) % NSIDE
        count += jnp.where((at == 0) | (at == NSIDE - 1), 1.0, 0.0)
    return count


def jumps_inside(x):
    nodes, elements = x.shape
    low, high = slice(0, BLOCK), slice(nodes - BLOCK, nodes)
    empty = jnp.zeros((BLOCK, LAYER), F32)
    below = jnp.concatenate([empty, x[high, : elements - LAYER]], axis=1)
    above = jnp.concatenate([x[low, LAYER:], empty], axis=1)
    middle = jnp.zeros((nodes - 2 * BLOCK, elements), F32)
    return lateral(x) + jnp.concatenate([below, middle, above], axis=0) - face_count(x.shape) * x


def kernel(
    n_space, n_tm,
    num_hbm, ctl_hbm, tgt_hbm, st_hbm, adj_hbm, a_hbm,
    newc_ref, nst_ref, nadj_ref, obj_ref,
    a_raw, a_ref, num, ctl_raw, ctl, tgt_raw, goal, adj_raw, adj, st, hist, r_ref, edge, gf, pulled, pa, pt,
    cost, rim_out, rim_in, st_out, st_in, adj_out, adj_in, slot_s, tree_out, tree_in,
    in_sem, a_sem, rim_send, rim_recv, st_sem, adj_sem,
    ss_send, ss_recv, tt_send, tt_recv, ready,
):
    steps, nodes, elements = ctl.shape
    me = lax.axis_index("space")
    t = lax.axis_index("tm")
    first = t * steps
    total_steps = steps * n_tm
    rounds = 2 * steps
    final = rounds - 1
    last_block = nodes - BLOCK
    blocks = [slice(s, s + BLOCK) for s in range(0, nodes, BLOCK)]
    edge_rows = (slice(0, BLOCK), slice(last_block, nodes))
    edge_lanes = (slice(0, LAYER), slice(elements - LAYER, elements))

    def weight(k):
        return (first + k).astype(F32) / total_steps

    loads = [
        pltpu.make_async_copy(src, dst, in_sem.at[i])
        for i, (src, dst) in enumerate(
            ((num_hbm, num), (st_hbm.at[0], st), (tgt_hbm, tgt_raw), (ctl_hbm, ctl_raw), (adj_hbm.at[0], adj_raw))
        )
    ]
    for c in loads[:2]:
        c.start()
    rim_in[...] = jnp.zeros_like(rim_in)
    barrier = pltpu.get_barrier_semaphore()
    for d in range(1, n_space):
        pl.semaphore_signal(barrier, inc=1, device_id={"space": lax.rem(me + d, n_space)},
                            device_id_type=pl.DeviceIdType.MESH)
    bits = (n_tm - 1).bit_length()

    def partner(j):
        size = 2**j
        return t + size - 2 * size * ((t // size) % 2)

    def beside(far):
        return jnp.where(t >= far, 1, 0) + jnp.where(t + far < n_tm, 1, 0)

    def greet(sem, far):
        @pl.when(t >= far)
        def _():
            pl.semaphore_signal(sem, inc=1, device_id={"tm": t - far}, device_id_type=pl.DeviceIdType.MESH)

        @pl.when(t + far < n_tm)
        def _():
            pl.semaphore_signal(sem, inc=1, device_id={"tm": t + far}, device_id_type=pl.DeviceIdType.MESH)

    greet(barrier, 1)

    def tell(j):
        if 0 < j < bits:
            greet(ready.at[j], 2 ** (j - 1))

    def hear(j):
        if 0 < j < bits:
            pl.semaphore_wait(ready.at[j], beside(2 ** (j - 1)))

    parts = a_sem.shape[0]
    chunk = nodes // parts
    a_loads = [
        pltpu.make_async_copy(a_hbm.at[pl.ds(i * chunk, chunk)], a_raw.at[pl.ds(i * chunk, chunk)], a_sem.at[i])
        for i in range(parts)
    ]
    outer = [0, parts - 1]
    inner = list(range(1, parts - 1))
    for i in outer + inner:
        a_loads[i].start()
    for c in loads[2:]:
        c.start()
    cost[...] = jnp.zeros_like(cost)

    loads[0].wait()
    own = num[...]
    for i in range(0, elements, LAYER):
        place = lax.broadcasted_iota(jnp.int32, (LAYER, elements), 0) + i
        pt[i : i + LAYER, :] = jnp.where(own == place, 1.0, 0.0).astype(BF16)
    down = jnp.broadcast_to(own.astype(F32), (128, elements)).T
    for i in range(0, elements, 128):
        place = lax.broadcasted_iota(jnp.int32, (elements, 128), 1) + i
        pa[:, i : i + 128] = jnp.where(down == place.astype(F32), 1.0, 0.0).astype(BF16)

    def split(x):
        high = x.astype(BF16)
        return jnp.concatenate([high, (x - high.astype(F32)).astype(BF16)], axis=0)

    def joined(x):
        return x[:nodes] + x[nodes:]

    def rim_peer(rnd, side):
        return {"tm": t - jnp.where(rnd == final, 1, 0), "space": me - 1 if side == 0 else me + 1}

    def rim_copy(rnd, side, slot):
        return pltpu.make_async_remote_copy(
            src_ref=rim_out.at[rnd, side], dst_ref=rim_in.at[rnd, slot],
            send_sem=rim_send.at[rnd, side], recv_sem=rim_recv.at[rnd, slot],
            device_id=rim_peer(rnd, side), device_id_type=pl.DeviceIdType.MESH,
        )

    def at_side(side):
        return me > 0 if side == 0 else me < n_space - 1

    def start_rims(rnd):
        for side in (0, 1):
            @pl.when(at_side(side) & ((rnd < final) | (t > 0)))
            def _():
                rim_copy(rnd, side, 1 - side).start()

    def wait_rims(rnd):
        for side in (0, 1):
            @pl.when(at_side(side))
            def _():
                rim_copy(rnd, side, side).wait()

    def wait_final_rims():
        for side in (0, 1):
            @pl.when(at_side(side) & (t < n_tm - 1))
            def _():
                rim_copy(final, side, side).wait_recv()

            @pl.when(at_side(side) & (t > 0))
            def _():
                rim_copy(final, side, side).wait_send()

    depth = BLOCK * BLOCK
    place_k = lax.broadcasted_iota(jnp.int32, (BLOCK, depth), 1)
    place_r = lax.broadcasted_iota(jnp.int32, (BLOCK, depth), 0)
    sum_rows = jnp.where(place_k // BLOCK == place_r, 1.0, 0.0).astype(BF16)
    sum_groups = jnp.where(place_k % BLOCK == place_r, 1.0, 0.0).astype(BF16)
    sum_rows2 = jnp.concatenate([sum_rows, sum_rows], axis=1)

    def groups(n):
        place_c = lax.broadcasted_iota(jnp.int32, (BLOCK, n), 1) % BLOCK
        return jnp.where(place_c == lax.broadcasted_iota(jnp.int32, (BLOCK, n), 0), 1.0, 0.0).astype(BF16)

    def product(out, into, lanes, right):
        return (a_ref[out, into, lanes] * right[None]).reshape(depth, LAYER)

    def product_pair(out, into, lanes, right):
        (i0, i1), (r0, r1) = into, right
        return (a_ref[out, i0, lanes] * r0[None] + a_ref[out, i1, lanes] * r1[None]).reshape(depth, LAYER)

    def inner_blocks(side):
        return [b for b in blocks if b != edge_rows[side]]

    def apply_inner(side, outs, write):
        lanes = edge_lanes[side]
        b0, b1, b2 = inner_blocks(side)
        if side == 0:
            pair, single = (b0, b1), b2
        else:
            pair, single = (b1, b2), b0
        rp = (r_ref[pair[0], lanes], r_ref[pair[1], lanes])
        rs = r_ref[single, lanes]
        for out in outs:
            q = jnp.concatenate([product_pair(out, pair, lanes, rp), product(out, single, lanes, rs)], axis=0)
            write(out, lanes, dot(sum_rows2, q))

    def transposed(out, into, lanes):
        rows = [i for b in into for i in range(b.start, b.stop)]

        def term(i):
            row = jnp.broadcast_to(gf[i : i + 1, lanes], (BLOCK, LAYER)).astype(BF16)
            return a_ref[i, out, lanes] * row

        pieces = [term(rows[i]) + term(rows[i + 1]) for i in range(0, len(rows), 2)]
        return dot(groups(BLOCK * len(pieces)), jnp.concatenate(pieces, axis=0))

    loads[1].wait()
    hist[0] = joined(dot(split(st[...]), pa[...]))
    for side in (0, 1):
        rim_out[0, side] = hist[0, edge_rows[side], edge_lanes[side]].astype(BF16)
    pl.semaphore_wait(barrier, n_space - 1 + beside(1))
    start_rims(0)
    tell(1)

    for c in loads[2:]:
        c.wait()
    goal[...] = dot(tgt_raw[...], pa[...])
    adj[...] = joined(dot(split(adj_raw[...]), pa[...]))
    for k in range(steps):
        ctl[k] = dot(ctl_raw[k], pa[...]).astype(BF16)
    piece = depth // nodes

    def permute(part):
        a_loads[part].wait()
        for i in range(part * chunk, (part + 1) * chunk, piece):
            rows = a_raw[i : i + piece].reshape(depth, elements)
            a_ref[i : i + piece] = dot(rows, pa[...]).astype(BF16).reshape(piece, nodes, elements)

    def prepare(k):
        u = hist[k]
        c = ctl[k].astype(F32)
        base = u + TIME_STEP * (u - u * u * u) + TIME_STEP * PENALTY * jumps_inside(u) + TIME_STEP * c
        r_ref[...] = base.astype(BF16)
        for side in (0, 1):
            edge[side] = base[edge_rows[side], edge_lanes[side]]

    def keep(k):
        def write(rows, lanes, v):
            hist[k + 1, rows, lanes] = v

        return write

    def count_cost(k):
        c = ctl[k].astype(F32)
        w = jnp.where(k > 0, weight(k), 0.0)
        d = hist[k] - goal[...]
        cost[...] += 0.5 * w * fold(d * d) + 0.5 * REGULAR * fold(c * c)

    def right_edges(k):
        return [
            (edge[side] + TIME_STEP * PENALTY * rim_in[k, side].astype(F32)).astype(BF16) for side in (0, 1)
        ]

    def step_edges(k, right):
        for side, (rows, lanes) in enumerate(zip(edge_rows, edge_lanes)):
            v = hist[k + 1, rows, lanes] + dot(sum_rows, product(rows, rows, lanes, right[side]))
            hist[k + 1, rows, lanes] = v
            rim_out[k + 1, side] = v.astype(BF16)

    def step_rest(k, right):
        for side, (rows, lanes) in enumerate(zip(edge_rows, edge_lanes)):
            for out in inner_blocks(side):
                hist[k + 1, out, lanes] += dot(sum_rows, product(out, rows, lanes, right[side]))

    prepare(0)
    for part in outer:
        permute(part)
    for side in (0, 1):
        apply_inner(side, [edge_rows[side]], keep(0))
    wait_rims(0)
    first_right = right_edges(0)
    step_edges(0, first_right)
    if steps > 1:
        start_rims(1)
    for part in inner:
        permute(part)
    for side in (0, 1):
        apply_inner(side, inner_blocks(side), keep(0))
    step_rest(0, first_right)
    count_cost(0)
    hear(1)
    tell(2)

    def forward(k, carry):
        prepare(k)
        for side in (0, 1):
            apply_inner(side, blocks, keep(k))
        count_cost(k)
        wait_rims(k)
        right = right_edges(k)
        step_edges(k, right)

        @pl.when(k < steps - 1)
        def _():
            start_rims(k + 1)

        step_rest(k, right)
        return carry

    lax.fori_loop(1, steps, forward, 0)
    for j in range(2, bits):
        hear(j)
        tell(j + 1)

    w_end = weight(steps)
    u = hist[steps]
    d = u - goal[...]
    cost[...] += 0.5 * w_end * fold(d * d)
    gf[...] = w_end * d + adj[...]

    for side, (rows, lanes) in enumerate(zip(edge_rows, edge_lanes)):
        v = transposed(rows, blocks, lanes)
        pulled[rows, lanes] = v
        rim_out[steps, side] = v.astype(BF16)
    start_rims(steps)

    st_out[...] = hist[steps].astype(BF16)

    def st_copy(dst):
        return pltpu.make_async_remote_copy(
            src_ref=st_out, dst_ref=st_in, send_sem=st_sem.at[0], recv_sem=st_sem.at[1],
            device_id={"tm": dst}, device_id_type=pl.DeviceIdType.MESH)

    slot_s[me] = cost[...]

    def gather_copy(slots, send, recv, axis, index, count, d):
        return pltpu.make_async_remote_copy(
            src_ref=slots.at[index], dst_ref=slots.at[index], send_sem=send.at[d], recv_sem=recv.at[index],
            device_id={axis: lax.rem(index + d, count)}, device_id_type=pl.DeviceIdType.MESH)

    def gather_wait(slots, send, recv, axis, index, count, d):
        gather_copy(slots, send, recv, axis, index, count, d).wait_send()
        origin = lax.rem(index + d, count)
        pltpu.make_async_remote_copy(
            src_ref=slots.at[origin], dst_ref=slots.at[origin], send_sem=send.at[d], recv_sem=recv.at[origin],
            device_id={axis: origin}, device_id_type=pl.DeviceIdType.MESH).wait_recv()

    over_s = (slot_s, ss_send, ss_recv, "space", me, n_space)

    def tree_copy(j):
        return pltpu.make_async_remote_copy(
            src_ref=tree_out.at[j], dst_ref=tree_in.at[j], send_sem=tt_send.at[j], recv_sem=tt_recv.at[j],
            device_id={"tm": partner(j)}, device_id_type=pl.DeviceIdType.MESH)

    def tree_sum(j):
        if j == 0:
            for d in range(1, n_space):
                gather_wait(*over_s, d)
            total = slot_s[0]
            for i in range(1, n_space):
                total = total + slot_s[i]
            return total
        tree_copy(j - 1).wait()
        return tree_out[j - 1] + tree_in[j - 1]

    def tree_stage(j):
        tree_out[j] = tree_sum(j)
        tree_copy(j).start()

    early = min(bits, steps - 1)
    for d in range(1, n_space):
        gather_copy(*over_s, d).start()

    @pl.when(t < n_tm - 1)
    def _():
        st_copy(t + 1).start()

    for side, lanes in enumerate(edge_lanes):
        for out in inner_blocks(side):
            pulled[out, lanes] = transposed(out, blocks, lanes)

    def carry_back(k, p):
        before = hist[k]
        carried = p + TIME_STEP * (1.0 - 3.0 * before * before) * p + TIME_STEP * PENALTY * jumps_inside(p)
        return before, carried

    def update(k, p):
        control = ctl[k].astype(F32)
        fresh = (control - (TIME_STEP * p + REGULAR * control)).astype(BF16)
        newc_ref[k] = dot(fresh, pt[...]).astype(BF16)

    def backward(i, carry):
        k = steps - 1 - i
        rnd = steps + i
        p = pulled[...]
        before, carried = carry_back(k, p)
        gf[...] = weight(k) * (before - goal[...]) + carried
        update(k, p)
        for side, lanes in enumerate(edge_lanes):
            for out in blocks:
                pulled[out, lanes] = transposed(out, inner_blocks(side), lanes)

        for j in range(early):
            pl.when(i == j)(functools.partial(tree_stage, j))

        wait_rims(rnd)
        for side, (rows, lanes) in enumerate(zip(edge_rows, edge_lanes)):
            gf[rows, lanes] += TIME_STEP * PENALTY * rim_in[rnd, side].astype(F32)
        for side, (rows, lanes) in enumerate(zip(edge_rows, edge_lanes)):
            v = pulled[rows, lanes] + transposed(rows, [rows], lanes)
            pulled[rows, lanes] = v
            rim_out[rnd + 1, side] = v.astype(BF16)
        start_rims(rnd + 1)
        for side, (rows, lanes) in enumerate(zip(edge_rows, edge_lanes)):
            for out in inner_blocks(side):
                pulled[out, lanes] += transposed(out, [rows], lanes)
        return carry

    lax.fori_loop(0, steps - 1, backward, 0)

    def adj_copy(dst):
        return pltpu.make_async_remote_copy(
            src_ref=adj_out, dst_ref=adj_in, send_sem=adj_sem.at[0], recv_sem=adj_sem.at[1],
            device_id={"tm": dst}, device_id_type=pl.DeviceIdType.MESH)

    p = pulled[...]
    adj_out[...] = carry_back(0, p)[1].astype(BF16)

    @pl.when(t > 0)
    def _():
        adj_copy(t - 1).start()

    update(0, p)

    @pl.when(t == 0)
    def _():
        nst_ref[0] = st[...]

    @pl.when(t > 0)
    def _():
        st_copy(t - 1).wait_recv()
        nst_ref[0] = dot(st_in[...], pt[...])

    @pl.when(t < n_tm - 1)
    def _():
        st_copy(t + 1).wait_send()

    for j in range(early, bits):
        tree_stage(j)
    total = tree_sum(bits)
    scaled = total * (1.0 / (total_steps * nodes * elements * n_space))
    obj_ref[...] = jnp.sum(jnp.sum(scaled, axis=0, keepdims=True), axis=1, keepdims=True)

    wait_final_rims()

    @pl.when(t == n_tm - 1)
    def _():
        nadj_ref[...] = jnp.zeros_like(nadj_ref)

    @pl.when(t < n_tm - 1)
    def _():
        adj_copy(t + 1).wait_recv()
        gf[...] = adj_in[...].astype(F32)
        for side, (rows, lanes) in enumerate(zip(edge_rows, edge_lanes)):
            gf[rows, lanes] += TIME_STEP * PENALTY * rim_in[final, side].astype(F32)
        nadj_ref[0] = joined(dot(split(gf[...]), pt[...]))

    @pl.when(t > 0)
    def _():
        adj_copy(t - 1).wait_send()


def store_kernel(count, *refs):
    gives = [pltpu.make_async_copy(refs[i], refs[count + i], refs[-1].at[i]) for i in range(count)]
    for c in gives:
        c.start()
    for c in gives:
        c.wait()


def store(values):
    count = len(values)
    return pl.pallas_call(
        functools.partial(store_kernel, count),
        out_shape=tuple(jax.ShapeDtypeStruct(v.shape, v.dtype) for v in values),
        in_specs=[pl.BlockSpec(memory_space=pltpu.VMEM)] * count,
        out_specs=(pl.BlockSpec(memory_space=pltpu.HBM),) * count,
        scratch_shapes=[pltpu.SemaphoreType.DMA((count,))],
        compiler_params=pltpu.CompilerParams(vmem_limit_bytes=4194304),
    )(*values)


def solution(mesh):
    n_space, n_tm = mesh.shape["space"], mesh.shape["tm"]

    def per_device(controls, target, state_in, adjoint_in, block_inverse, numbering):
        steps, nodes, elements = controls.shape
        vm = pl.BlockSpec(memory_space=pltpu.VMEM)
        hbm = pl.BlockSpec(memory_space=pltpu.HBM)
        field = (nodes, elements)
        rounds = 2 * steps
        bits = (n_tm - 1).bit_length()
        dma = pltpu.SemaphoreType.DMA
        new_controls, next_state, next_adjoint, objective = pl.pallas_call(
            functools.partial(kernel, n_space, n_tm),
            out_shape=(
                pltpu.VMEM(controls.shape, BF16),
                pltpu.VMEM(state_in.shape, F32),
                pltpu.VMEM(adjoint_in.shape, F32),
                pltpu.VMEM((1, 1), F32),
            ),
            in_specs=[hbm] * 6,
            out_specs=(vm, vm, vm, vm),
            scratch_shapes=[
                pltpu.VMEM(block_inverse.shape, BF16),
                pltpu.VMEM(block_inverse.shape, BF16),
                pltpu.VMEM(numbering.shape, jnp.int32),
                pltpu.VMEM(controls.shape, BF16),
                pltpu.VMEM(controls.shape, BF16),
                pltpu.VMEM(field, BF16),
                pltpu.VMEM(field, F32),
                pltpu.VMEM(field, F32),
                pltpu.VMEM(field, F32),
                pltpu.VMEM(field, F32),
                pltpu.VMEM((steps + 1,) + field, F32),
                pltpu.VMEM(field, BF16),
                pltpu.VMEM((2, BLOCK, LAYER), F32),
                pltpu.VMEM(field, F32),
                pltpu.VMEM(field, F32),
                pltpu.VMEM((elements, elements), BF16),
                pltpu.VMEM((elements, elements), BF16),
                pltpu.VMEM((8, 128), F32),
                pltpu.VMEM((rounds, 2, BLOCK, LAYER), BF16),
                pltpu.VMEM((rounds, 2, BLOCK, LAYER), BF16),
                pltpu.VMEM(field, BF16),
                pltpu.VMEM(field, BF16),
                pltpu.VMEM(field, BF16),
                pltpu.VMEM(field, BF16),
                pltpu.VMEM((n_space, 8, 128), F32),
                pltpu.VMEM((bits, 8, 128), F32),
                pltpu.VMEM((bits, 8, 128), F32),
                dma((5,)),
                dma((4,)),
                dma((rounds, 2)),
                dma((rounds, 2)),
                dma((2,)),
                dma((2,)),
                dma((n_space,)),
                dma((n_space,)),
                dma((bits,)),
                dma((bits,)),
                pltpu.SemaphoreType.REGULAR((bits,)),
            ],
            compiler_params=pltpu.CompilerParams(
                collective_id=0, has_side_effects=True, vmem_limit_bytes=60000000
            ),
        )(numbering, controls, target, state_in, adjoint_in, block_inverse)
        out = store((new_controls, next_state, next_adjoint, objective))
        return out[:3] + (out[3].reshape(()),)

    return jax.shard_map(
        per_device,
        mesh=mesh,
        in_specs=(
            P("tm", None, "space"),
            P(None, "space"),
            P("tm", None, "space"),
            P("tm", None, "space"),
            P(None, None, "space"),
            P("space", None),
        ),
        out_specs=(P("tm", None, "space"), P("tm", None, "space"), P("tm", None, "space"), P()),
        check_vma=False,
    )
```

```python
import functools

import jax
import jax.numpy as jnp
from jax import lax
from jax.experimental import pallas as pl
from jax.experimental.pallas import tpu as pltpu
from jax.sharding import PartitionSpec as P

NSIDE = 4
EXY = 16
BLOCK = NSIDE * NSIDE
LAYER = EXY * EXY
TIME_STEP = 0.1
PENALTY = 0.5
REGULAR = 0.1
F32 = jnp.float32
BF16 = jnp.bfloat16


def dot(a, b):
    return jnp.dot(a, b, preferred_element_type=F32)


def fold(x):
    total = None
    for i in range(0, x.shape[0], 8):
        for j in range(0, x.shape[1], 128):
            piece = x[i : i + 8, j : j + 128]
            total = piece if total is None else total + piece
    return total


def lateral(x):
    rows, lanes = x.shape
    q = lax.broadcasted_iota(jnp.int32, x.shape, 0)
    s = lax.broadcasted_iota(jnp.int32, x.shape, 1)
    a, b = q % NSIDE, (q // NSIDE) % NSIDE
    col, row = s % EXY, (s // EXY) % EXY
    last = NSIDE - 1

    def along(which, node_step, place, lane_step):
        back = (EXY - 1) * lane_step
        low = which == 0
        z = jnp.where(low, pltpu.roll(x, rows - last * node_step, 0), pltpu.roll(x, last * node_step, 0))
        down = jnp.where(place == 0, pltpu.roll(z, lanes - back, 1), pltpu.roll(z, lane_step, 1))
        up = jnp.where(place == EXY - 1, pltpu.roll(z, back, 1), pltpu.roll(z, lanes - lane_step, 1))
        return jnp.where(low, down, jnp.where(which == last, up, 0.0))

    return along(a, 1, col, 1) + along(b, NSIDE, row, EXY)


def face_count(shape):
    q = lax.broadcasted_iota(jnp.int32, shape, 0)
    count = jnp.zeros(shape, F32)
    for step in (1, NSIDE, BLOCK):
        at = (q // step) % NSIDE
        count += jnp.where((at == 0) | (at == NSIDE - 1), 1.0, 0.0)
    return count


def jumps_inside(x):
    nodes, elements = x.shape
    low, high = slice(0, BLOCK), slice(nodes - BLOCK, nodes)
    empty = jnp.zeros((BLOCK, LAYER), F32)
    below = jnp.concatenate([empty, x[high, : elements - LAYER]], axis=1)
    above = jnp.concatenate([x[low, LAYER:], empty], axis=1)
    middle = jnp.zeros((nodes - 2 * BLOCK, elements), F32)
    return lateral(x) + jnp.concatenate([below, middle, above], axis=0) - face_count(x.shape) * x


def kernel(
    n_space, n_tm,
    num_hbm, ctl_hbm, tgt_hbm, st_hbm, adj_hbm, a_hbm,
    newc_ref, nst_ref, nadj_ref, obj_ref,
    a_raw, a_ref, num, ctl_raw, ctl, tgt_raw, goal, adj_raw, adj, st, hist, r_ref, edge, gf, pulled, pa, pt,
    cost, rim_out, rim_in, st_out, st_in, adj_out, adj_in, rate_out, rate_in, face_out, face_in, slot_s, tree_out, tree_in,
    in_sem, a_sem, rim_send, rim_recv, st_sem, adj_sem,
    ss_send, ss_recv, tt_send, tt_recv, ready,
):
    steps, nodes, elements = ctl.shape
    me = lax.axis_index("space")
    t = lax.axis_index("tm")
    first = t * steps
    total_steps = steps * n_tm
    rounds = 2 * steps
    final = rounds - 1
    last_block = nodes - BLOCK
    blocks = [slice(s, s + BLOCK) for s in range(0, nodes, BLOCK)]
    edge_rows = (slice(0, BLOCK), slice(last_block, nodes))
    edge_lanes = (slice(0, LAYER), slice(elements - LAYER, elements))

    def weight(k):
        return (first + k).astype(F32) / total_steps

    loads = [
        pltpu.make_async_copy(src, dst, in_sem.at[i])
        for i, (src, dst) in enumerate(
            ((num_hbm, num), (st_hbm.at[0], st), (tgt_hbm, tgt_raw), (ctl_hbm, ctl_raw), (adj_hbm.at[0], adj_raw))
        )
    ]
    for c in loads[:2]:
        c.start()
    rim_in[...] = jnp.zeros_like(rim_in)
    barrier = pltpu.get_barrier_semaphore()
    for d in range(1, n_space):
        pl.semaphore_signal(barrier, inc=1, device_id={"space": lax.rem(me + d, n_space)},
                            device_id_type=pl.DeviceIdType.MESH)
    bits = (n_tm - 1).bit_length()

    def partner(j):
        size = 2**j
        return t + size - 2 * size * ((t // size) % 2)

    def beside(far):
        return jnp.where(t >= far, 1, 0) + jnp.where(t + far < n_tm, 1, 0)

    def greet(sem, far):
        @pl.when(t >= far)
        def _():
            pl.semaphore_signal(sem, inc=1, device_id={"tm": t - far}, device_id_type=pl.DeviceIdType.MESH)

        @pl.when(t + far < n_tm)
        def _():
            pl.semaphore_signal(sem, inc=1, device_id={"tm": t + far}, device_id_type=pl.DeviceIdType.MESH)

    greet(barrier, 1)

    def tell(j):
        if 0 < j < bits:
            greet(ready.at[j], 2 ** (j - 1))

    def hear(j):
        if 0 < j < bits:
            pl.semaphore_wait(ready.at[j], beside(2 ** (j - 1)))

    parts = a_sem.shape[0]
    chunk = nodes // parts
    a_loads = [
        pltpu.make_async_copy(a_hbm.at[pl.ds(i * chunk, chunk)], a_raw.at[pl.ds(i * chunk, chunk)], a_sem.at[i])
        for i in range(parts)
    ]
    outer = [0, parts - 1]
    inner = list(range(1, parts - 1))
    for i in outer + inner:
        a_loads[i].start()
    for c in loads[2:]:
        c.start()
    cost[...] = jnp.zeros_like(cost)

    loads[0].wait()
    own = num[...]
    for i in range(0, elements, LAYER):
        place = lax.broadcasted_iota(jnp.int32, (LAYER, elements), 0) + i
        pt[i : i + LAYER, :] = jnp.where(own == place, 1.0, 0.0).astype(BF16)
    down = jnp.broadcast_to(own.astype(F32), (128, elements)).T
    for i in range(0, elements, 128):
        place = lax.broadcasted_iota(jnp.int32, (elements, 128), 1) + i
        pa[:, i : i + 128] = jnp.where(down == place.astype(F32), 1.0, 0.0).astype(BF16)

    def split(x):
        high = x.astype(BF16)
        return jnp.concatenate([high, (x - high.astype(F32)).astype(BF16)], axis=0)

    def joined(x):
        return x[:nodes] + x[nodes:]

    def rim_peer(rnd, side):
        return {"tm": t - jnp.where(rnd == final, 1, 0), "space": me - 1 if side == 0 else me + 1}

    def rim_copy(rnd, side, slot):
        return pltpu.make_async_remote_copy(
            src_ref=rim_out.at[rnd, side], dst_ref=rim_in.at[rnd, slot],
            send_sem=rim_send.at[rnd, side], recv_sem=rim_recv.at[rnd, slot],
            device_id=rim_peer(rnd, side), device_id_type=pl.DeviceIdType.MESH,
        )

    def at_side(side):
        return me > 0 if side == 0 else me < n_space - 1

    def start_rims(rnd):
        for side in (0, 1):
            @pl.when(at_side(side) & ((rnd < final) | (t > 0)))
            def _():
                rim_copy(rnd, side, 1 - side).start()

    def wait_rims(rnd):
        for side in (0, 1):
            @pl.when(at_side(side))
            def _():
                rim_copy(rnd, side, side).wait()

    def wait_final_rims():
        for side in (0, 1):
            @pl.when(at_side(side) & (t < n_tm - 1))
            def _():
                rim_copy(final, side, side).wait_recv()

            @pl.when(at_side(side) & (t > 0))
            def _():
                rim_copy(final, side, side).wait_send()

    depth = BLOCK * BLOCK
    place_k = lax.broadcasted_iota(jnp.int32, (BLOCK, depth), 1)
    place_r = lax.broadcasted_iota(jnp.int32, (BLOCK, depth), 0)
    sum_rows = jnp.where(place_k // BLOCK == place_r, 1.0, 0.0).astype(BF16)
    sum_groups = jnp.where(place_k % BLOCK == place_r, 1.0, 0.0).astype(BF16)
    sum_rows2 = jnp.concatenate([sum_rows, sum_rows], axis=1)

    def groups(n):
        place_c = lax.broadcasted_iota(jnp.int32, (BLOCK, n), 1) % BLOCK
        return jnp.where(place_c == lax.broadcasted_iota(jnp.int32, (BLOCK, n), 0), 1.0, 0.0).astype(BF16)

    def product(out, into, lanes, right):
        return (a_ref[out, into, lanes] * right[None]).reshape(depth, LAYER)

    def product_pair(out, into, lanes, right):
        (i0, i1), (r0, r1) = into, right
        return (a_ref[out, i0, lanes] * r0[None] + a_ref[out, i1, lanes] * r1[None]).reshape(depth, LAYER)

    def inner_blocks(side):
        return [b for b in blocks if b != edge_rows[side]]

    def apply_inner(side, outs, write):
        lanes = edge_lanes[side]
        b0, b1, b2 = inner_blocks(side)
        if side == 0:
            pair, single = (b0, b1), b2
        else:
            pair, single = (b1, b2), b0
        rp = (r_ref[pair[0], lanes], r_ref[pair[1], lanes])
        rs = r_ref[single, lanes]
        for out in outs:
            q = jnp.concatenate([product_pair(out, pair, lanes, rp), product(out, single, lanes, rs)], axis=0)
            write(out, lanes, dot(sum_rows2, q))

    def transposed(out, into, lanes):
        rows = [i for b in into for i in range(b.start, b.stop)]

        def term(i):
            row = jnp.broadcast_to(gf[i : i + 1, lanes], (BLOCK, LAYER)).astype(BF16)
            return a_ref[i, out, lanes] * row

        pieces = [term(rows[i]) + term(rows[i + 1]) for i in range(0, len(rows), 2)]
        return dot(groups(BLOCK * len(pieces)), jnp.concatenate(pieces, axis=0))

    loads[1].wait()
    hist[0] = joined(dot(split(st[...]), pa[...]))
    for side in (0, 1):
        rim_out[0, side] = hist[0, edge_rows[side], edge_lanes[side]].astype(BF16)
    pl.semaphore_wait(barrier, n_space - 1 + beside(1))
    start_rims(0)
    tell(1)

    for c in loads[2:]:
        c.wait()
    goal[...] = dot(tgt_raw[...], pa[...])
    adj[...] = joined(dot(split(adj_raw[...]), pa[...]))
    for k in range(steps):
        ctl[k] = dot(ctl_raw[k], pa[...]).astype(BF16)
    piece = depth // nodes

    def permute(part):
        a_loads[part].wait()
        for i in range(part * chunk, (part + 1) * chunk, piece):
            rows = a_raw[i : i + piece].reshape(depth, elements)
            a_ref[i : i + piece] = dot(rows, pa[...]).astype(BF16).reshape(piece, nodes, elements)

    def prepare(k):
        u = hist[k]
        c = ctl[k].astype(F32)
        base = u + TIME_STEP * (u - u * u * u) + TIME_STEP * PENALTY * jumps_inside(u) + TIME_STEP * c
        r_ref[...] = base.astype(BF16)
        for side in (0, 1):
            edge[side] = base[edge_rows[side], edge_lanes[side]]

    def keep(k):
        def write(rows, lanes, v):
            hist[k + 1, rows, lanes] = v

        return write

    def count_cost(k):
        c = ctl[k].astype(F32)
        w = jnp.where(k > 0, weight(k), 0.0)
        d = hist[k] - goal[...]
        cost[...] += 0.5 * w * fold(d * d) + 0.5 * REGULAR * fold(c * c)

    def right_edges(k):
        return [
            (edge[side] + TIME_STEP * PENALTY * rim_in[k, side].astype(F32)).astype(BF16) for side in (0, 1)
        ]

    def step_edges(k, right):
        for side, (rows, lanes) in enumerate(zip(edge_rows, edge_lanes)):
            v = hist[k + 1, rows, lanes] + dot(sum_rows, product(rows, rows, lanes, right[side]))
            hist[k + 1, rows, lanes] = v
            rim_out[k + 1, side] = v.astype(BF16)

    def step_rest(k, right):
        for side, (rows, lanes) in enumerate(zip(edge_rows, edge_lanes)):
            for out in inner_blocks(side):
                hist[k + 1, out, lanes] += dot(sum_rows, product(out, rows, lanes, right[side]))

    prepare(0)
    for part in outer:
        permute(part)
    for side in (0, 1):
        apply_inner(side, [edge_rows[side]], keep(0))
    wait_rims(0)
    first_right = right_edges(0)
    step_edges(0, first_right)
    if steps > 1:
        start_rims(1)
    for part in inner:
        permute(part)
    for side in (0, 1):
        apply_inner(side, inner_blocks(side), keep(0))
    step_rest(0, first_right)
    count_cost(0)
    hear(1)
    tell(2)

    def forward(k, carry):
        prepare(k)
        for side in (0, 1):
            apply_inner(side, blocks, keep(k))
        count_cost(k)
        wait_rims(k)
        right = right_edges(k)
        step_edges(k, right)

        @pl.when(k < steps - 1)
        def _():
            start_rims(k + 1)

        step_rest(k, right)
        return carry

    lax.fori_loop(1, steps, forward, 0)
    for j in range(2, bits):
        hear(j)
        tell(j + 1)

    w_end = weight(steps)
    u = hist[steps]
    d = u - goal[...]
    cost[...] += 0.5 * w_end * fold(d * d)
    gf[...] = w_end * d + adj[...]

    for side, (rows, lanes) in enumerate(zip(edge_rows, edge_lanes)):
        v = transposed(rows, blocks, lanes)
        pulled[rows, lanes] = v
        rim_out[steps, side] = v.astype(BF16)
    start_rims(steps)

    st_out[...] = hist[steps].astype(BF16)

    def st_copy(dst):
        return pltpu.make_async_remote_copy(
            src_ref=st_out, dst_ref=st_in, send_sem=st_sem.at[0], recv_sem=st_sem.at[1],
            device_id={"tm": dst}, device_id_type=pl.DeviceIdType.MESH)

    def back_copy(i, dst):
        src, land = ((rate_out, rate_in), (adj_out, adj_in), (face_out, face_in))[i]
        return pltpu.make_async_remote_copy(
            src_ref=src, dst_ref=land, send_sem=adj_sem.at[0, i], recv_sem=adj_sem.at[1, i],
            device_id={"tm": dst}, device_id_type=pl.DeviceIdType.MESH)

    def send_back(i):
        @pl.when(t > 0)
        def _():
            back_copy(i, t - 1).start()

    slot_s[me] = cost[...]

    def gather_copy(slots, send, recv, axis, index, count, d):
        return pltpu.make_async_remote_copy(
            src_ref=slots.at[index], dst_ref=slots.at[index], send_sem=send.at[d], recv_sem=recv.at[index],
            device_id={axis: lax.rem(index + d, count)}, device_id_type=pl.DeviceIdType.MESH)

    def gather_wait(slots, send, recv, axis, index, count, d):
        gather_copy(slots, send, recv, axis, index, count, d).wait_send()
        origin = lax.rem(index + d, count)
        pltpu.make_async_remote_copy(
            src_ref=slots.at[origin], dst_ref=slots.at[origin], send_sem=send.at[d], recv_sem=recv.at[origin],
            device_id={axis: origin}, device_id_type=pl.DeviceIdType.MESH).wait_recv()

    over_s = (slot_s, ss_send, ss_recv, "space", me, n_space)

    def tree_copy(j):
        return pltpu.make_async_remote_copy(
            src_ref=tree_out.at[j], dst_ref=tree_in.at[j], send_sem=tt_send.at[j], recv_sem=tt_recv.at[j],
            device_id={"tm": partner(j)}, device_id_type=pl.DeviceIdType.MESH)

    def tree_sum(j):
        if j == 0:
            for d in range(1, n_space):
                gather_wait(*over_s, d)
            total = slot_s[0]
            for i in range(1, n_space):
                total = total + slot_s[i]
            return total
        tree_copy(j - 1).wait()
        return tree_out[j - 1] + tree_in[j - 1]

    def tree_stage(j):
        tree_out[j] = tree_sum(j)
        tree_copy(j).start()

    def rate(k):
        before = hist[k]
        return 1.0 + TIME_STEP * (1.0 - 3.0 * before * before)

    early = min(bits, steps - 1)
    for d in range(1, n_space):
        gather_copy(*over_s, d).start()

    @pl.when(t < n_tm - 1)
    def _():
        st_copy(t + 1).start()

    rate_out[...] = rate(0).astype(BF16)
    send_back(0)

    for side, lanes in enumerate(edge_lanes):
        for out in inner_blocks(side):
            pulled[out, lanes] = transposed(out, blocks, lanes)

    def carry_back(factor, p):
        return factor * p + TIME_STEP * PENALTY * jumps_inside(p)

    def update(k, p):
        control = ctl[k].astype(F32)
        fresh = (control - (TIME_STEP * p + REGULAR * control)).astype(BF16)
        newc_ref[k] = dot(fresh, pt[...]).astype(BF16)

    def backward(i, carry):
        k = steps - 1 - i
        rnd = steps + i
        p = pulled[...]
        gf[...] = weight(k) * (hist[k] - goal[...]) + carry_back(rate(k), p)
        update(k, p)
        for side, lanes in enumerate(edge_lanes):
            for out in blocks:
                pulled[out, lanes] = transposed(out, inner_blocks(side), lanes)

        @pl.when(i == steps - 2)
        def _():
            adj_out[...] = carry_back(rate(0), pulled[...]).astype(BF16)
            send_back(1)

        wait_rims(rnd)
        for side, (rows, lanes) in enumerate(zip(edge_rows, edge_lanes)):
            g = gf[rows, lanes] + TIME_STEP * PENALTY * rim_in[rnd, side].astype(F32)
            gf[rows, lanes] = g
            face_out[side] = g.astype(BF16)

        @pl.when(i == steps - 2)
        def _():
            send_back(2)

        for side, (rows, lanes) in enumerate(zip(edge_rows, edge_lanes)):
            v = pulled[rows, lanes] + transposed(rows, [rows], lanes)
            pulled[rows, lanes] = v
            rim_out[rnd + 1, side] = v.astype(BF16)
        start_rims(rnd + 1)
        for side, (rows, lanes) in enumerate(zip(edge_rows, edge_lanes)):
            for out in inner_blocks(side):
                pulled[out, lanes] += transposed(out, [rows], lanes)
        for j in range(early):
            pl.when(i == j)(functools.partial(tree_stage, j))
        return carry

    lax.fori_loop(0, steps - 1, backward, 0)

    update(0, pulled[...])

    @pl.when(t == 0)
    def _():
        nst_ref[0] = st[...]

    @pl.when(t > 0)
    def _():
        st_copy(t - 1).wait_recv()
        nst_ref[0] = dot(st_in[...], pt[...])

    @pl.when(t < n_tm - 1)
    def _():
        st_copy(t + 1).wait_send()

    for j in range(early, bits):
        tree_stage(j)
    total = tree_sum(bits)
    scaled = total * (1.0 / (total_steps * nodes * elements * n_space))
    obj_ref[...] = jnp.sum(jnp.sum(scaled, axis=0, keepdims=True), axis=1, keepdims=True)

    @pl.when(t == n_tm - 1)
    def _():
        nadj_ref[...] = jnp.zeros_like(nadj_ref)

    @pl.when(t < n_tm - 1)
    def _():
        for i in (0, 2):
            back_copy(i, t + 1).wait_recv()
        for side, (rows, lanes) in enumerate(zip(edge_rows, edge_lanes)):
            gf[rows, lanes] = face_in[side].astype(F32)
        for side, (rows, lanes) in enumerate(zip(edge_rows, edge_lanes)):
            for out in blocks:
                pulled[out, lanes] = transposed(out, [rows], lanes)
        gf[...] = carry_back(rate_in[...].astype(F32), pulled[...])
        back_copy(1, t + 1).wait_recv()

    wait_final_rims()

    @pl.when(t < n_tm - 1)
    def _():
        for side, (rows, lanes) in enumerate(zip(edge_rows, edge_lanes)):
            gf[rows, lanes] += TIME_STEP * PENALTY * rim_in[final, side].astype(F32)
        nadj_ref[0] = joined(dot(split(gf[...] + adj_in[...].astype(F32)), pt[...]))

    @pl.when(t > 0)
    def _():
        for i in range(3):
            back_copy(i, t - 1).wait_send()


def store_kernel(count, *refs):
    gives = [pltpu.make_async_copy(refs[i], refs[count + i], refs[-1].at[i]) for i in range(count)]
    for c in gives:
        c.start()
    for c in gives:
        c.wait()


def store(values):
    count = len(values)
    return pl.pallas_call(
        functools.partial(store_kernel, count),
        out_shape=tuple(jax.ShapeDtypeStruct(v.shape, v.dtype) for v in values),
        in_specs=[pl.BlockSpec(memory_space=pltpu.VMEM)] * count,
        out_specs=(pl.BlockSpec(memory_space=pltpu.HBM),) * count,
        scratch_shapes=[pltpu.SemaphoreType.DMA((count,))],
        compiler_params=pltpu.CompilerParams(vmem_limit_bytes=4194304),
    )(*values)


def solution(mesh):
    n_space, n_tm = mesh.shape["space"], mesh.shape["tm"]

    def per_device(controls, target, state_in, adjoint_in, block_inverse, numbering):
        steps, nodes, elements = controls.shape
        vm = pl.BlockSpec(memory_space=pltpu.VMEM)
        hbm = pl.BlockSpec(memory_space=pltpu.HBM)
        field = (nodes, elements)
        rounds = 2 * steps
        bits = (n_tm - 1).bit_length()
        dma = pltpu.SemaphoreType.DMA
        new_controls, next_state, next_adjoint, objective = pl.pallas_call(
            functools.partial(kernel, n_space, n_tm),
            out_shape=(
                pltpu.VMEM(controls.shape, BF16),
                pltpu.VMEM(state_in.shape, F32),
                pltpu.VMEM(adjoint_in.shape, F32),
                pltpu.VMEM((1, 1), F32),
            ),
            in_specs=[hbm] * 6,
            out_specs=(vm, vm, vm, vm),
            scratch_shapes=[
                pltpu.VMEM(block_inverse.shape, BF16),
                pltpu.VMEM(block_inverse.shape, BF16),
                pltpu.VMEM(numbering.shape, jnp.int32),
                pltpu.VMEM(controls.shape, BF16),
                pltpu.VMEM(controls.shape, BF16),
                pltpu.VMEM(field, BF16),
                pltpu.VMEM(field, F32),
                pltpu.VMEM(field, F32),
                pltpu.VMEM(field, F32),
                pltpu.VMEM(field, F32),
                pltpu.VMEM((steps + 1,) + field, F32),
                pltpu.VMEM(field, BF16),
                pltpu.VMEM((2, BLOCK, LAYER), F32),
                pltpu.VMEM(field, F32),
                pltpu.VMEM(field, F32),
                pltpu.VMEM((elements, elements), BF16),
                pltpu.VMEM((elements, elements), BF16),
                pltpu.VMEM((8, 128), F32),
                pltpu.VMEM((rounds, 2, BLOCK, LAYER), BF16),
                pltpu.VMEM((rounds, 2, BLOCK, LAYER), BF16),
                pltpu.VMEM(field, BF16),
                pltpu.VMEM(field, BF16),
                pltpu.VMEM(field, BF16),
                pltpu.VMEM(field, BF16),
                pltpu.VMEM(field, BF16),
                pltpu.VMEM(field, BF16),
                pltpu.VMEM((2, BLOCK, LAYER), BF16),
                pltpu.VMEM((2, BLOCK, LAYER), BF16),
                pltpu.VMEM((n_space, 8, 128), F32),
                pltpu.VMEM((bits, 8, 128), F32),
                pltpu.VMEM((bits, 8, 128), F32),
                dma((5,)),
                dma((4,)),
                dma((rounds, 2)),
                dma((rounds, 2)),
                dma((2,)),
                dma((2, 3)),
                dma((n_space,)),
                dma((n_space,)),
                dma((bits,)),
                dma((bits,)),
                pltpu.SemaphoreType.REGULAR((bits,)),
            ],
            compiler_params=pltpu.CompilerParams(
                collective_id=0, has_side_effects=True, vmem_limit_bytes=60000000
            ),
        )(numbering, controls, target, state_in, adjoint_in, block_inverse)
        out = store((new_controls, next_state, next_adjoint, objective))
        return out[:3] + (out[3].reshape(()),)

    return jax.shard_map(
        per_device,
        mesh=mesh,
        in_specs=(
            P("tm", None, "space"),
            P(None, "space"),
            P("tm", None, "space"),
            P("tm", None, "space"),
            P(None, None, "space"),
            P("space", None),
        ),
        out_specs=(P("tm", None, "space"), P("tm", None, "space"), P("tm", None, "space"), P()),
        check_vma=False,
    )
```

```python
import functools

import jax
import jax.numpy as jnp
from jax import lax
from jax.experimental import pallas as pl
from jax.experimental.pallas import tpu as pltpu
from jax.sharding import PartitionSpec as P

NSIDE = 4
EXY = 16
BLOCK = NSIDE * NSIDE
LAYER = EXY * EXY
TIME_STEP = 0.1
PENALTY = 0.5
REGULAR = 0.1
F32 = jnp.float32
BF16 = jnp.bfloat16


def dot(a, b):
    return jnp.dot(a, b, preferred_element_type=F32)


def fold(x):
    total = None
    for i in range(0, x.shape[0], 8):
        for j in range(0, x.shape[1], 128):
            piece = x[i : i + 8, j : j + 128]
            total = piece if total is None else total + piece
    return total


def lateral(x):
    rows, lanes = x.shape
    q = lax.broadcasted_iota(jnp.int32, x.shape, 0)
    s = lax.broadcasted_iota(jnp.int32, x.shape, 1)
    a, b = q % NSIDE, (q // NSIDE) % NSIDE
    col, row = s % EXY, (s // EXY) % EXY
    last = NSIDE - 1

    def along(which, node_step, place, lane_step):
        back = (EXY - 1) * lane_step
        low = which == 0
        z = jnp.where(low, pltpu.roll(x, rows - last * node_step, 0), pltpu.roll(x, last * node_step, 0))
        down = jnp.where(place == 0, pltpu.roll(z, lanes - back, 1), pltpu.roll(z, lane_step, 1))
        up = jnp.where(place == EXY - 1, pltpu.roll(z, back, 1), pltpu.roll(z, lanes - lane_step, 1))
        return jnp.where(low, down, jnp.where(which == last, up, 0.0))

    return along(a, 1, col, 1) + along(b, NSIDE, row, EXY)


def face_count(shape):
    q = lax.broadcasted_iota(jnp.int32, shape, 0)
    count = jnp.zeros(shape, F32)
    for step in (1, NSIDE, BLOCK):
        at = (q // step) % NSIDE
        count += jnp.where((at == 0) | (at == NSIDE - 1), 1.0, 0.0)
    return count


def jumps_inside(x):
    nodes, elements = x.shape
    low, high = slice(0, BLOCK), slice(nodes - BLOCK, nodes)
    empty = jnp.zeros((BLOCK, LAYER), F32)
    below = jnp.concatenate([empty, x[high, : elements - LAYER]], axis=1)
    above = jnp.concatenate([x[low, LAYER:], empty], axis=1)
    middle = jnp.zeros((nodes - 2 * BLOCK, elements), F32)
    return lateral(x) + jnp.concatenate([below, middle, above], axis=0) - face_count(x.shape) * x


def kernel(
    n_space, n_tm,
    num_hbm, ctl_hbm, tgt_hbm, st_hbm, adj_hbm, a_hbm,
    newc_ref, nst_ref, nadj_ref, obj_ref,
    a_raw, a_ref, num, ctl_raw, ctl, tgt_raw, goal, adj_raw, adj, st, hist, r_ref, edge, gf, pulled, pa, pt,
    cost, rim_out, rim_in, st_out, st_in, adj_out, adj_in, rate_out, rate_in, face_out, face_in, slot_s, slot_t,
    in_sem, a_sem, rim_send, rim_recv, st_sem, adj_sem,
    ss_send, ss_recv, tt_send, tt_recv, ready,
):
    steps, nodes, elements = ctl.shape
    me = lax.axis_index("space")
    t = lax.axis_index("tm")
    first = t * steps
    total_steps = steps * n_tm
    rounds = 2 * steps
    final = rounds - 1
    last_block = nodes - BLOCK
    blocks = [slice(s, s + BLOCK) for s in range(0, nodes, BLOCK)]
    edge_rows = (slice(0, BLOCK), slice(last_block, nodes))
    edge_lanes = (slice(0, LAYER), slice(elements - LAYER, elements))

    def weight(k):
        return (first + k).astype(F32) / total_steps

    loads = [
        pltpu.make_async_copy(src, dst, in_sem.at[i])
        for i, (src, dst) in enumerate(
            ((num_hbm, num), (st_hbm.at[0], st), (tgt_hbm, tgt_raw), (ctl_hbm, ctl_raw), (adj_hbm.at[0], adj_raw))
        )
    ]
    for c in loads[:2]:
        c.start()
    rim_in[...] = jnp.zeros_like(rim_in)
    barrier = pltpu.get_barrier_semaphore()
    for d in range(1, n_space):
        pl.semaphore_signal(barrier, inc=1, device_id={"space": lax.rem(me + d, n_space)},
                            device_id_type=pl.DeviceIdType.MESH)
    bits = (n_tm - 1).bit_length()

    def beside(far):
        return jnp.where(t >= far, 1, 0) + jnp.where(t + far < n_tm, 1, 0)

    def greet(sem, far):
        @pl.when(t >= far)
        def _():
            pl.semaphore_signal(sem, inc=1, device_id={"tm": t - far}, device_id_type=pl.DeviceIdType.MESH)

        @pl.when(t + far < n_tm)
        def _():
            pl.semaphore_signal(sem, inc=1, device_id={"tm": t + far}, device_id_type=pl.DeviceIdType.MESH)

    greet(barrier, 1)

    def tell(j):
        if j <= bits:
            greet(ready.at[j - 1], 2 ** (j - 1))

    def hear(j):
        if j <= bits:
            pl.semaphore_wait(ready.at[j - 1], beside(2 ** (j - 1)))

    def pass_on(j):
        hear(j)
        tell(j + 1)

    parts = a_sem.shape[0]
    chunk = nodes // parts
    a_loads = [
        pltpu.make_async_copy(a_hbm.at[pl.ds(i * chunk, chunk)], a_raw.at[pl.ds(i * chunk, chunk)], a_sem.at[i])
        for i in range(parts)
    ]
    outer = [0, parts - 1]
    inner = list(range(1, parts - 1))
    for i in outer + inner:
        a_loads[i].start()
    for c in loads[2:]:
        c.start()
    cost[...] = jnp.zeros_like(cost)

    loads[0].wait()
    own = num[...]
    for i in range(0, elements, LAYER):
        place = lax.broadcasted_iota(jnp.int32, (LAYER, elements), 0) + i
        pt[i : i + LAYER, :] = jnp.where(own == place, 1.0, 0.0).astype(BF16)
    down = jnp.broadcast_to(own.astype(F32), (128, elements)).T
    for i in range(0, elements, 128):
        place = lax.broadcasted_iota(jnp.int32, (elements, 128), 1) + i
        pa[:, i : i + 128] = jnp.where(down == place.astype(F32), 1.0, 0.0).astype(BF16)

    def split(x):
        high = x.astype(BF16)
        return jnp.concatenate([high, (x - high.astype(F32)).astype(BF16)], axis=0)

    def joined(x):
        return x[:nodes] + x[nodes:]

    def rim_peer(rnd, side):
        return {"tm": t - jnp.where(rnd == final, 1, 0), "space": me - 1 if side == 0 else me + 1}

    def rim_copy(rnd, side, slot):
        return pltpu.make_async_remote_copy(
            src_ref=rim_out.at[rnd, side], dst_ref=rim_in.at[rnd, slot],
            send_sem=rim_send.at[rnd, side], recv_sem=rim_recv.at[rnd, slot],
            device_id=rim_peer(rnd, side), device_id_type=pl.DeviceIdType.MESH,
        )

    def at_side(side):
        return me > 0 if side == 0 else me < n_space - 1

    def start_rims(rnd):
        for side in (0, 1):
            @pl.when(at_side(side) & ((rnd < final) | (t > 0)))
            def _():
                rim_copy(rnd, side, 1 - side).start()

    def wait_rims(rnd):
        for side in (0, 1):
            @pl.when(at_side(side))
            def _():
                rim_copy(rnd, side, side).wait()

    def wait_final_rims():
        for side in (0, 1):
            @pl.when(at_side(side) & (t < n_tm - 1))
            def _():
                rim_copy(final, side, side).wait_recv()

            @pl.when(at_side(side) & (t > 0))
            def _():
                rim_copy(final, side, side).wait_send()

    depth = BLOCK * BLOCK
    place_k = lax.broadcasted_iota(jnp.int32, (BLOCK, depth), 1)
    place_r = lax.broadcasted_iota(jnp.int32, (BLOCK, depth), 0)
    sum_rows = jnp.where(place_k // BLOCK == place_r, 1.0, 0.0).astype(BF16)
    sum_groups = jnp.where(place_k % BLOCK == place_r, 1.0, 0.0).astype(BF16)
    sum_rows2 = jnp.concatenate([sum_rows, sum_rows], axis=1)

    def groups(n):
        place_c = lax.broadcasted_iota(jnp.int32, (BLOCK, n), 1) % BLOCK
        return jnp.where(place_c == lax.broadcasted_iota(jnp.int32, (BLOCK, n), 0), 1.0, 0.0).astype(BF16)

    def product(out, into, lanes, right):
        return (a_ref[out, into, lanes] * right[None]).reshape(depth, LAYER)

    def product_pair(out, into, lanes, right):
        (i0, i1), (r0, r1) = into, right
        return (a_ref[out, i0, lanes] * r0[None] + a_ref[out, i1, lanes] * r1[None]).reshape(depth, LAYER)

    def inner_blocks(side):
        return [b for b in blocks if b != edge_rows[side]]

    def apply_inner(side, outs, write):
        lanes = edge_lanes[side]
        b0, b1, b2 = inner_blocks(side)
        if side == 0:
            pair, single = (b0, b1), b2
        else:
            pair, single = (b1, b2), b0
        rp = (r_ref[pair[0], lanes], r_ref[pair[1], lanes])
        rs = r_ref[single, lanes]
        for out in outs:
            q = jnp.concatenate([product_pair(out, pair, lanes, rp), product(out, single, lanes, rs)], axis=0)
            write(out, lanes, dot(sum_rows2, q))

    def transposed(out, into, lanes):
        rows = [i for b in into for i in range(b.start, b.stop)]

        def term(i):
            row = jnp.broadcast_to(gf[i : i + 1, lanes], (BLOCK, LAYER)).astype(BF16)
            return a_ref[i, out, lanes] * row

        pieces = [term(rows[i]) + term(rows[i + 1]) for i in range(0, len(rows), 2)]
        return dot(groups(BLOCK * len(pieces)), jnp.concatenate(pieces, axis=0))

    loads[1].wait()
    hist[0] = joined(dot(split(st[...]), pa[...]))
    for side in (0, 1):
        rim_out[0, side] = hist[0, edge_rows[side], edge_lanes[side]].astype(BF16)
    pl.semaphore_wait(barrier, n_space - 1 + beside(1))
    start_rims(0)
    tell(1)

    for c in loads[2:]:
        c.wait()
    goal[...] = dot(tgt_raw[...], pa[...])
    adj[...] = joined(dot(split(adj_raw[...]), pa[...]))
    for k in range(steps):
        ctl[k] = dot(ctl_raw[k], pa[...]).astype(BF16)
    piece = depth // nodes

    def permute(part):
        a_loads[part].wait()
        for i in range(part * chunk, (part + 1) * chunk, piece):
            rows = a_raw[i : i + piece].reshape(depth, elements)
            a_ref[i : i + piece] = dot(rows, pa[...]).astype(BF16).reshape(piece, nodes, elements)

    def prepare(k):
        u = hist[k]
        c = ctl[k].astype(F32)
        base = u + TIME_STEP * (u - u * u * u) + TIME_STEP * PENALTY * jumps_inside(u) + TIME_STEP * c
        r_ref[...] = base.astype(BF16)
        for side in (0, 1):
            edge[side] = base[edge_rows[side], edge_lanes[side]]

    def keep(k):
        def write(rows, lanes, v):
            hist[k + 1, rows, lanes] = v

        return write

    def count_cost(k):
        c = ctl[k].astype(F32)
        w = jnp.where(k > 0, weight(k), 0.0)
        d = hist[k] - goal[...]
        cost[...] += 0.5 * w * fold(d * d) + 0.5 * REGULAR * fold(c * c)

    def right_edges(k):
        return [
            (edge[side] + TIME_STEP * PENALTY * rim_in[k, side].astype(F32)).astype(BF16) for side in (0, 1)
        ]

    def step_edges(k, right):
        for side, (rows, lanes) in enumerate(zip(edge_rows, edge_lanes)):
            v = hist[k + 1, rows, lanes] + dot(sum_rows, product(rows, rows, lanes, right[side]))
            hist[k + 1, rows, lanes] = v
            rim_out[k + 1, side] = v.astype(BF16)

    def step_rest(k, right):
        for side, (rows, lanes) in enumerate(zip(edge_rows, edge_lanes)):
            for out in inner_blocks(side):
                hist[k + 1, out, lanes] += dot(sum_rows, product(out, rows, lanes, right[side]))

    prepare(0)
    for part in outer:
        permute(part)
    for side in (0, 1):
        apply_inner(side, [edge_rows[side]], keep(0))
    wait_rims(0)
    first_right = right_edges(0)
    step_edges(0, first_right)
    if steps > 1:
        start_rims(1)
    for part in inner:
        permute(part)
    for side in (0, 1):
        apply_inner(side, inner_blocks(side), keep(0))
    step_rest(0, first_right)
    count_cost(0)
    pass_on(1)

    def forward(k, carry):
        prepare(k)
        for side in (0, 1):
            apply_inner(side, blocks, keep(k))
        count_cost(k)
        wait_rims(k)
        right = right_edges(k)
        step_edges(k, right)

        @pl.when(k < steps - 1)
        def _():
            start_rims(k + 1)

        step_rest(k, right)
        for j in range(2, min(bits, steps)):
            pl.when(k == j - 1)(functools.partial(pass_on, j))
        return carry

    lax.fori_loop(1, steps, forward, 0)
    for j in range(max(2, min(bits, steps)), bits + 1):
        pass_on(j)

    w_end = weight(steps)
    u = hist[steps]
    d = u - goal[...]
    cost[...] += 0.5 * w_end * fold(d * d)
    gf[...] = w_end * d + adj[...]

    for side, (rows, lanes) in enumerate(zip(edge_rows, edge_lanes)):
        v = transposed(rows, blocks, lanes)
        pulled[rows, lanes] = v
        rim_out[steps, side] = v.astype(BF16)
    start_rims(steps)

    st_out[...] = hist[steps].astype(BF16)

    def st_copy(dst):
        return pltpu.make_async_remote_copy(
            src_ref=st_out, dst_ref=st_in, send_sem=st_sem.at[0], recv_sem=st_sem.at[1],
            device_id={"tm": dst}, device_id_type=pl.DeviceIdType.MESH)

    def back_copy(i, dst):
        src, land = ((rate_out, rate_in), (adj_out, adj_in), (face_out, face_in))[i]
        return pltpu.make_async_remote_copy(
            src_ref=src, dst_ref=land, send_sem=adj_sem.at[0, i], recv_sem=adj_sem.at[1, i],
            device_id={"tm": dst}, device_id_type=pl.DeviceIdType.MESH)

    def send_back(i):
        @pl.when(t > 0)
        def _():
            back_copy(i, t - 1).start()

    slot_s[me] = cost[...]

    def gather_copy(slots, send, recv, axis, index, count, d):
        return pltpu.make_async_remote_copy(
            src_ref=slots.at[index], dst_ref=slots.at[index], send_sem=send.at[d], recv_sem=recv.at[index],
            device_id={axis: lax.rem(index + d, count)}, device_id_type=pl.DeviceIdType.MESH)

    def gather_wait(slots, send, recv, axis, index, count, d):
        gather_copy(slots, send, recv, axis, index, count, d).wait_send()
        origin = lax.rem(index + d, count)
        pltpu.make_async_remote_copy(
            src_ref=slots.at[origin], dst_ref=slots.at[origin], send_sem=send.at[d], recv_sem=recv.at[origin],
            device_id={axis: origin}, device_id_type=pl.DeviceIdType.MESH).wait_recv()

    over_s = (slot_s, ss_send, ss_recv, "space", me, n_space)

    over_t = (slot_t, tt_send, tt_recv, "tm", t, n_tm)

    def gathered(slots, *rest):
        count = rest[-1]
        for d in range(1, count):
            gather_wait(slots, *rest, d)
        total = slots[0]
        for i in range(1, count):
            total = total + slots[i]
        return total

    def hand_round():
        slot_t[t] = gathered(*over_s)
        for d in range(1, n_tm):
            gather_copy(*over_t, d).start()

    def rate(k):
        before = hist[k]
        return 1.0 + TIME_STEP * (1.0 - 3.0 * before * before)

    for d in range(1, n_space):
        gather_copy(*over_s, d).start()

    @pl.when(t < n_tm - 1)
    def _():
        st_copy(t + 1).start()

    rate_out[...] = rate(0).astype(BF16)
    send_back(0)

    for side, lanes in enumerate(edge_lanes):
        for out in inner_blocks(side):
            pulled[out, lanes] = transposed(out, blocks, lanes)

    def carry_back(factor, p):
        return factor * p + TIME_STEP * PENALTY * jumps_inside(p)

    def update(k, p):
        control = ctl[k].astype(F32)
        fresh = (control - (TIME_STEP * p + REGULAR * control)).astype(BF16)
        newc_ref[k] = dot(fresh, pt[...]).astype(BF16)

    def backward(i, carry):
        k = steps - 1 - i
        rnd = steps + i
        p = pulled[...]
        gf[...] = weight(k) * (hist[k] - goal[...]) + carry_back(rate(k), p)
        update(k, p)
        for side, lanes in enumerate(edge_lanes):
            for out in blocks:
                pulled[out, lanes] = transposed(out, inner_blocks(side), lanes)

        @pl.when(i == steps - 2)
        def _():
            adj_out[...] = carry_back(rate(0), pulled[...]).astype(BF16)
            send_back(1)

        wait_rims(rnd)
        for side, (rows, lanes) in enumerate(zip(edge_rows, edge_lanes)):
            g = gf[rows, lanes] + TIME_STEP * PENALTY * rim_in[rnd, side].astype(F32)
            gf[rows, lanes] = g
            face_out[side] = g.astype(BF16)

        @pl.when(i == steps - 2)
        def _():
            send_back(2)

        for side, (rows, lanes) in enumerate(zip(edge_rows, edge_lanes)):
            v = pulled[rows, lanes] + transposed(rows, [rows], lanes)
            pulled[rows, lanes] = v
            rim_out[rnd + 1, side] = v.astype(BF16)
        start_rims(rnd + 1)
        for side, (rows, lanes) in enumerate(zip(edge_rows, edge_lanes)):
            for out in inner_blocks(side):
                pulled[out, lanes] += transposed(out, [rows], lanes)
        pl.when(i == 0)(hand_round)
        return carry

    lax.fori_loop(0, steps - 1, backward, 0)

    update(0, pulled[...])

    @pl.when(t == 0)
    def _():
        nst_ref[0] = st[...]

    @pl.when(t > 0)
    def _():
        st_copy(t - 1).wait_recv()
        nst_ref[0] = dot(st_in[...], pt[...])

    @pl.when(t < n_tm - 1)
    def _():
        st_copy(t + 1).wait_send()

    total = gathered(*over_t)
    scaled = total * (1.0 / (total_steps * nodes * elements * n_space))
    obj_ref[...] = jnp.sum(jnp.sum(scaled, axis=0, keepdims=True), axis=1, keepdims=True)

    @pl.when(t == n_tm - 1)
    def _():
        nadj_ref[...] = jnp.zeros_like(nadj_ref)

    @pl.when(t < n_tm - 1)
    def _():
        for i in (0, 2):
            back_copy(i, t + 1).wait_recv()
        for side, (rows, lanes) in enumerate(zip(edge_rows, edge_lanes)):
            gf[rows, lanes] = face_in[side].astype(F32)
        for side, (rows, lanes) in enumerate(zip(edge_rows, edge_lanes)):
            for out in blocks:
                pulled[out, lanes] = transposed(out, [rows], lanes)
        gf[...] = carry_back(rate_in[...].astype(F32), pulled[...])
        back_copy(1, t + 1).wait_recv()

    wait_final_rims()

    @pl.when(t < n_tm - 1)
    def _():
        for side, (rows, lanes) in enumerate(zip(edge_rows, edge_lanes)):
            gf[rows, lanes] += TIME_STEP * PENALTY * rim_in[final, side].astype(F32)
        nadj_ref[0] = joined(dot(split(gf[...] + adj_in[...].astype(F32)), pt[...]))

    @pl.when(t > 0)
    def _():
        for i in range(3):
            back_copy(i, t - 1).wait_send()


def store_kernel(count, *refs):
    gives = [pltpu.make_async_copy(refs[i], refs[count + i], refs[-1].at[i]) for i in range(count)]
    for c in gives:
        c.start()
    for c in gives:
        c.wait()


def store(values):
    count = len(values)
    return pl.pallas_call(
        functools.partial(store_kernel, count),
        out_shape=tuple(jax.ShapeDtypeStruct(v.shape, v.dtype) for v in values),
        in_specs=[pl.BlockSpec(memory_space=pltpu.VMEM)] * count,
        out_specs=(pl.BlockSpec(memory_space=pltpu.HBM),) * count,
        scratch_shapes=[pltpu.SemaphoreType.DMA((count,))],
        compiler_params=pltpu.CompilerParams(vmem_limit_bytes=4194304),
    )(*values)


def solution(mesh):
    n_space, n_tm = mesh.shape["space"], mesh.shape["tm"]

    def per_device(controls, target, state_in, adjoint_in, block_inverse, numbering):
        steps, nodes, elements = controls.shape
        vm = pl.BlockSpec(memory_space=pltpu.VMEM)
        hbm = pl.BlockSpec(memory_space=pltpu.HBM)
        field = (nodes, elements)
        rounds = 2 * steps
        bits = (n_tm - 1).bit_length()
        dma = pltpu.SemaphoreType.DMA
        new_controls, next_state, next_adjoint, objective = pl.pallas_call(
            functools.partial(kernel, n_space, n_tm),
            out_shape=(
                pltpu.VMEM(controls.shape, BF16),
                pltpu.VMEM(state_in.shape, F32),
                pltpu.VMEM(adjoint_in.shape, F32),
                pltpu.VMEM((1, 1), F32),
            ),
            in_specs=[hbm] * 6,
            out_specs=(vm, vm, vm, vm),
            scratch_shapes=[
                pltpu.VMEM(block_inverse.shape, BF16),
                pltpu.VMEM(block_inverse.shape, BF16),
                pltpu.VMEM(numbering.shape, jnp.int32),
                pltpu.VMEM(controls.shape, BF16),
                pltpu.VMEM(controls.shape, BF16),
                pltpu.VMEM(field, BF16),
                pltpu.VMEM(field, F32),
                pltpu.VMEM(field, F32),
                pltpu.VMEM(field, F32),
                pltpu.VMEM(field, F32),
                pltpu.VMEM((steps + 1,) + field, F32),
                pltpu.VMEM(field, BF16),
                pltpu.VMEM((2, BLOCK, LAYER), F32),
                pltpu.VMEM(field, F32),
                pltpu.VMEM(field, F32),
                pltpu.VMEM((elements, elements), BF16),
                pltpu.VMEM((elements, elements), BF16),
                pltpu.VMEM((8, 128), F32),
                pltpu.VMEM((rounds, 2, BLOCK, LAYER), BF16),
                pltpu.VMEM((rounds, 2, BLOCK, LAYER), BF16),
                pltpu.VMEM(field, BF16),
                pltpu.VMEM(field, BF16),
                pltpu.VMEM(field, BF16),
                pltpu.VMEM(field, BF16),
                pltpu.VMEM(field, BF16),
                pltpu.VMEM(field, BF16),
                pltpu.VMEM((2, BLOCK, LAYER), BF16),
                pltpu.VMEM((2, BLOCK, LAYER), BF16),
                pltpu.VMEM((n_space, 8, 128), F32),
                pltpu.VMEM((n_tm, 8, 128), F32),
                dma((5,)),
                dma((4,)),
                dma((rounds, 2)),
                dma((rounds, 2)),
                dma((2,)),
                dma((2, 3)),
                dma((n_space,)),
                dma((n_space,)),
                dma((n_tm,)),
                dma((n_tm,)),
                pltpu.SemaphoreType.REGULAR((bits,)),
            ],
            compiler_params=pltpu.CompilerParams(
                collective_id=0, has_side_effects=True, vmem_limit_bytes=60000000
            ),
        )(numbering, controls, target, state_in, adjoint_in, block_inverse)
        out = store((new_controls, next_state, next_adjoint, objective))
        return out[:3] + (out[3].reshape(()),)

    return jax.shard_map(
        per_device,
        mesh=mesh,
        in_specs=(
            P("tm", None, "space"),
            P(None, "space"),
            P("tm", None, "space"),
            P("tm", None, "space"),
            P(None, None, "space"),
            P("space", None),
        ),
        out_specs=(P("tm", None, "space"), P("tm", None, "space"), P("tm", None, "space"), P()),
        check_vma=False,
    )
```

```python
import functools

import jax
import jax.numpy as jnp
from jax import lax
from jax.experimental import pallas as pl
from jax.experimental.pallas import tpu as pltpu
from jax.sharding import PartitionSpec as P

NSIDE = 4
EXY = 16
BLOCK = NSIDE * NSIDE
LAYER = EXY * EXY
TIME_STEP = 0.1
PENALTY = 0.5
REGULAR = 0.1
F32 = jnp.float32
BF16 = jnp.bfloat16


def dot(a, b):
    return jnp.dot(a, b, preferred_element_type=F32)


def fold(x):
    total = None
    for i in range(0, x.shape[0], 8):
        for j in range(0, x.shape[1], 128):
            piece = x[i : i + 8, j : j + 128]
            total = piece if total is None else total + piece
    return total


def lateral(x):
    rows, lanes = x.shape
    q = lax.broadcasted_iota(jnp.int32, x.shape, 0)
    s = lax.broadcasted_iota(jnp.int32, x.shape, 1)
    a, b = q % NSIDE, (q // NSIDE) % NSIDE
    col, row = s % EXY, (s // EXY) % EXY
    last = NSIDE - 1

    def along(which, node_step, place, lane_step):
        back = (EXY - 1) * lane_step
        low = which == 0
        z = jnp.where(low, pltpu.roll(x, rows - last * node_step, 0), pltpu.roll(x, last * node_step, 0))
        down = jnp.where(place == 0, pltpu.roll(z, lanes - back, 1), pltpu.roll(z, lane_step, 1))
        up = jnp.where(place == EXY - 1, pltpu.roll(z, back, 1), pltpu.roll(z, lanes - lane_step, 1))
        return jnp.where(low, down, jnp.where(which == last, up, 0.0))

    return along(a, 1, col, 1) + along(b, NSIDE, row, EXY)


def face_count(shape):
    q = lax.broadcasted_iota(jnp.int32, shape, 0)
    count = jnp.zeros(shape, F32)
    for step in (1, NSIDE, BLOCK):
        at = (q // step) % NSIDE
        count += jnp.where((at == 0) | (at == NSIDE - 1), 1.0, 0.0)
    return count


def jumps_inside(x):
    nodes, elements = x.shape
    low, high = slice(0, BLOCK), slice(nodes - BLOCK, nodes)
    empty = jnp.zeros((BLOCK, LAYER), F32)
    below = jnp.concatenate([empty, x[high, : elements - LAYER]], axis=1)
    above = jnp.concatenate([x[low, LAYER:], empty], axis=1)
    middle = jnp.zeros((nodes - 2 * BLOCK, elements), F32)
    return lateral(x) + jnp.concatenate([below, middle, above], axis=0) - face_count(x.shape) * x


def kernel(
    n_space, n_tm,
    num_hbm, ctl_hbm, tgt_hbm, st_hbm, adj_hbm, a_hbm,
    newc_ref, nst_ref, nadj_ref, obj_ref,
    a_raw, a_ref, num, ctl_raw, ctl, tgt_raw, goal, adj_raw, adj, st, hist, r_ref, edge, gf, pulled, pa, pt,
    cost, rim_out, rim_in, msg_out, msg_in, near_out, near_in, rim, prev, far_g, held, st_out, st_in, adj_out, adj_in, rate_out, rate_in, face_out, face_in, slot_s, slot_t,
    in_sem, a_sem, rim_send, rim_recv, msg_send, msg_recv, near_send, near_recv, st_sem, adj_sem,
    ss_send, ss_recv, tt_send, tt_recv, ready,
):
    steps, nodes, elements = ctl.shape
    me = lax.axis_index("space")
    t = lax.axis_index("tm")
    first = t * steps
    total_steps = steps * n_tm
    turn, final = 1, 2
    last_block = nodes - BLOCK
    blocks = [slice(s, s + BLOCK) for s in range(0, nodes, BLOCK)]
    edge_rows = (slice(0, BLOCK), slice(last_block, nodes))
    edge_lanes = (slice(0, LAYER), slice(elements - LAYER, elements))

    def weight(k):
        return (first + k).astype(F32) / total_steps

    loads = [
        pltpu.make_async_copy(src, dst, in_sem.at[i])
        for i, (src, dst) in enumerate(
            ((num_hbm, num), (st_hbm.at[0], st), (tgt_hbm, tgt_raw), (ctl_hbm, ctl_raw), (adj_hbm.at[0], adj_raw))
        )
    ]
    for c in loads[:2]:
        c.start()
    for landing in (rim_in, msg_in, near_in):
        landing[...] = jnp.zeros_like(landing)
    barrier = pltpu.get_barrier_semaphore()
    for d in range(1, n_space):
        pl.semaphore_signal(barrier, inc=1, device_id={"space": lax.rem(me + d, n_space)},
                            device_id_type=pl.DeviceIdType.MESH)
    bits = (n_tm - 1).bit_length()

    def beside(far):
        return jnp.where(t >= far, 1, 0) + jnp.where(t + far < n_tm, 1, 0)

    def greet(sem, far):
        @pl.when(t >= far)
        def _():
            pl.semaphore_signal(sem, inc=1, device_id={"tm": t - far}, device_id_type=pl.DeviceIdType.MESH)

        @pl.when(t + far < n_tm)
        def _():
            pl.semaphore_signal(sem, inc=1, device_id={"tm": t + far}, device_id_type=pl.DeviceIdType.MESH)

    greet(barrier, 1)

    def tell(j):
        if j <= bits:
            greet(ready.at[j - 1], 2 ** (j - 1))

    def hear(j):
        if j <= bits:
            pl.semaphore_wait(ready.at[j - 1], beside(2 ** (j - 1)))

    def pass_on(j):
        hear(j)
        tell(j + 1)

    parts = a_sem.shape[0]
    chunk = nodes // parts
    a_loads = [
        pltpu.make_async_copy(a_hbm.at[pl.ds(i * chunk, chunk)], a_raw.at[pl.ds(i * chunk, chunk)], a_sem.at[i])
        for i in range(parts)
    ]
    outer = [0, parts - 1]
    inner = list(range(1, parts - 1))
    for i in outer + inner:
        a_loads[i].start()
    for c in loads[2:]:
        c.start()
    cost[...] = jnp.zeros_like(cost)

    loads[0].wait()
    own = num[...]
    for i in range(0, elements, LAYER):
        place = lax.broadcasted_iota(jnp.int32, (LAYER, elements), 0) + i
        pt[i : i + LAYER, :] = jnp.where(own == place, 1.0, 0.0).astype(BF16)
    down = jnp.broadcast_to(own.astype(F32), (128, elements)).T
    for i in range(0, elements, 128):
        place = lax.broadcasted_iota(jnp.int32, (elements, 128), 1) + i
        pa[:, i : i + 128] = jnp.where(down == place.astype(F32), 1.0, 0.0).astype(BF16)

    def split(x):
        high = x.astype(BF16)
        return jnp.concatenate([high, (x - high.astype(F32)).astype(BF16)], axis=0)

    def joined(x):
        return x[:nodes] + x[nodes:]

    def across(src, dst, send, recv, side, back=0):
        return pltpu.make_async_remote_copy(
            src_ref=src, dst_ref=dst, send_sem=send, recv_sem=recv,
            device_id={"tm": t - back, "space": me - 1 if side == 0 else me + 1},
            device_id_type=pl.DeviceIdType.MESH,
        )

    def rim_copy(rnd, side, slot):
        return across(rim_out.at[rnd, side], rim_in.at[rnd, slot], rim_send.at[rnd, side], rim_recv.at[rnd, slot],
                      side, 1 if rnd == final else 0)

    def msg_copy(rnd, side, slot):
        return across(msg_out.at[rnd, side], msg_in.at[rnd, slot], msg_send.at[rnd, side], msg_recv.at[rnd, slot], side)

    def near_copy(side, slot):
        return across(near_out.at[side], near_in.at[slot], near_send.at[side], near_recv.at[slot], side)

    def at_side(side):
        return me > 0 if side == 0 else me < n_space - 1

    def start_both(copy):
        for side in (0, 1):
            @pl.when(at_side(side))
            def _():
                copy(side, 1 - side).start()

    def wait_both(copy):
        for side in (0, 1):
            @pl.when(at_side(side))
            def _():
                copy(side, side).wait()

    def send_msg(rnd, base, ahead):
        for side in (0, 1):
            msg_out[rnd, side, 0] = base(side).astype(BF16)
            msg_out[rnd, side, 1] = ahead(side).astype(BF16)
        start_both(functools.partial(msg_copy, rnd))

    def wait_final_rims():
        for side in (0, 1):
            @pl.when(at_side(side) & (t < n_tm - 1))
            def _():
                rim_copy(final, side, side).wait_recv()

            @pl.when(at_side(side) & (t > 0))
            def _():
                rim_copy(final, side, side).wait_send()

    depth = BLOCK * BLOCK
    place_k = lax.broadcasted_iota(jnp.int32, (BLOCK, depth), 1)
    place_r = lax.broadcasted_iota(jnp.int32, (BLOCK, depth), 0)
    sum_rows = jnp.where(place_k // BLOCK == place_r, 1.0, 0.0).astype(BF16)
    sum_groups = jnp.where(place_k % BLOCK == place_r, 1.0, 0.0).astype(BF16)
    sum_rows2 = jnp.concatenate([sum_rows, sum_rows], axis=1)

    def groups(n):
        place_c = lax.broadcasted_iota(jnp.int32, (BLOCK, n), 1) % BLOCK
        return jnp.where(place_c == lax.broadcasted_iota(jnp.int32, (BLOCK, n), 0), 1.0, 0.0).astype(BF16)

    def product(out, into, lanes, right):
        return (a_ref[out, into, lanes] * right[None]).reshape(depth, LAYER)

    def product_pair(out, into, lanes, right):
        (i0, i1), (r0, r1) = into, right
        return (a_ref[out, i0, lanes] * r0[None] + a_ref[out, i1, lanes] * r1[None]).reshape(depth, LAYER)

    def inner_blocks(side):
        return [b for b in blocks if b != edge_rows[side]]

    def apply_inner(side, outs, write):
        lanes = edge_lanes[side]
        b0, b1, b2 = inner_blocks(side)
        if side == 0:
            pair, single = (b0, b1), b2
        else:
            pair, single = (b1, b2), b0
        rp = (r_ref[pair[0], lanes], r_ref[pair[1], lanes])
        rs = r_ref[single, lanes]
        for out in outs:
            q = jnp.concatenate([product_pair(out, pair, lanes, rp), product(out, single, lanes, rs)], axis=0)
            write(out, lanes, dot(sum_rows2, q))

    def transposed(out, into, lanes):
        rows = [i for b in into for i in range(b.start, b.stop)]

        def term(i):
            row = jnp.broadcast_to(gf[i : i + 1, lanes], (BLOCK, LAYER)).astype(BF16)
            return a_ref[i, out, lanes] * row

        pieces = [term(rows[i]) + term(rows[i + 1]) for i in range(0, len(rows), 2)]
        return dot(groups(BLOCK * len(pieces)), jnp.concatenate(pieces, axis=0))

    def near_transposed(side):
        def term(i):
            row = jnp.broadcast_to(far_g[side, i : i + 1], (BLOCK, LAYER)).astype(BF16)
            return near_in[side, i] * row

        pieces = [term(i) + term(i + 1) for i in range(0, BLOCK, 2)]
        return dot(groups(BLOCK * len(pieces)), jnp.concatenate(pieces, axis=0))

    loads[1].wait()
    hist[0] = joined(dot(split(st[...]), pa[...]))
    for side in (0, 1):
        rim_out[0, side] = hist[0, edge_rows[side], edge_lanes[side]].astype(BF16)
    pl.semaphore_wait(barrier, n_space - 1 + beside(1))
    start_both(functools.partial(rim_copy, 0))
    tell(1)

    for c in loads[2:]:
        c.wait()
    goal[...] = dot(tgt_raw[...], pa[...])
    adj[...] = joined(dot(split(adj_raw[...]), pa[...]))
    for k in range(steps):
        ctl[k] = dot(ctl_raw[k], pa[...]).astype(BF16)
    piece = depth // nodes

    def permute(part):
        a_loads[part].wait()
        for i in range(part * chunk, (part + 1) * chunk, piece):
            rows = a_raw[i : i + piece].reshape(depth, elements)
            a_ref[i : i + piece] = dot(rows, pa[...]).astype(BF16).reshape(piece, nodes, elements)

    def prepare(k):
        u = hist[k]
        c = ctl[k].astype(F32)
        base = u + TIME_STEP * (u - u * u * u) + TIME_STEP * PENALTY * jumps_inside(u) + TIME_STEP * c
        r_ref[...] = base.astype(BF16)
        for side in (0, 1):
            edge[side] = base[edge_rows[side], edge_lanes[side]]

    def keep(k):
        def write(rows, lanes, v):
            hist[k + 1, rows, lanes] = v

        return write

    def count_cost(k):
        c = ctl[k].astype(F32)
        w = jnp.where(k > 0, weight(k), 0.0)
        d = hist[k] - goal[...]
        cost[...] += 0.5 * w * fold(d * d) + 0.5 * REGULAR * fold(c * c)

    def right_edges():
        return [(edge[side] + TIME_STEP * PENALTY * rim[side]).astype(BF16) for side in (0, 1)]

    def step_edges(k, right):
        for side, (rows, lanes) in enumerate(zip(edge_rows, edge_lanes)):
            hist[k + 1, rows, lanes] += dot(sum_rows, product(rows, rows, lanes, right[side]))

    def send_ahead(k):
        send_msg(k, lambda side: edge[side], lambda side: hist[k + 1, edge_rows[side], edge_lanes[side]])

    def far_rims(k):
        for side, (rows, lanes) in enumerate(zip(edge_rows, edge_lanes)):
            far = msg_in[k, side, 0].astype(F32) + TIME_STEP * PENALTY * hist[k, rows, lanes]
            q = (near_in[side] * far.astype(BF16)[None]).reshape(depth, LAYER)
            rim[side] = msg_in[k, side, 1].astype(F32) + dot(sum_rows, q)

    def step_rest(k, right):
        for side, (rows, lanes) in enumerate(zip(edge_rows, edge_lanes)):
            for out in inner_blocks(side):
                hist[k + 1, out, lanes] += dot(sum_rows, product(out, rows, lanes, right[side]))

    prepare(0)
    for part in outer:
        permute(part)
    for side in (0, 1):
        apply_inner(side, [edge_rows[side]], keep(0))
    if steps > 1:
        send_ahead(0)
    for side, (rows, lanes) in enumerate(zip(edge_rows, edge_lanes)):
        near_out[side] = a_ref[rows, rows, lanes]
    start_both(near_copy)
    for part in inner:
        permute(part)
    for side in (0, 1):
        apply_inner(side, inner_blocks(side), keep(0))
    wait_both(functools.partial(rim_copy, 0))
    for side in (0, 1):
        rim[side] = rim_in[0, side].astype(F32)
    first_right = right_edges()
    step_edges(0, first_right)
    step_rest(0, first_right)
    count_cost(0)
    pass_on(1)

    def forward(k, carry):
        prepare(k)
        for side in (0, 1):
            apply_inner(side, [edge_rows[side]], keep(k))
        pl.when(k < steps - 1)(functools.partial(send_ahead, k))
        for side in (0, 1):
            apply_inner(side, inner_blocks(side), keep(k))
        count_cost(k)
        pl.when(k == 1)(functools.partial(wait_both, near_copy))
        wait_both(functools.partial(msg_copy, k - 1))
        far_rims(k - 1)
        right = right_edges()
        step_edges(k, right)
        step_rest(k, right)
        for j in range(2, min(bits, steps)):
            pl.when(k == j - 1)(functools.partial(pass_on, j))
        return carry

    lax.fori_loop(1, steps, forward, 0)
    for j in range(max(2, min(bits, steps)), bits + 1):
        pass_on(j)

    w_end = weight(steps)
    u = hist[steps]
    d = u - goal[...]
    cost[...] += 0.5 * w_end * fold(d * d)
    gf[...] = w_end * d + adj[...]

    for side, (rows, lanes) in enumerate(zip(edge_rows, edge_lanes)):
        v = transposed(rows, blocks, lanes)
        pulled[rows, lanes] = v
        rim_out[turn, side] = v.astype(BF16)
    start_both(functools.partial(rim_copy, turn))

    st_out[...] = hist[steps].astype(BF16)

    def st_copy(dst):
        return pltpu.make_async_remote_copy(
            src_ref=st_out, dst_ref=st_in, send_sem=st_sem.at[0], recv_sem=st_sem.at[1],
            device_id={"tm": dst}, device_id_type=pl.DeviceIdType.MESH)

    def back_copy(i, dst):
        src, land = ((rate_out, rate_in), (adj_out, adj_in), (face_out, face_in))[i]
        return pltpu.make_async_remote_copy(
            src_ref=src, dst_ref=land, send_sem=adj_sem.at[0, i], recv_sem=adj_sem.at[1, i],
            device_id={"tm": dst}, device_id_type=pl.DeviceIdType.MESH)

    def send_back(i):
        @pl.when(t > 0)
        def _():
            back_copy(i, t - 1).start()

    slot_s[me] = cost[...]

    def gather_copy(slots, send, recv, axis, index, count, d):
        return pltpu.make_async_remote_copy(
            src_ref=slots.at[index], dst_ref=slots.at[index], send_sem=send.at[d], recv_sem=recv.at[index],
            device_id={axis: lax.rem(index + d, count)}, device_id_type=pl.DeviceIdType.MESH)

    def gather_wait(slots, send, recv, axis, index, count, d):
        gather_copy(slots, send, recv, axis, index, count, d).wait_send()
        origin = lax.rem(index + d, count)
        pltpu.make_async_remote_copy(
            src_ref=slots.at[origin], dst_ref=slots.at[origin], send_sem=send.at[d], recv_sem=recv.at[origin],
            device_id={axis: origin}, device_id_type=pl.DeviceIdType.MESH).wait_recv()

    over_s = (slot_s, ss_send, ss_recv, "space", me, n_space)

    over_t = (slot_t, tt_send, tt_recv, "tm", t, n_tm)

    def gathered(slots, *rest):
        count = rest[-1]
        for d in range(1, count):
            gather_wait(slots, *rest, d)
        total = slots[0]
        for i in range(1, count):
            total = total + slots[i]
        return total

    def hand_round():
        slot_t[t] = gathered(*over_s)
        for d in range(1, n_tm):
            gather_copy(*over_t, d).start()

    def rate(k):
        before = hist[k]
        return 1.0 + TIME_STEP * (1.0 - 3.0 * before * before)

    for d in range(1, n_space):
        gather_copy(*over_s, d).start()

    @pl.when(t < n_tm - 1)
    def _():
        st_copy(t + 1).start()

    rate_out[...] = rate(0).astype(BF16)
    send_back(0)

    for side, lanes in enumerate(edge_lanes):
        for out in inner_blocks(side):
            pulled[out, lanes] = transposed(out, blocks, lanes)

    def carry_back(factor, p):
        return factor * p + TIME_STEP * PENALTY * jumps_inside(p)

    def update(k, p):
        control = ctl[k].astype(F32)
        fresh = (control - (TIME_STEP * p + REGULAR * control)).astype(BF16)
        newc_ref[k] = dot(fresh, pt[...]).astype(BF16)

    def backward(i, carry):
        k = steps - 1 - i
        rnd = steps - 1 + i
        p = pulled[...]
        gf[...] = weight(k) * (hist[k] - goal[...]) + carry_back(rate(k), p)
        held[...] = p
        for side, (rows, lanes) in enumerate(zip(edge_rows, edge_lanes)):
            pulled[rows, lanes] = transposed(rows, inner_blocks(side), lanes)

        @pl.when(i < steps - 2)
        def _():
            send_msg(rnd, lambda side: gf[edge_rows[side], edge_lanes[side]],
                     lambda side: pulled[edge_rows[side], edge_lanes[side]])

        for side, lanes in enumerate(edge_lanes):
            for out in inner_blocks(side):
                pulled[out, lanes] = transposed(out, inner_blocks(side), lanes)

        @pl.when(i == steps - 2)
        def _():
            adj_out[...] = carry_back(rate(0), pulled[...]).astype(BF16)
            send_back(1)

        @pl.when(i == 0)
        def _():
            wait_both(functools.partial(rim_copy, turn))
            for side in (0, 1):
                rim[side] = rim_in[turn, side].astype(F32)

        @pl.when(i > 0)
        def _():
            wait_both(functools.partial(msg_copy, rnd - 1))
            for side in (0, 1):
                far_g[side] = msg_in[rnd - 1, side, 0].astype(F32) + TIME_STEP * PENALTY * prev[side]
            for side in (0, 1):
                rim[side] = msg_in[rnd - 1, side, 1].astype(F32) + near_transposed(side)

        for side, (rows, lanes) in enumerate(zip(edge_rows, edge_lanes)):
            g = gf[rows, lanes] + TIME_STEP * PENALTY * rim[side]
            gf[rows, lanes] = g
            face_out[side] = g.astype(BF16)

        @pl.when(i == steps - 2)
        def _():
            send_back(2)

        for side, (rows, lanes) in enumerate(zip(edge_rows, edge_lanes)):
            pulled[rows, lanes] += transposed(rows, [rows], lanes)

        @pl.when(i == steps - 2)
        def _():
            for side, (rows, lanes) in enumerate(zip(edge_rows, edge_lanes)):
                rim_out[final, side] = pulled[rows, lanes].astype(BF16)

                @pl.when(at_side(side) & (t > 0))
                def _():
                    rim_copy(final, side, 1 - side).start()

        for side, (rows, lanes) in enumerate(zip(edge_rows, edge_lanes)):
            for out in inner_blocks(side):
                pulled[out, lanes] += transposed(out, [rows], lanes)
        for side, (rows, lanes) in enumerate(zip(edge_rows, edge_lanes)):
            prev[side] = held[rows, lanes]
        update(k, held[...])
        pl.when(i == 0)(hand_round)
        return carry

    lax.fori_loop(0, steps - 1, backward, 0)

    update(0, pulled[...])

    @pl.when(t == 0)
    def _():
        nst_ref[0] = st[...]

    @pl.when(t > 0)
    def _():
        st_copy(t - 1).wait_recv()
        nst_ref[0] = dot(st_in[...], pt[...])

    @pl.when(t < n_tm - 1)
    def _():
        st_copy(t + 1).wait_send()

    total = gathered(*over_t)
    scaled = total * (1.0 / (total_steps * nodes * elements * n_space))
    obj_ref[...] = jnp.sum(jnp.sum(scaled, axis=0, keepdims=True), axis=1, keepdims=True)

    @pl.when(t == n_tm - 1)
    def _():
        nadj_ref[...] = jnp.zeros_like(nadj_ref)

    @pl.when(t < n_tm - 1)
    def _():
        for i in (0, 2):
            back_copy(i, t + 1).wait_recv()
        for side, (rows, lanes) in enumerate(zip(edge_rows, edge_lanes)):
            gf[rows, lanes] = face_in[side].astype(F32)
        for side, (rows, lanes) in enumerate(zip(edge_rows, edge_lanes)):
            for out in blocks:
                pulled[out, lanes] = transposed(out, [rows], lanes)
        gf[...] = carry_back(rate_in[...].astype(F32), pulled[...])
        back_copy(1, t + 1).wait_recv()

    wait_final_rims()

    @pl.when(t < n_tm - 1)
    def _():
        for side, (rows, lanes) in enumerate(zip(edge_rows, edge_lanes)):
            gf[rows, lanes] += TIME_STEP * PENALTY * rim_in[final, side].astype(F32)
        nadj_ref[0] = joined(dot(split(gf[...] + adj_in[...].astype(F32)), pt[...]))

    @pl.when(t > 0)
    def _():
        for i in range(3):
            back_copy(i, t - 1).wait_send()


def store_kernel(count, *refs):
    gives = [pltpu.make_async_copy(refs[i], refs[count + i], refs[-1].at[i]) for i in range(count)]
    for c in gives:
        c.start()
    for c in gives:
        c.wait()


def store(values):
    count = len(values)
    return pl.pallas_call(
        functools.partial(store_kernel, count),
        out_shape=tuple(jax.ShapeDtypeStruct(v.shape, v.dtype) for v in values),
        in_specs=[pl.BlockSpec(memory_space=pltpu.VMEM)] * count,
        out_specs=(pl.BlockSpec(memory_space=pltpu.HBM),) * count,
        scratch_shapes=[pltpu.SemaphoreType.DMA((count,))],
        compiler_params=pltpu.CompilerParams(vmem_limit_bytes=4194304),
    )(*values)


def solution(mesh):
    n_space, n_tm = mesh.shape["space"], mesh.shape["tm"]

    def per_device(controls, target, state_in, adjoint_in, block_inverse, numbering):
        steps, nodes, elements = controls.shape
        vm = pl.BlockSpec(memory_space=pltpu.VMEM)
        hbm = pl.BlockSpec(memory_space=pltpu.HBM)
        field = (nodes, elements)
        messages = max(2 * steps - 3, 1)
        bits = (n_tm - 1).bit_length()
        dma = pltpu.SemaphoreType.DMA
        new_controls, next_state, next_adjoint, objective = pl.pallas_call(
            functools.partial(kernel, n_space, n_tm),
            out_shape=(
                pltpu.VMEM(controls.shape, BF16),
                pltpu.VMEM(state_in.shape, F32),
                pltpu.VMEM(adjoint_in.shape, F32),
                pltpu.VMEM((1, 1), F32),
            ),
            in_specs=[hbm] * 6,
            out_specs=(vm, vm, vm, vm),
            scratch_shapes=[
                pltpu.VMEM(block_inverse.shape, BF16),
                pltpu.VMEM(block_inverse.shape, BF16),
                pltpu.VMEM(numbering.shape, jnp.int32),
                pltpu.VMEM(controls.shape, BF16),
                pltpu.VMEM(controls.shape, BF16),
                pltpu.VMEM(field, BF16),
                pltpu.VMEM(field, F32),
                pltpu.VMEM(field, F32),
                pltpu.VMEM(field, F32),
                pltpu.VMEM(field, F32),
                pltpu.VMEM((steps + 1,) + field, F32),
                pltpu.VMEM(field, BF16),
                pltpu.VMEM((2, BLOCK, LAYER), F32),
                pltpu.VMEM(field, F32),
                pltpu.VMEM(field, F32),
                pltpu.VMEM((elements, elements), BF16),
                pltpu.VMEM((elements, elements), BF16),
                pltpu.VMEM((8, 128), F32),
                pltpu.VMEM((3, 2, BLOCK, LAYER), BF16),
                pltpu.VMEM((3, 2, BLOCK, LAYER), BF16),
                pltpu.VMEM((messages, 2, 2, BLOCK, LAYER), BF16),
                pltpu.VMEM((messages, 2, 2, BLOCK, LAYER), BF16),
                pltpu.VMEM((2, BLOCK, BLOCK, LAYER), BF16),
                pltpu.VMEM((2, BLOCK, BLOCK, LAYER), BF16),
                pltpu.VMEM((2, BLOCK, LAYER), F32),
                pltpu.VMEM((2, BLOCK, LAYER), F32),
                pltpu.VMEM((2, BLOCK, LAYER), F32),
                pltpu.VMEM(field, F32),
                pltpu.VMEM(field, BF16),
                pltpu.VMEM(field, BF16),
                pltpu.VMEM(field, BF16),
                pltpu.VMEM(field, BF16),
                pltpu.VMEM(field, BF16),
                pltpu.VMEM(field, BF16),
                pltpu.VMEM((2, BLOCK, LAYER), BF16),
                pltpu.VMEM((2, BLOCK, LAYER), BF16),
                pltpu.VMEM((n_space, 8, 128), F32),
                pltpu.VMEM((n_tm, 8, 128), F32),
                dma((5,)),
                dma((4,)),
                dma((3, 2)),
                dma((3, 2)),
                dma((messages, 2)),
                dma((messages, 2)),
                dma((2,)),
                dma((2,)),
                dma((2,)),
                dma((2, 3)),
                dma((n_space,)),
                dma((n_space,)),
                dma((n_tm,)),
                dma((n_tm,)),
                pltpu.SemaphoreType.REGULAR((bits,)),
            ],
            compiler_params=pltpu.CompilerParams(
                collective_id=0, has_side_effects=True, vmem_limit_bytes=60000000
            ),
        )(numbering, controls, target, state_in, adjoint_in, block_inverse)
        out = store((new_controls, next_state, next_adjoint, objective))
        return out[:3] + (out[3].reshape(()),)

    return jax.shard_map(
        per_device,
        mesh=mesh,
        in_specs=(
            P("tm", None, "space"),
            P(None, "space"),
            P("tm", None, "space"),
            P("tm", None, "space"),
            P(None, None, "space"),
            P("space", None),
        ),
        out_specs=(P("tm", None, "space"), P("tm", None, "space"), P("tm", None, "space"), P()),
        check_vma=False,
    )
```

```python
import functools

import jax
import jax.numpy as jnp
from jax import lax
from jax.experimental import pallas as pl
from jax.experimental.pallas import tpu as pltpu
from jax.sharding import PartitionSpec as P

NSIDE = 4
EXY = 16
BLOCK = NSIDE * NSIDE
LAYER = EXY * EXY
TIME_STEP = 0.1
PENALTY = 0.5
REGULAR = 0.1
F32 = jnp.float32
BF16 = jnp.bfloat16


def dot(a, b):
    return jnp.dot(a, b, preferred_element_type=F32)


def fold(x):
    total = None
    for i in range(0, x.shape[0], 8):
        for j in range(0, x.shape[1], 128):
            piece = x[i : i + 8, j : j + 128]
            total = piece if total is None else total + piece
    return total


def lateral(x):
    nodes, elements = x.shape
    last = NSIDE - 1

    def by_layer(y, shift):
        return jnp.concatenate(
            [pltpu.roll(y[:, i : i + LAYER], shift, 1) for i in range(0, elements, LAYER)], axis=1
        )

    a = lax.broadcasted_iota(jnp.int32, x.shape, 0) % NSIDE
    y = jnp.where(a == last, by_layer(x, EXY), by_layer(x, LAYER - EXY)).reshape(nodes // 8, 8, elements)
    to_low = pltpu.roll(y, 8 - last, 1).reshape(nodes, elements)
    to_high = pltpu.roll(y, last, 1).reshape(nodes, elements)
    along_a = jnp.where(a == 0, to_low, jnp.where(a == last, to_high, 0.0))

    count = nodes // BLOCK
    tall = x.reshape(count, 2, 8, elements)
    low3 = lax.broadcasted_iota(jnp.int32, (count, 8, elements), 1) < NSIDE
    w = jnp.where(low3, tall[:, 0], tall[:, 1]).reshape(count * 8, elements)
    low2 = lax.broadcasted_iota(jnp.int32, w.shape, 0) % 8 < NSIDE
    row = lax.broadcasted_iota(jnp.int32, w.shape, 1) % EXY
    down = jnp.where(row == 0, pltpu.roll(w, elements - EXY + 1, 1), pltpu.roll(w, 1, 1))
    up = jnp.where(row == EXY - 1, pltpu.roll(w, EXY - 1, 1), pltpu.roll(w, elements - 1, 1))
    r = pltpu.roll(jnp.where(low2, up, down).reshape(count, 8, elements), NSIDE, 1)
    first, second = jnp.where(low3, r, 0.0), jnp.where(low3, 0.0, r)
    along_b = jnp.concatenate([v for i in range(count) for v in (first[i], second[i])], axis=0)
    return along_a + along_b


def face_count(shape):
    q = lax.broadcasted_iota(jnp.int32, shape, 0)
    count = jnp.zeros(shape, F32)
    for step in (1, NSIDE, BLOCK):
        at = (q // step) % NSIDE
        count += jnp.where((at == 0) | (at == NSIDE - 1), 1.0, 0.0)
    return count


def jumps_inside(x):
    nodes, elements = x.shape
    low, high = slice(0, BLOCK), slice(nodes - BLOCK, nodes)
    empty = jnp.zeros((BLOCK, LAYER), F32)
    below = jnp.concatenate([empty, x[high, : elements - LAYER]], axis=1)
    above = jnp.concatenate([x[low, LAYER:], empty], axis=1)
    middle = jnp.zeros((nodes - 2 * BLOCK, elements), F32)
    return lateral(x) + jnp.concatenate([below, middle, above], axis=0) - face_count(x.shape) * x


def kernel(
    n_space, n_tm,
    num_hbm, ctl_hbm, tgt_hbm, st_hbm, adj_hbm, a_hbm,
    newc_ref, nst_ref, nadj_ref, obj_ref,
    a_raw, a_ref, num, ctl_raw, ctl, tgt_raw, goal, adj_raw, adj, st, hist, r_ref, edge, gf, pulled, pa, pt,
    rim_out, rim_in, msg_out, msg_in, near_out, near_in, rim, prev, far_g, held, st_out, st_in, adj_out, adj_in, rate_out, rate_in, face_out, face_in, slot_s, slot_t,
    in_sem, a_sem, rim_send, rim_recv, msg_send, msg_recv, near_send, near_recv, st_sem, adj_sem,
    ss_send, ss_recv, tt_send, tt_recv, ready,
):
    steps, nodes, elements = ctl.shape
    me = lax.axis_index("space")
    t = lax.axis_index("tm")
    first = t * steps
    total_steps = steps * n_tm
    turn, final = 1, 2
    last_block = nodes - BLOCK
    blocks = [slice(s, s + BLOCK) for s in range(0, nodes, BLOCK)]
    edge_rows = (slice(0, BLOCK), slice(last_block, nodes))
    edge_lanes = (slice(0, LAYER), slice(elements - LAYER, elements))

    def weight(k):
        return lax.convert_element_type(first + k, F32) / total_steps

    loads = [
        pltpu.make_async_copy(src, dst, in_sem.at[i])
        for i, (src, dst) in enumerate(
            ((num_hbm, num), (st_hbm.at[0], st), (tgt_hbm, tgt_raw), (ctl_hbm, ctl_raw), (adj_hbm.at[0], adj_raw))
        )
    ]
    for c in loads[:2]:
        c.start()
    for landing in (rim_in, msg_in, near_in):
        landing[...] = jnp.zeros_like(landing)
    barrier = pltpu.get_barrier_semaphore()
    for d in range(1, n_space):
        pl.semaphore_signal(barrier, inc=1, device_id={"space": lax.rem(me + d, n_space)},
                            device_id_type=pl.DeviceIdType.MESH)
    bits = (n_tm - 1).bit_length()

    def beside(far):
        return jnp.where(t >= far, 1, 0) + jnp.where(t + far < n_tm, 1, 0)

    def greet(sem, far):
        @pl.when(t >= far)
        def _():
            pl.semaphore_signal(sem, inc=1, device_id={"tm": t - far}, device_id_type=pl.DeviceIdType.MESH)

        @pl.when(t + far < n_tm)
        def _():
            pl.semaphore_signal(sem, inc=1, device_id={"tm": t + far}, device_id_type=pl.DeviceIdType.MESH)

    greet(barrier, 1)

    def tell(j):
        if j <= bits:
            greet(ready.at[j - 1], 2 ** (j - 1))

    def hear(j):
        if j <= bits:
            pl.semaphore_wait(ready.at[j - 1], beside(2 ** (j - 1)))

    def pass_on(j):
        hear(j)
        tell(j + 1)

    parts = a_sem.shape[0]
    chunk = nodes // parts
    a_loads = [
        pltpu.make_async_copy(a_hbm.at[pl.ds(i * chunk, chunk)], a_raw.at[pl.ds(i * chunk, chunk)], a_sem.at[i])
        for i in range(parts)
    ]
    outer = [0, parts - 1]
    inner = list(range(1, parts - 1))
    for i in outer + inner:
        a_loads[i].start()
    for c in loads[2:]:
        c.start()

    loads[0].wait()
    stored = num[...]
    own = stored // LAYER * LAYER + stored % EXY * EXY + stored // EXY % EXY
    for i in range(0, elements, LAYER):
        place = lax.broadcasted_iota(jnp.int32, (LAYER, elements), 0) + i
        pt[i : i + LAYER, :] = jnp.where(own == place, 1.0, 0.0).astype(BF16)
    down = jnp.broadcast_to(own.astype(F32), (128, elements)).T
    for i in range(0, elements, 128):
        place = lax.broadcasted_iota(jnp.int32, (elements, 128), 1) + i
        pa[:, i : i + 128] = jnp.where(down == place.astype(F32), 1.0, 0.0).astype(BF16)

    def split(x):
        high = x.astype(BF16)
        return jnp.concatenate([high, (x - high.astype(F32)).astype(BF16)], axis=0)

    def joined(x):
        return x[:nodes] + x[nodes:]

    def across(src, dst, send, recv, side, back=0):
        return pltpu.make_async_remote_copy(
            src_ref=src, dst_ref=dst, send_sem=send, recv_sem=recv,
            device_id={"tm": t - back, "space": me - 1 if side == 0 else me + 1},
            device_id_type=pl.DeviceIdType.MESH,
        )

    def rim_copy(rnd, side, slot):
        return across(rim_out.at[rnd, side], rim_in.at[rnd, slot], rim_send.at[rnd, side], rim_recv.at[rnd, slot],
                      side, 1 if rnd == final else 0)

    def msg_copy(rnd, side, slot):
        return across(msg_out.at[rnd, side], msg_in.at[rnd, slot], msg_send.at[rnd, side], msg_recv.at[rnd, slot], side)

    def near_copy(side, slot):
        return across(near_out.at[side], near_in.at[slot], near_send.at[side], near_recv.at[slot], side)

    def at_side(side):
        return me > 0 if side == 0 else me < n_space - 1

    def start_both(copy):
        for side in (0, 1):
            @pl.when(at_side(side))
            def _():
                copy(side, 1 - side).start()

    def wait_both(copy):
        for side in (0, 1):
            @pl.when(at_side(side))
            def _():
                copy(side, side).wait()

    def send_msg(rnd, base, ahead):
        for side in (0, 1):
            msg_out[rnd, side, 0] = base(side).astype(BF16)
            msg_out[rnd, side, 1] = ahead(side).astype(BF16)
        start_both(functools.partial(msg_copy, rnd))

    def wait_final_rims():
        for side in (0, 1):
            @pl.when(at_side(side) & (t < n_tm - 1))
            def _():
                rim_copy(final, side, side).wait_recv()

            @pl.when(at_side(side) & (t > 0))
            def _():
                rim_copy(final, side, side).wait_send()

    depth = BLOCK * BLOCK
    place_k = lax.broadcasted_iota(jnp.int32, (BLOCK, depth), 1)
    place_r = lax.broadcasted_iota(jnp.int32, (BLOCK, depth), 0)
    sum_rows = jnp.where(place_k // BLOCK == place_r, 1.0, 0.0).astype(BF16)
    sum_groups = jnp.where(place_k % BLOCK == place_r, 1.0, 0.0).astype(BF16)
    sum_rows2 = jnp.concatenate([sum_rows, sum_rows], axis=1)

    def groups(n):
        place_c = lax.broadcasted_iota(jnp.int32, (BLOCK, n), 1) % BLOCK
        return jnp.where(place_c == lax.broadcasted_iota(jnp.int32, (BLOCK, n), 0), 1.0, 0.0).astype(BF16)

    def product(out, into, lanes, right):
        return (a_ref[out, into, lanes] * right[None]).reshape(depth, LAYER)

    def product_pair(out, into, lanes, right):
        (i0, i1), (r0, r1) = into, right
        return (a_ref[out, i0, lanes] * r0[None] + a_ref[out, i1, lanes] * r1[None]).reshape(depth, LAYER)

    def inner_blocks(side):
        return [b for b in blocks if b != edge_rows[side]]

    def apply_inner(side, outs, write):
        lanes = edge_lanes[side]
        b0, b1, b2 = inner_blocks(side)
        if side == 0:
            pair, single = (b0, b1), b2
        else:
            pair, single = (b1, b2), b0
        rp = (r_ref[pair[0], lanes], r_ref[pair[1], lanes])
        rs = r_ref[single, lanes]
        for out in outs:
            q = jnp.concatenate([product_pair(out, pair, lanes, rp), product(out, single, lanes, rs)], axis=0)
            write(out, lanes, dot(sum_rows2, q))

    def transposed(out, into, lanes):
        rows = [i for b in into for i in range(b.start, b.stop)]

        def term(i):
            row = jnp.broadcast_to(gf[i : i + 1, lanes], (BLOCK, LAYER)).astype(BF16)
            return a_ref[i, out, lanes] * row

        pieces = [term(rows[i]) + term(rows[i + 1]) for i in range(0, len(rows), 2)]
        return dot(groups(BLOCK * len(pieces)), jnp.concatenate(pieces, axis=0))

    def near_transposed(side):
        def term(i):
            row = jnp.broadcast_to(far_g[side, i : i + 1], (BLOCK, LAYER)).astype(BF16)
            return near_in[side, i] * row

        pieces = [term(i) + term(i + 1) for i in range(0, BLOCK, 2)]
        return dot(groups(BLOCK * len(pieces)), jnp.concatenate(pieces, axis=0))

    loads[1].wait()
    hist[0] = joined(dot(split(st[...]), pa[...]))
    for side in (0, 1):
        rim_out[0, side] = hist[0, edge_rows[side], edge_lanes[side]].astype(BF16)
    pl.semaphore_wait(barrier, n_space - 1 + beside(1))
    start_both(functools.partial(rim_copy, 0))
    tell(1)
    for part in outer:
        a_loads[part].wait()
    for side, (rows, lanes) in enumerate(zip(edge_rows, edge_lanes)):
        corner = dot(a_raw[rows, rows].reshape(depth, elements), pa[:, lanes])
        near_out[side] = corner.astype(BF16).reshape(BLOCK, BLOCK, LAYER)
    start_both(near_copy)

    for c in loads[2:]:
        c.wait()
    goal[...] = dot(tgt_raw[...], pa[...])
    adj[...] = joined(dot(split(adj_raw[...]), pa[...]))
    for k in range(steps):
        ctl[k] = dot(ctl_raw[k], pa[...]).astype(BF16)
    piece = depth // nodes

    def permute(part):
        if part in inner:
            a_loads[part].wait()
        for i in range(part * chunk, (part + 1) * chunk, piece):
            rows = a_raw[i : i + piece].reshape(depth, elements)
            a_ref[i : i + piece] = dot(rows, pa[...]).astype(BF16).reshape(piece, nodes, elements)

    def prepare(k):
        u = hist[k]
        c = ctl[k].astype(F32)
        base = u + TIME_STEP * (u - u * u * u) + TIME_STEP * PENALTY * jumps_inside(u) + TIME_STEP * c
        r_ref[...] = base.astype(BF16)
        for side in (0, 1):
            edge[side] = base[edge_rows[side], edge_lanes[side]]

    def keep(k):
        def write(rows, lanes, v):
            hist[k + 1, rows, lanes] = v

        return write

    def right_edges():
        return [(edge[side] + TIME_STEP * PENALTY * rim[side]).astype(BF16) for side in (0, 1)]

    def step_edges(k, right):
        for side, (rows, lanes) in enumerate(zip(edge_rows, edge_lanes)):
            hist[k + 1, rows, lanes] += dot(sum_rows, product(rows, rows, lanes, right[side]))

    def send_ahead(k):
        send_msg(k, lambda side: edge[side], lambda side: hist[k + 1, edge_rows[side], edge_lanes[side]])

    def far_rims(k):
        for side, (rows, lanes) in enumerate(zip(edge_rows, edge_lanes)):
            far = msg_in[k, side, 0].astype(F32) + TIME_STEP * PENALTY * hist[k, rows, lanes]
            q = (near_in[side] * far.astype(BF16)[None]).reshape(depth, LAYER)
            rim[side] = msg_in[k, side, 1].astype(F32) + dot(sum_rows, q)

    def step_rest(k, right):
        for side, (rows, lanes) in enumerate(zip(edge_rows, edge_lanes)):
            for out in inner_blocks(side):
                hist[k + 1, out, lanes] += dot(sum_rows, product(out, rows, lanes, right[side]))

    prepare(0)
    for part in outer:
        permute(part)
    for side in (0, 1):
        apply_inner(side, [edge_rows[side]], keep(0))
    if steps > 1:
        send_ahead(0)
    for part in inner:
        permute(part)
    for side in (0, 1):
        apply_inner(side, inner_blocks(side), keep(0))
    wait_both(functools.partial(rim_copy, 0))
    for side in (0, 1):
        rim[side] = rim_in[0, side].astype(F32)
    first_right = right_edges()
    step_edges(0, first_right)
    step_rest(0, first_right)
    pass_on(1)

    def forward(k, carry):
        prepare(k)
        for side in (0, 1):
            apply_inner(side, [edge_rows[side]], keep(k))
        pl.when(k < steps - 1)(functools.partial(send_ahead, k))
        for side in (0, 1):
            apply_inner(side, inner_blocks(side), keep(k))
        pl.when(k == 1)(functools.partial(wait_both, near_copy))
        wait_both(functools.partial(msg_copy, k - 1))
        far_rims(k - 1)
        right = right_edges()
        step_edges(k, right)
        step_rest(k, right)
        for j in range(2, min(bits, steps)):
            pl.when(k == j - 1)(functools.partial(pass_on, j))
        return carry

    lax.fori_loop(1, steps, forward, 0)
    for j in range(max(2, min(bits, steps)), bits + 1):
        pass_on(j)

    w_end = weight(steps)
    u = hist[steps]
    gf[...] = w_end * (u - goal[...]) + adj[...]

    for side, (rows, lanes) in enumerate(zip(edge_rows, edge_lanes)):
        v = transposed(rows, blocks, lanes)
        pulled[rows, lanes] = v
        rim_out[turn, side] = v.astype(BF16)
    start_both(functools.partial(rim_copy, turn))

    st_out[...] = hist[steps].astype(BF16)

    def st_copy(dst):
        return pltpu.make_async_remote_copy(
            src_ref=st_out, dst_ref=st_in, send_sem=st_sem.at[0], recv_sem=st_sem.at[1],
            device_id={"tm": dst}, device_id_type=pl.DeviceIdType.MESH)

    def back_copy(i, dst):
        src, land = ((rate_out, rate_in), (adj_out, adj_in), (face_out, face_in))[i]
        return pltpu.make_async_remote_copy(
            src_ref=src, dst_ref=land, send_sem=adj_sem.at[0, i], recv_sem=adj_sem.at[1, i],
            device_id={"tm": dst}, device_id_type=pl.DeviceIdType.MESH)

    def send_back(i):
        @pl.when(t > 0)
        def _():
            back_copy(i, t - 1).start()


    def gather_copy(slots, send, recv, axis, index, count, d):
        return pltpu.make_async_remote_copy(
            src_ref=slots.at[index], dst_ref=slots.at[index], send_sem=send.at[d], recv_sem=recv.at[index],
            device_id={axis: lax.rem(index + d, count)}, device_id_type=pl.DeviceIdType.MESH)

    def gather_wait(slots, send, recv, axis, index, count, d):
        gather_copy(slots, send, recv, axis, index, count, d).wait_send()
        origin = lax.rem(index + d, count)
        pltpu.make_async_remote_copy(
            src_ref=slots.at[origin], dst_ref=slots.at[origin], send_sem=send.at[d], recv_sem=recv.at[origin],
            device_id={axis: origin}, device_id_type=pl.DeviceIdType.MESH).wait_recv()

    over_s = (slot_s, ss_send, ss_recv, "space", me, n_space)

    over_t = (slot_t, tt_send, tt_recv, "tm", t, n_tm)

    def gathered(slots, *rest):
        count = rest[-1]
        for d in range(1, count):
            gather_wait(slots, *rest, d)
        total = slots[0]
        for i in range(1, count):
            total = total + slots[i]
        return total

    def hand_round():
        slot_t[t] = gathered(*over_s)
        for d in range(1, n_tm):
            gather_copy(*over_t, d).start()

    def rate(k):
        before = hist[k]
        return 1.0 + TIME_STEP * (1.0 - 3.0 * before * before)


    @pl.when(t < n_tm - 1)
    def _():
        st_copy(t + 1).start()

    rate_out[...] = rate(0).astype(BF16)
    send_back(0)

    for side, lanes in enumerate(edge_lanes):
        for out in inner_blocks(side):
            pulled[out, lanes] = transposed(out, blocks, lanes)

    total = jnp.zeros((8, 128), F32)
    for k in range(steps):
        d = hist[k + 1] - goal[...]
        c = ctl[k].astype(F32)
        total += 0.5 * weight(k + 1) * fold(d * d) + 0.5 * REGULAR * fold(c * c)
    slot_s[me] = total
    for d in range(1, n_space):
        gather_copy(*over_s, d).start()

    def carry_back(factor, p):
        return factor * p + TIME_STEP * PENALTY * jumps_inside(p)

    def update(k, p):
        control = ctl[k].astype(F32)
        ctl[k] = (control - (TIME_STEP * p + REGULAR * control)).astype(BF16)

    def backward(i, carry):
        k = steps - 1 - i
        rnd = steps - 1 + i
        p = pulled[...]
        gf[...] = weight(k) * (hist[k] - goal[...]) + carry_back(rate(k), p)
        held[...] = p
        for side, (rows, lanes) in enumerate(zip(edge_rows, edge_lanes)):
            pulled[rows, lanes] = transposed(rows, inner_blocks(side), lanes)

        @pl.when(i < steps - 2)
        def _():
            send_msg(rnd, lambda side: gf[edge_rows[side], edge_lanes[side]],
                     lambda side: pulled[edge_rows[side], edge_lanes[side]])

        for side, lanes in enumerate(edge_lanes):
            for out in inner_blocks(side):
                pulled[out, lanes] = transposed(out, inner_blocks(side), lanes)

        @pl.when(i == steps - 2)
        def _():
            adj_out[...] = carry_back(rate(0), pulled[...]).astype(BF16)
            send_back(1)

        @pl.when(i == 0)
        def _():
            wait_both(functools.partial(rim_copy, turn))
            for side in (0, 1):
                rim[side] = rim_in[turn, side].astype(F32)

        @pl.when(i > 0)
        def _():
            wait_both(functools.partial(msg_copy, rnd - 1))
            for side in (0, 1):
                far_g[side] = msg_in[rnd - 1, side, 0].astype(F32) + TIME_STEP * PENALTY * prev[side]
            for side in (0, 1):
                rim[side] = msg_in[rnd - 1, side, 1].astype(F32) + near_transposed(side)

        for side, (rows, lanes) in enumerate(zip(edge_rows, edge_lanes)):
            g = gf[rows, lanes] + TIME_STEP * PENALTY * rim[side]
            gf[rows, lanes] = g
            face_out[side] = g.astype(BF16)

        @pl.when(i == steps - 2)
        def _():
            send_back(2)

        for side, (rows, lanes) in enumerate(zip(edge_rows, edge_lanes)):
            pulled[rows, lanes] += transposed(rows, [rows], lanes)

        @pl.when(i == steps - 2)
        def _():
            for side, (rows, lanes) in enumerate(zip(edge_rows, edge_lanes)):
                rim_out[final, side] = pulled[rows, lanes].astype(BF16)

                @pl.when(at_side(side) & (t > 0))
                def _():
                    rim_copy(final, side, 1 - side).start()

        for side, (rows, lanes) in enumerate(zip(edge_rows, edge_lanes)):
            for out in inner_blocks(side):
                pulled[out, lanes] += transposed(out, [rows], lanes)
        for side, (rows, lanes) in enumerate(zip(edge_rows, edge_lanes)):
            prev[side] = held[rows, lanes]
        update(k, held[...])
        pl.when(i == 0)(hand_round)
        return carry

    lax.fori_loop(0, steps - 1, backward, 0)

    update(0, pulled[...])
    for k in range(steps):
        newc_ref[k] = dot(ctl[k], pt[...]).astype(BF16)

    @pl.when(t == 0)
    def _():
        nst_ref[0] = st[...]

    @pl.when(t > 0)
    def _():
        st_copy(t - 1).wait_recv()
        nst_ref[0] = dot(st_in[...], pt[...])

    @pl.when(t < n_tm - 1)
    def _():
        st_copy(t + 1).wait_send()

    total = gathered(*over_t)
    scaled = total * (1.0 / (total_steps * nodes * elements * n_space))
    obj_ref[...] = jnp.sum(jnp.sum(scaled, axis=0, keepdims=True), axis=1, keepdims=True)

    @pl.when(t == n_tm - 1)
    def _():
        nadj_ref[...] = jnp.zeros_like(nadj_ref)

    @pl.when(t < n_tm - 1)
    def _():
        for i in (0, 2):
            back_copy(i, t + 1).wait_recv()
        for side, (rows, lanes) in enumerate(zip(edge_rows, edge_lanes)):
            gf[rows, lanes] = face_in[side].astype(F32)
        for side, (rows, lanes) in enumerate(zip(edge_rows, edge_lanes)):
            for out in blocks:
                pulled[out, lanes] = transposed(out, [rows], lanes)
        gf[...] = carry_back(rate_in[...].astype(F32), pulled[...])
        back_copy(1, t + 1).wait_recv()

    wait_final_rims()

    @pl.when(t < n_tm - 1)
    def _():
        for side, (rows, lanes) in enumerate(zip(edge_rows, edge_lanes)):
            gf[rows, lanes] += TIME_STEP * PENALTY * rim_in[final, side].astype(F32)
        nadj_ref[0] = joined(dot(split(gf[...] + adj_in[...].astype(F32)), pt[...]))

    @pl.when(t > 0)
    def _():
        for i in range(3):
            back_copy(i, t - 1).wait_send()


def store_kernel(count, *refs):
    gives = [pltpu.make_async_copy(refs[i], refs[count + i], refs[-1].at[i]) for i in range(count)]
    for c in gives:
        c.start()
    for c in gives:
        c.wait()


def store(values):
    count = len(values)
    return pl.pallas_call(
        functools.partial(store_kernel, count),
        out_shape=tuple(jax.ShapeDtypeStruct(v.shape, v.dtype) for v in values),
        in_specs=[pl.BlockSpec(memory_space=pltpu.VMEM)] * count,
        out_specs=(pl.BlockSpec(memory_space=pltpu.HBM),) * count,
        scratch_shapes=[pltpu.SemaphoreType.DMA((count,))],
        compiler_params=pltpu.CompilerParams(vmem_limit_bytes=4194304),
    )(*values)


def solution(mesh):
    n_space, n_tm = mesh.shape["space"], mesh.shape["tm"]

    def per_device(controls, target, state_in, adjoint_in, block_inverse, numbering):
        steps, nodes, elements = controls.shape
        vm = pl.BlockSpec(memory_space=pltpu.VMEM)
        hbm = pl.BlockSpec(memory_space=pltpu.HBM)
        field = (nodes, elements)
        messages = max(2 * steps - 3, 1)
        bits = (n_tm - 1).bit_length()
        dma = pltpu.SemaphoreType.DMA
        new_controls, next_state, next_adjoint, objective = pl.pallas_call(
            functools.partial(kernel, n_space, n_tm),
            out_shape=(
                pltpu.VMEM(controls.shape, BF16),
                pltpu.VMEM(state_in.shape, F32),
                pltpu.VMEM(adjoint_in.shape, F32),
                pltpu.VMEM((1, 1), F32),
            ),
            in_specs=[hbm] * 6,
            out_specs=(vm, vm, vm, vm),
            scratch_shapes=[
                pltpu.VMEM(block_inverse.shape, BF16),
                pltpu.VMEM(block_inverse.shape, BF16),
                pltpu.VMEM(numbering.shape, jnp.int32),
                pltpu.VMEM(controls.shape, BF16),
                pltpu.VMEM(controls.shape, BF16),
                pltpu.VMEM(field, BF16),
                pltpu.VMEM(field, F32),
                pltpu.VMEM(field, F32),
                pltpu.VMEM(field, F32),
                pltpu.VMEM(field, F32),
                pltpu.VMEM((steps + 1,) + field, F32),
                pltpu.VMEM(field, BF16),
                pltpu.VMEM((2, BLOCK, LAYER), F32),
                pltpu.VMEM(field, F32),
                pltpu.VMEM(field, F32),
                pltpu.VMEM((elements, elements), BF16),
                pltpu.VMEM((elements, elements), BF16),
                pltpu.VMEM((3, 2, BLOCK, LAYER), BF16),
                pltpu.VMEM((3, 2, BLOCK, LAYER), BF16),
                pltpu.VMEM((messages, 2, 2, BLOCK, LAYER), BF16),
                pltpu.VMEM((messages, 2, 2, BLOCK, LAYER), BF16),
                pltpu.VMEM((2, BLOCK, BLOCK, LAYER), BF16),
                pltpu.VMEM((2, BLOCK, BLOCK, LAYER), BF16),
                pltpu.VMEM((2, BLOCK, LAYER), F32),
                pltpu.VMEM((2, BLOCK, LAYER), F32),
                pltpu.VMEM((2, BLOCK, LAYER), F32),
                pltpu.VMEM(field, F32),
                pltpu.VMEM(field, BF16),
                pltpu.VMEM(field, BF16),
                pltpu.VMEM(field, BF16),
                pltpu.VMEM(field, BF16),
                pltpu.VMEM(field, BF16),
                pltpu.VMEM(field, BF16),
                pltpu.VMEM((2, BLOCK, LAYER), BF16),
                pltpu.VMEM((2, BLOCK, LAYER), BF16),
                pltpu.VMEM((n_space, 8, 128), F32),
                pltpu.VMEM((n_tm, 8, 128), F32),
                dma((5,)),
                dma((4,)),
                dma((3, 2)),
                dma((3, 2)),
                dma((messages, 2)),
                dma((messages, 2)),
                dma((2,)),
                dma((2,)),
                dma((2,)),
                dma((2, 3)),
                dma((n_space,)),
                dma((n_space,)),
                dma((n_tm,)),
                dma((n_tm,)),
                pltpu.SemaphoreType.REGULAR((bits,)),
            ],
            compiler_params=pltpu.CompilerParams(
                collective_id=0, has_side_effects=True, vmem_limit_bytes=60000000
            ),
        )(numbering, controls, target, state_in, adjoint_in, block_inverse)
        out = store((new_controls, next_state, next_adjoint, objective))
        return out[:3] + (out[3].reshape(()),)

    return jax.shard_map(
        per_device,
        mesh=mesh,
        in_specs=(
            P("tm", None, "space"),
            P(None, "space"),
            P("tm", None, "space"),
            P("tm", None, "space"),
            P(None, None, "space"),
            P("space", None),
        ),
        out_specs=(P("tm", None, "space"), P("tm", None, "space"), P("tm", None, "space"), P()),
        check_vma=False,
    )
```

```python
import functools

import jax
import jax.numpy as jnp
from jax import lax
from jax.experimental import pallas as pl
from jax.experimental.pallas import tpu as pltpu
from jax.sharding import PartitionSpec as P

NSIDE = 4
EXY = 16
BLOCK = NSIDE * NSIDE
LAYER = EXY * EXY
TIME_STEP = 0.1
PENALTY = 0.5
REGULAR = 0.1
F32 = jnp.float32
BF16 = jnp.bfloat16


def dot(a, b):
    return jnp.dot(a, b, preferred_element_type=F32)


def fold(x):
    total = None
    for i in range(0, x.shape[0], 8):
        for j in range(0, x.shape[1], 128):
            piece = x[i : i + 8, j : j + 128]
            total = piece if total is None else total + piece
    return total


def lateral(x):
    nodes, elements = x.shape
    last = NSIDE - 1

    def by_layer(y, shift):
        return jnp.concatenate(
            [pltpu.roll(y[:, i : i + LAYER], shift, 1) for i in range(0, elements, LAYER)], axis=1
        )

    a = lax.broadcasted_iota(jnp.int32, x.shape, 0) % NSIDE
    y = jnp.where(a == last, by_layer(x, EXY), by_layer(x, LAYER - EXY)).reshape(nodes // 8, 8, elements)
    to_low = pltpu.roll(y, 8 - last, 1).reshape(nodes, elements)
    to_high = pltpu.roll(y, last, 1).reshape(nodes, elements)
    along_a = jnp.where(a == 0, to_low, jnp.where(a == last, to_high, 0.0))

    count = nodes // BLOCK
    tall = x.reshape(count, 2, 8, elements)
    low3 = lax.broadcasted_iota(jnp.int32, (count, 8, elements), 1) < NSIDE
    w = jnp.where(low3, tall[:, 0], tall[:, 1]).reshape(count * 8, elements)
    low2 = lax.broadcasted_iota(jnp.int32, w.shape, 0) % 8 < NSIDE
    row = lax.broadcasted_iota(jnp.int32, w.shape, 1) % EXY
    down = jnp.where(row == 0, pltpu.roll(w, elements - EXY + 1, 1), pltpu.roll(w, 1, 1))
    up = jnp.where(row == EXY - 1, pltpu.roll(w, EXY - 1, 1), pltpu.roll(w, elements - 1, 1))
    r = pltpu.roll(jnp.where(low2, up, down).reshape(count, 8, elements), NSIDE, 1)
    first, second = jnp.where(low3, r, 0.0), jnp.where(low3, 0.0, r)
    along_b = jnp.concatenate([v for i in range(count) for v in (first[i], second[i])], axis=0)
    return along_a + along_b


def face_count(shape):
    q = lax.broadcasted_iota(jnp.int32, shape, 0)
    count = jnp.zeros(shape, F32)
    for step in (1, NSIDE, BLOCK):
        at = (q // step) % NSIDE
        count += jnp.where((at == 0) | (at == NSIDE - 1), 1.0, 0.0)
    return count


def jumps_inside(x):
    nodes, elements = x.shape
    low, high = slice(0, BLOCK), slice(nodes - BLOCK, nodes)
    empty = jnp.zeros((BLOCK, LAYER), F32)
    below = jnp.concatenate([empty, x[high, : elements - LAYER]], axis=1)
    above = jnp.concatenate([x[low, LAYER:], empty], axis=1)
    middle = jnp.zeros((nodes - 2 * BLOCK, elements), F32)
    return lateral(x) + jnp.concatenate([below, middle, above], axis=0) - face_count(x.shape) * x


def kernel(
    n_space, n_tm,
    num_hbm, ctl_hbm, tgt_hbm, st_hbm, adj_hbm, a_hbm,
    newc_ref, nst_ref, nadj_ref, obj_ref,
    a_raw, a_ref, num, ctl_raw, ctl, tgt_raw, goal, adj_raw, adj, st, hist, r_ref, edge, gf, pulled, pa, pt,
    rim_out, rim_in, msg_out, msg_in, near_out, near_in, rim, prev, far_g, held, st_out, st_in, adj_out, adj_in, rate_out, rate_in, face_out, face_in, slot_s, slot_t,
    in_sem, a_sem, rim_send, rim_recv, msg_send, msg_recv, near_send, near_recv, st_sem, adj_sem,
    ss_send, ss_recv, tt_send, tt_recv, ready,
):
    steps, nodes, elements = ctl.shape
    me = lax.axis_index("space")
    t = lax.axis_index("tm")
    first = t * steps
    total_steps = steps * n_tm
    turn, final = 1, 2
    last_block = nodes - BLOCK
    blocks = [slice(s, s + BLOCK) for s in range(0, nodes, BLOCK)]
    edge_rows = (slice(0, BLOCK), slice(last_block, nodes))
    edge_lanes = (slice(0, LAYER), slice(elements - LAYER, elements))

    def weight(k):
        return lax.convert_element_type(first + k, F32) / total_steps

    loads = [
        pltpu.make_async_copy(src, dst, in_sem.at[i])
        for i, (src, dst) in enumerate(
            ((num_hbm, num), (st_hbm.at[0], st), (tgt_hbm, tgt_raw), (ctl_hbm, ctl_raw), (adj_hbm.at[0], adj_raw))
        )
    ]
    for c in loads[:2]:
        c.start()
    for landing in (rim_in, msg_in, near_in):
        landing[...] = jnp.zeros_like(landing)
    barrier = pltpu.get_barrier_semaphore()
    for d in range(1, n_space):
        pl.semaphore_signal(barrier, inc=1, device_id={"space": lax.rem(me + d, n_space)},
                            device_id_type=pl.DeviceIdType.MESH)
    bits = (n_tm - 1).bit_length()

    def beside(far):
        return jnp.where(t >= far, 1, 0) + jnp.where(t + far < n_tm, 1, 0)

    def greet(sem, far):
        @pl.when(t >= far)
        def _():
            pl.semaphore_signal(sem, inc=1, device_id={"tm": t - far}, device_id_type=pl.DeviceIdType.MESH)

        @pl.when(t + far < n_tm)
        def _():
            pl.semaphore_signal(sem, inc=1, device_id={"tm": t + far}, device_id_type=pl.DeviceIdType.MESH)

    greet(barrier, 1)

    def tell(j):
        if j <= bits:
            greet(ready.at[j - 1], 2 ** (j - 1))

    def hear(j):
        if j <= bits:
            pl.semaphore_wait(ready.at[j - 1], beside(2 ** (j - 1)))

    def pass_on(j):
        hear(j)
        tell(j + 1)

    parts = a_sem.shape[0]
    chunk = nodes // parts
    a_loads = [
        pltpu.make_async_copy(a_hbm.at[pl.ds(i * chunk, chunk)], a_raw.at[pl.ds(i * chunk, chunk)], a_sem.at[i])
        for i in range(parts)
    ]
    outer = [0, parts - 1]
    inner = list(range(1, parts - 1))
    for i in outer + inner:
        a_loads[i].start()
    for c in loads[2:]:
        c.start()

    loads[0].wait()
    stored = num[...]
    own = stored // LAYER * LAYER + stored % EXY * EXY + stored // EXY % EXY
    for i in range(0, elements, LAYER):
        place = lax.broadcasted_iota(jnp.int32, (LAYER, elements), 0) + i
        pt[i : i + LAYER, :] = jnp.where(own == place, 1.0, 0.0).astype(BF16)
    down = jnp.broadcast_to(own.astype(F32), (128, elements)).T
    for i in range(0, elements, 128):
        place = lax.broadcasted_iota(jnp.int32, (elements, 128), 1) + i
        pa[:, i : i + 128] = jnp.where(down == place.astype(F32), 1.0, 0.0).astype(BF16)

    def split(x):
        high = x.astype(BF16)
        return jnp.concatenate([high, (x - high.astype(F32)).astype(BF16)], axis=0)

    def joined(x):
        return x[:nodes] + x[nodes:]

    def across(src, dst, send, recv, side, back=0):
        return pltpu.make_async_remote_copy(
            src_ref=src, dst_ref=dst, send_sem=send, recv_sem=recv,
            device_id={"tm": t - back, "space": me - 1 if side == 0 else me + 1},
            device_id_type=pl.DeviceIdType.MESH,
        )

    def rim_copy(rnd, side, slot):
        return across(rim_out.at[rnd, side], rim_in.at[rnd, slot], rim_send.at[rnd, side], rim_recv.at[rnd, slot],
                      side, 1 if rnd == final else 0)

    def msg_copy(rnd, side, slot):
        return across(msg_out.at[rnd, side], msg_in.at[rnd, slot], msg_send.at[rnd, side], msg_recv.at[rnd, slot], side)

    def near_copy(side, slot):
        return across(near_out.at[side], near_in.at[slot], near_send.at[side], near_recv.at[slot], side)

    def at_side(side):
        return me > 0 if side == 0 else me < n_space - 1

    def start_both(copy):
        for side in (0, 1):
            @pl.when(at_side(side))
            def _():
                copy(side, 1 - side).start()

    def wait_both(copy):
        for side in (0, 1):
            @pl.when(at_side(side))
            def _():
                copy(side, side).wait()

    def send_msg(rnd, base, ahead):
        for side in (0, 1):
            msg_out[rnd, side, 0] = base(side).astype(BF16)
            msg_out[rnd, side, 1] = ahead(side).astype(BF16)
        start_both(functools.partial(msg_copy, rnd))

    def wait_final_rims():
        for side in (0, 1):
            @pl.when(at_side(side) & (t < n_tm - 1))
            def _():
                rim_copy(final, side, side).wait_recv()

            @pl.when(at_side(side) & (t > 0))
            def _():
                rim_copy(final, side, side).wait_send()

    depth = BLOCK * BLOCK
    place_k = lax.broadcasted_iota(jnp.int32, (BLOCK, depth), 1)
    place_r = lax.broadcasted_iota(jnp.int32, (BLOCK, depth), 0)
    sum_rows = jnp.where(place_k // BLOCK == place_r, 1.0, 0.0).astype(BF16)
    sum_groups = jnp.where(place_k % BLOCK == place_r, 1.0, 0.0).astype(BF16)
    sum_rows2 = jnp.concatenate([sum_rows, sum_rows], axis=1)

    def groups(n):
        place_c = lax.broadcasted_iota(jnp.int32, (BLOCK, n), 1) % BLOCK
        return jnp.where(place_c == lax.broadcasted_iota(jnp.int32, (BLOCK, n), 0), 1.0, 0.0).astype(BF16)

    def product(out, into, lanes, right):
        return (a_ref[out, into, lanes] * right[None]).reshape(depth, LAYER)

    def product_pair(out, into, lanes, right):
        (i0, i1), (r0, r1) = into, right
        return (a_ref[out, i0, lanes] * r0[None] + a_ref[out, i1, lanes] * r1[None]).reshape(depth, LAYER)

    def inner_blocks(side):
        return [b for b in blocks if b != edge_rows[side]]

    def apply_inner(side, outs, write):
        lanes = edge_lanes[side]
        b0, b1, b2 = inner_blocks(side)
        if side == 0:
            pair, single = (b0, b1), b2
        else:
            pair, single = (b1, b2), b0
        rp = (r_ref[pair[0], lanes], r_ref[pair[1], lanes])
        rs = r_ref[single, lanes]
        for out in outs:
            q = jnp.concatenate([product_pair(out, pair, lanes, rp), product(out, single, lanes, rs)], axis=0)
            write(out, lanes, dot(sum_rows2, q))

    def transposed(out, into, lanes):
        rows = [i for b in into for i in range(b.start, b.stop)]

        def term(i):
            row = jnp.broadcast_to(gf[i : i + 1, lanes], (BLOCK, LAYER)).astype(BF16)
            return a_ref[i, out, lanes] * row

        pieces = [term(rows[i]) + term(rows[i + 1]) for i in range(0, len(rows), 2)]
        return dot(groups(BLOCK * len(pieces)), jnp.concatenate(pieces, axis=0))

    def near_transposed(side):
        def term(i):
            row = jnp.broadcast_to(far_g[side, i : i + 1], (BLOCK, LAYER)).astype(BF16)
            return near_in[side, i] * row

        pieces = [term(i) + term(i + 1) for i in range(0, BLOCK, 2)]
        return dot(groups(BLOCK * len(pieces)), jnp.concatenate(pieces, axis=0))

    loads[1].wait()
    hist[0] = joined(dot(split(st[...]), pa[...]))
    for side in (0, 1):
        rim_out[0, side] = hist[0, edge_rows[side], edge_lanes[side]].astype(BF16)
    piece = depth // nodes

    def permute(part):
        for i in range(part * chunk, (part + 1) * chunk, piece):
            rows = a_raw[i : i + piece].reshape(depth, elements)
            a_ref[i : i + piece] = dot(rows, pa[...]).astype(BF16).reshape(piece, nodes, elements)

    a_loads[outer[0]].wait()
    permute(outer[0])
    pl.semaphore_wait(barrier, n_space - 1 + beside(1))
    start_both(functools.partial(rim_copy, 0))
    tell(1)
    near_out[0] = a_ref[edge_rows[0], edge_rows[0], edge_lanes[0]]
    a_loads[outer[1]].wait()
    corner = dot(a_raw[edge_rows[1], edge_rows[1]].reshape(depth, elements), pa[:, edge_lanes[1]])
    near_out[1] = corner.astype(BF16).reshape(BLOCK, BLOCK, LAYER)
    start_both(near_copy)

    for c in loads[2:]:
        c.wait()
    goal[...] = dot(tgt_raw[...], pa[...])
    adj[...] = joined(dot(split(adj_raw[...]), pa[...]))
    for k in range(steps):
        ctl[k] = dot(ctl_raw[k], pa[...]).astype(BF16)
    def prepare(k):
        u = hist[k]
        c = ctl[k].astype(F32)
        base = u + TIME_STEP * (u - u * u * u) + TIME_STEP * PENALTY * jumps_inside(u) + TIME_STEP * c
        r_ref[...] = base.astype(BF16)
        for side in (0, 1):
            edge[side] = base[edge_rows[side], edge_lanes[side]]

    def keep(k):
        def write(rows, lanes, v):
            hist[k + 1, rows, lanes] = v

        return write

    def right_edges():
        return [(edge[side] + TIME_STEP * PENALTY * rim[side]).astype(BF16) for side in (0, 1)]

    def step_edges(k, right):
        for side, (rows, lanes) in enumerate(zip(edge_rows, edge_lanes)):
            hist[k + 1, rows, lanes] += dot(sum_rows, product(rows, rows, lanes, right[side]))

    def send_ahead(k):
        send_msg(k, lambda side: edge[side], lambda side: hist[k + 1, edge_rows[side], edge_lanes[side]])

    def far_rims(k):
        for side, (rows, lanes) in enumerate(zip(edge_rows, edge_lanes)):
            far = msg_in[k, side, 0].astype(F32) + TIME_STEP * PENALTY * hist[k, rows, lanes]
            q = (near_in[side] * far.astype(BF16)[None]).reshape(depth, LAYER)
            rim[side] = msg_in[k, side, 1].astype(F32) + dot(sum_rows, q)

    def step_rest(k, right):
        for side, (rows, lanes) in enumerate(zip(edge_rows, edge_lanes)):
            for out in inner_blocks(side):
                hist[k + 1, out, lanes] += dot(sum_rows, product(out, rows, lanes, right[side]))

    prepare(0)
    permute(outer[1])
    pass_on(1)
    for side in (0, 1):
        apply_inner(side, [edge_rows[side]], keep(0))
    if steps > 1:
        send_ahead(0)
    for part in inner:
        a_loads[part].wait()
        permute(part)
    pass_on(2)
    for side in (0, 1):
        apply_inner(side, inner_blocks(side), keep(0))
    wait_both(functools.partial(rim_copy, 0))
    for side in (0, 1):
        rim[side] = rim_in[0, side].astype(F32)
    first_right = right_edges()
    step_edges(0, first_right)
    step_rest(0, first_right)

    def forward(k, carry):
        prepare(k)
        for side in (0, 1):
            apply_inner(side, [edge_rows[side]], keep(k))
        pl.when(k < steps - 1)(functools.partial(send_ahead, k))
        for side in (0, 1):
            apply_inner(side, inner_blocks(side), keep(k))
        pl.when(k == 1)(functools.partial(wait_both, near_copy))
        wait_both(functools.partial(msg_copy, k - 1))
        far_rims(k - 1)
        right = right_edges()
        step_edges(k, right)
        step_rest(k, right)
        for j in range(3, min(bits, steps + 2)):
            pl.when(k == j - 2)(functools.partial(pass_on, j))
        return carry

    lax.fori_loop(1, steps, forward, 0)

    w_end = weight(steps)
    u = hist[steps]
    gf[...] = w_end * (u - goal[...]) + adj[...]

    for side, (rows, lanes) in enumerate(zip(edge_rows, edge_lanes)):
        v = transposed(rows, blocks, lanes)
        pulled[rows, lanes] = v
        rim_out[turn, side] = v.astype(BF16)
    start_both(functools.partial(rim_copy, turn))

    st_out[...] = hist[steps].astype(BF16)

    def st_copy(dst):
        return pltpu.make_async_remote_copy(
            src_ref=st_out, dst_ref=st_in, send_sem=st_sem.at[0], recv_sem=st_sem.at[1],
            device_id={"tm": dst}, device_id_type=pl.DeviceIdType.MESH)

    def back_copy(i, dst):
        src, land = ((rate_out, rate_in), (adj_out, adj_in), (face_out, face_in))[i]
        return pltpu.make_async_remote_copy(
            src_ref=src, dst_ref=land, send_sem=adj_sem.at[0, i], recv_sem=adj_sem.at[1, i],
            device_id={"tm": dst}, device_id_type=pl.DeviceIdType.MESH)

    def send_back(i):
        @pl.when(t > 0)
        def _():
            back_copy(i, t - 1).start()


    def gather_copy(slots, send, recv, axis, index, count, d):
        return pltpu.make_async_remote_copy(
            src_ref=slots.at[index], dst_ref=slots.at[index], send_sem=send.at[d], recv_sem=recv.at[index],
            device_id={axis: lax.rem(index + d, count)}, device_id_type=pl.DeviceIdType.MESH)

    def gather_wait(slots, send, recv, axis, index, count, d):
        gather_copy(slots, send, recv, axis, index, count, d).wait_send()
        origin = lax.rem(index + d, count)
        pltpu.make_async_remote_copy(
            src_ref=slots.at[origin], dst_ref=slots.at[origin], send_sem=send.at[d], recv_sem=recv.at[origin],
            device_id={axis: origin}, device_id_type=pl.DeviceIdType.MESH).wait_recv()

    over_s = (slot_s, ss_send, ss_recv, "space", me, n_space)

    over_t = (slot_t, tt_send, tt_recv, "tm", t, n_tm)

    def gathered(slots, *rest):
        count = rest[-1]
        for d in range(1, count):
            gather_wait(slots, *rest, d)
        total = slots[0]
        for i in range(1, count):
            total = total + slots[i]
        return total

    def hand_round():
        for j in range(max(3, min(bits, steps + 2)), bits + 1):
            pass_on(j)
        slot_t[t] = gathered(*over_s)
        for d in range(1, n_tm):
            gather_copy(*over_t, d).start()

    def rate(k):
        before = hist[k]
        return 1.0 + TIME_STEP * (1.0 - 3.0 * before * before)


    @pl.when(t < n_tm - 1)
    def _():
        st_copy(t + 1).start()

    rate_out[...] = rate(0).astype(BF16)
    send_back(0)

    for side, lanes in enumerate(edge_lanes):
        for out in inner_blocks(side):
            pulled[out, lanes] = transposed(out, blocks, lanes)

    total = jnp.zeros((8, 128), F32)
    for k in range(steps):
        d = hist[k + 1] - goal[...]
        c = ctl[k].astype(F32)
        total += 0.5 * weight(k + 1) * fold(d * d) + 0.5 * REGULAR * fold(c * c)
    slot_s[me] = total
    for d in range(1, n_space):
        gather_copy(*over_s, d).start()

    def carry_back(factor, p):
        return factor * p + TIME_STEP * PENALTY * jumps_inside(p)

    def update(k, p):
        control = ctl[k].astype(F32)
        ctl[k] = (control - (TIME_STEP * p + REGULAR * control)).astype(BF16)

    def backward(i, carry):
        k = steps - 1 - i
        rnd = steps - 1 + i
        p = pulled[...]
        gf[...] = weight(k) * (hist[k] - goal[...]) + carry_back(rate(k), p)
        held[...] = p
        for side, (rows, lanes) in enumerate(zip(edge_rows, edge_lanes)):
            pulled[rows, lanes] = transposed(rows, inner_blocks(side), lanes)

        @pl.when(i < steps - 2)
        def _():
            send_msg(rnd, lambda side: gf[edge_rows[side], edge_lanes[side]],
                     lambda side: pulled[edge_rows[side], edge_lanes[side]])

        for side, lanes in enumerate(edge_lanes):
            for out in inner_blocks(side):
                pulled[out, lanes] = transposed(out, inner_blocks(side), lanes)

        @pl.when(i == steps - 2)
        def _():
            adj_out[...] = carry_back(rate(0), pulled[...]).astype(BF16)
            send_back(1)

        @pl.when(i == 0)
        def _():
            wait_both(functools.partial(rim_copy, turn))
            for side in (0, 1):
                rim[side] = rim_in[turn, side].astype(F32)

        @pl.when(i > 0)
        def _():
            wait_both(functools.partial(msg_copy, rnd - 1))
            for side in (0, 1):
                far_g[side] = msg_in[rnd - 1, side, 0].astype(F32) + TIME_STEP * PENALTY * prev[side]
            for side in (0, 1):
                rim[side] = msg_in[rnd - 1, side, 1].astype(F32) + near_transposed(side)

        for side, (rows, lanes) in enumerate(zip(edge_rows, edge_lanes)):
            g = gf[rows, lanes] + TIME_STEP * PENALTY * rim[side]
            gf[rows, lanes] = g
            face_out[side] = g.astype(BF16)

        @pl.when(i == steps - 2)
        def _():
            send_back(2)

        for side, (rows, lanes) in enumerate(zip(edge_rows, edge_lanes)):
            pulled[rows, lanes] += transposed(rows, [rows], lanes)

        @pl.when(i == steps - 2)
        def _():
            for side, (rows, lanes) in enumerate(zip(edge_rows, edge_lanes)):
                rim_out[final, side] = pulled[rows, lanes].astype(BF16)

                @pl.when(at_side(side) & (t > 0))
                def _():
                    rim_copy(final, side, 1 - side).start()

        for side, (rows, lanes) in enumerate(zip(edge_rows, edge_lanes)):
            for out in inner_blocks(side):
                pulled[out, lanes] += transposed(out, [rows], lanes)
        for side, (rows, lanes) in enumerate(zip(edge_rows, edge_lanes)):
            prev[side] = held[rows, lanes]
        update(k, held[...])
        pl.when(i == 0)(hand_round)
        return carry

    lax.fori_loop(0, steps - 1, backward, 0)

    update(0, pulled[...])
    for k in range(steps):
        newc_ref[k] = dot(ctl[k], pt[...]).astype(BF16)

    @pl.when(t == 0)
    def _():
        nst_ref[0] = st[...]

    @pl.when(t > 0)
    def _():
        st_copy(t - 1).wait_recv()
        nst_ref[0] = dot(st_in[...], pt[...])

    @pl.when(t < n_tm - 1)
    def _():
        st_copy(t + 1).wait_send()

    total = gathered(*over_t)
    scaled = total * (1.0 / (total_steps * nodes * elements * n_space))
    obj_ref[...] = jnp.sum(jnp.sum(scaled, axis=0, keepdims=True), axis=1, keepdims=True)

    @pl.when(t == n_tm - 1)
    def _():
        nadj_ref[...] = jnp.zeros_like(nadj_ref)

    @pl.when(t < n_tm - 1)
    def _():
        for i in (0, 2):
            back_copy(i, t + 1).wait_recv()
        for side, (rows, lanes) in enumerate(zip(edge_rows, edge_lanes)):
            gf[rows, lanes] = face_in[side].astype(F32)
        for side, (rows, lanes) in enumerate(zip(edge_rows, edge_lanes)):
            for out in blocks:
                pulled[out, lanes] = transposed(out, [rows], lanes)
        gf[...] = carry_back(rate_in[...].astype(F32), pulled[...])
        back_copy(1, t + 1).wait_recv()

    wait_final_rims()

    @pl.when(t < n_tm - 1)
    def _():
        for side, (rows, lanes) in enumerate(zip(edge_rows, edge_lanes)):
            gf[rows, lanes] += TIME_STEP * PENALTY * rim_in[final, side].astype(F32)
        nadj_ref[0] = joined(dot(split(gf[...] + adj_in[...].astype(F32)), pt[...]))

    @pl.when(t > 0)
    def _():
        for i in range(3):
            back_copy(i, t - 1).wait_send()


def store_kernel(count, *refs):
    gives = [pltpu.make_async_copy(refs[i], refs[count + i], refs[-1].at[i]) for i in range(count)]
    for c in gives:
        c.start()
    for c in gives:
        c.wait()


def store(values):
    count = len(values)
    return pl.pallas_call(
        functools.partial(store_kernel, count),
        out_shape=tuple(jax.ShapeDtypeStruct(v.shape, v.dtype) for v in values),
        in_specs=[pl.BlockSpec(memory_space=pltpu.VMEM)] * count,
        out_specs=(pl.BlockSpec(memory_space=pltpu.HBM),) * count,
        scratch_shapes=[pltpu.SemaphoreType.DMA((count,))],
        compiler_params=pltpu.CompilerParams(vmem_limit_bytes=4194304),
    )(*values)


def solution(mesh):
    n_space, n_tm = mesh.shape["space"], mesh.shape["tm"]

    def per_device(controls, target, state_in, adjoint_in, block_inverse, numbering):
        steps, nodes, elements = controls.shape
        vm = pl.BlockSpec(memory_space=pltpu.VMEM)
        hbm = pl.BlockSpec(memory_space=pltpu.HBM)
        field = (nodes, elements)
        messages = max(2 * steps - 3, 1)
        bits = (n_tm - 1).bit_length()
        dma = pltpu.SemaphoreType.DMA
        new_controls, next_state, next_adjoint, objective = pl.pallas_call(
            functools.partial(kernel, n_space, n_tm),
            out_shape=(
                pltpu.VMEM(controls.shape, BF16),
                pltpu.VMEM(state_in.shape, F32),
                pltpu.VMEM(adjoint_in.shape, F32),
                pltpu.VMEM((1, 1), F32),
            ),
            in_specs=[hbm] * 6,
            out_specs=(vm, vm, vm, vm),
            scratch_shapes=[
                pltpu.VMEM(block_inverse.shape, BF16),
                pltpu.VMEM(block_inverse.shape, BF16),
                pltpu.VMEM(numbering.shape, jnp.int32),
                pltpu.VMEM(controls.shape, BF16),
                pltpu.VMEM(controls.shape, BF16),
                pltpu.VMEM(field, BF16),
                pltpu.VMEM(field, F32),
                pltpu.VMEM(field, F32),
                pltpu.VMEM(field, F32),
                pltpu.VMEM(field, F32),
                pltpu.VMEM((steps + 1,) + field, F32),
                pltpu.VMEM(field, BF16),
                pltpu.VMEM((2, BLOCK, LAYER), F32),
                pltpu.VMEM(field, F32),
                pltpu.VMEM(field, F32),
                pltpu.VMEM((elements, elements), BF16),
                pltpu.VMEM((elements, elements), BF16),
                pltpu.VMEM((3, 2, BLOCK, LAYER), BF16),
                pltpu.VMEM((3, 2, BLOCK, LAYER), BF16),
                pltpu.VMEM((messages, 2, 2, BLOCK, LAYER), BF16),
                pltpu.VMEM((messages, 2, 2, BLOCK, LAYER), BF16),
                pltpu.VMEM((2, BLOCK, BLOCK, LAYER), BF16),
                pltpu.VMEM((2, BLOCK, BLOCK, LAYER), BF16),
                pltpu.VMEM((2, BLOCK, LAYER), F32),
                pltpu.VMEM((2, BLOCK, LAYER), F32),
                pltpu.VMEM((2, BLOCK, LAYER), F32),
                pltpu.VMEM(field, F32),
                pltpu.VMEM(field, BF16),
                pltpu.VMEM(field, BF16),
                pltpu.VMEM(field, BF16),
                pltpu.VMEM(field, BF16),
                pltpu.VMEM(field, BF16),
                pltpu.VMEM(field, BF16),
                pltpu.VMEM((2, BLOCK, LAYER), BF16),
                pltpu.VMEM((2, BLOCK, LAYER), BF16),
                pltpu.VMEM((n_space, 8, 128), F32),
                pltpu.VMEM((n_tm, 8, 128), F32),
                dma((5,)),
                dma((4,)),
                dma((3, 2)),
                dma((3, 2)),
                dma((messages, 2)),
                dma((messages, 2)),
                dma((2,)),
                dma((2,)),
                dma((2,)),
                dma((2, 3)),
                dma((n_space,)),
                dma((n_space,)),
                dma((n_tm,)),
                dma((n_tm,)),
                pltpu.SemaphoreType.REGULAR((bits,)),
            ],
            compiler_params=pltpu.CompilerParams(
                collective_id=0, has_side_effects=True, vmem_limit_bytes=60000000
            ),
        )(numbering, controls, target, state_in, adjoint_in, block_inverse)
        out = store((new_controls, next_state, next_adjoint, objective))
        return out[:3] + (out[3].reshape(()),)

    return jax.shard_map(
        per_device,
        mesh=mesh,
        in_specs=(
            P("tm", None, "space"),
            P(None, "space"),
            P("tm", None, "space"),
            P("tm", None, "space"),
            P(None, None, "space"),
            P("space", None),
        ),
        out_specs=(P("tm", None, "space"), P("tm", None, "space"), P("tm", None, "space"), P()),
        check_vma=False,
    )
```

```python
import functools

import jax
import jax.numpy as jnp
from jax import lax
from jax.experimental import pallas as pl
from jax.experimental.pallas import tpu as pltpu
from jax.sharding import PartitionSpec as P

NSIDE = 4
EXY = 16
BLOCK = NSIDE * NSIDE
LAYER = EXY * EXY
TIME_STEP = 0.1
PENALTY = 0.5
REGULAR = 0.1
F32 = jnp.float32
BF16 = jnp.bfloat16


def dot(a, b):
    return jnp.dot(a, b, preferred_element_type=F32)


def fold(x):
    total = None
    for i in range(0, x.shape[0], 8):
        for j in range(0, x.shape[1], 128):
            piece = x[i : i + 8, j : j + 128]
            total = piece if total is None else total + piece
    return total


def lateral(x):
    nodes, elements = x.shape
    last = NSIDE - 1

    def by_layer(y, shift):
        return jnp.concatenate(
            [pltpu.roll(y[:, i : i + LAYER], shift, 1) for i in range(0, elements, LAYER)], axis=1
        )

    a = lax.broadcasted_iota(jnp.int32, x.shape, 0) % NSIDE
    y = jnp.where(a == last, by_layer(x, EXY), by_layer(x, LAYER - EXY)).reshape(nodes // 8, 8, elements)
    to_low = pltpu.roll(y, 8 - last, 1).reshape(nodes, elements)
    to_high = pltpu.roll(y, last, 1).reshape(nodes, elements)
    along_a = jnp.where(a == 0, to_low, jnp.where(a == last, to_high, 0.0))

    count = nodes // BLOCK
    tall = x.reshape(count, 2, 8, elements)
    low3 = lax.broadcasted_iota(jnp.int32, (count, 8, elements), 1) < NSIDE
    w = jnp.where(low3, tall[:, 0], tall[:, 1]).reshape(count * 8, elements)
    low2 = lax.broadcasted_iota(jnp.int32, w.shape, 0) % 8 < NSIDE
    row = lax.broadcasted_iota(jnp.int32, w.shape, 1) % EXY
    down = jnp.where(row == 0, pltpu.roll(w, elements - EXY + 1, 1), pltpu.roll(w, 1, 1))
    up = jnp.where(row == EXY - 1, pltpu.roll(w, EXY - 1, 1), pltpu.roll(w, elements - 1, 1))
    r = pltpu.roll(jnp.where(low2, up, down).reshape(count, 8, elements), NSIDE, 1)
    first, second = jnp.where(low3, r, 0.0), jnp.where(low3, 0.0, r)
    along_b = jnp.concatenate([v for i in range(count) for v in (first[i], second[i])], axis=0)
    return along_a + along_b


def face_count(shape):
    q = lax.broadcasted_iota(jnp.int32, shape, 0)
    count = jnp.zeros(shape, F32)
    for step in (1, NSIDE, BLOCK):
        at = (q // step) % NSIDE
        count += jnp.where((at == 0) | (at == NSIDE - 1), 1.0, 0.0)
    return count


def jumps_inside(x):
    nodes, elements = x.shape
    low, high = slice(0, BLOCK), slice(nodes - BLOCK, nodes)
    empty = jnp.zeros((BLOCK, LAYER), F32)
    below = jnp.concatenate([empty, x[high, : elements - LAYER]], axis=1)
    above = jnp.concatenate([x[low, LAYER:], empty], axis=1)
    middle = jnp.zeros((nodes - 2 * BLOCK, elements), F32)
    return lateral(x) + jnp.concatenate([below, middle, above], axis=0) - face_count(x.shape) * x


def kernel(
    n_space, n_tm,
    num_hbm, ctl_hbm, tgt_hbm, st_hbm, adj_hbm, a_hbm,
    newc_ref, nst_ref, nadj_ref, obj_ref,
    a_raw, a_ref, num, ctl_raw, ctl, tgt_raw, goal, adj_raw, adj, st, hist, r_ref, edge, gf, pulled, pa, pt,
    rim_out, rim_in, msg_out, msg_in, near_out, near_in, rim, prev, far_g, held, st_out, st_in, adj_out, adj_in, rate_out, rate_in, face_out, face_in, slot_s, slot_t,
    in_sem, a_sem, rim_send, rim_recv, msg_send, msg_recv, near_send, near_recv, st_sem, adj_sem,
    ss_send, ss_recv, tt_send, tt_recv, ready,
):
    steps, nodes, elements = ctl.shape
    me = lax.axis_index("space")
    t = lax.axis_index("tm")
    first = t * steps
    total_steps = steps * n_tm
    turn, final = 1, 2
    last_block = nodes - BLOCK
    blocks = [slice(s, s + BLOCK) for s in range(0, nodes, BLOCK)]
    edge_rows = (slice(0, BLOCK), slice(last_block, nodes))
    edge_lanes = (slice(0, LAYER), slice(elements - LAYER, elements))

    def weight(k):
        return lax.convert_element_type(first + k, F32) / total_steps

    loads = [
        pltpu.make_async_copy(src, dst, in_sem.at[i])
        for i, (src, dst) in enumerate(
            ((num_hbm, num), (st_hbm.at[0], st), (tgt_hbm, tgt_raw), (ctl_hbm, ctl_raw), (adj_hbm.at[0], adj_raw))
        )
    ]
    for c in loads[:2]:
        c.start()
    for landing in (rim_in, msg_in, near_in):
        landing[...] = jnp.zeros_like(landing)
    barrier = pltpu.get_barrier_semaphore()
    for d in range(1, n_space):
        pl.semaphore_signal(barrier, inc=1, device_id={"space": lax.rem(me + d, n_space)},
                            device_id_type=pl.DeviceIdType.MESH)
    bits = (n_tm - 1).bit_length()

    def beside(far):
        return jnp.where(t >= far, 1, 0) + jnp.where(t + far < n_tm, 1, 0)

    def greet(sem, far):
        @pl.when(t >= far)
        def _():
            pl.semaphore_signal(sem, inc=1, device_id={"tm": t - far}, device_id_type=pl.DeviceIdType.MESH)

        @pl.when(t + far < n_tm)
        def _():
            pl.semaphore_signal(sem, inc=1, device_id={"tm": t + far}, device_id_type=pl.DeviceIdType.MESH)

    greet(barrier, 1)

    def tell(j):
        if j <= bits:
            greet(ready.at[j - 1], 2 ** (j - 1))

    def hear(j):
        if j <= bits:
            pl.semaphore_wait(ready.at[j - 1], beside(2 ** (j - 1)))

    def pass_on(j):
        hear(j)
        tell(j + 1)

    parts = a_sem.shape[0]
    chunk = nodes // parts
    a_loads = [
        pltpu.make_async_copy(a_hbm.at[pl.ds(i * chunk, chunk)], a_raw.at[pl.ds(i * chunk, chunk)], a_sem.at[i])
        for i in range(parts)
    ]
    outer = [0, parts - 1]
    inner = list(range(1, parts - 1))
    for i in outer + inner:
        a_loads[i].start()
    for c in loads[2:]:
        c.start()

    loads[0].wait()
    stored = num[...]
    own = stored // LAYER * LAYER + stored % EXY * EXY + stored // EXY % EXY
    for i in range(0, elements, LAYER):
        place = lax.broadcasted_iota(jnp.int32, (LAYER, elements), 0) + i
        pt[i : i + LAYER, :] = jnp.where(own == place, 1.0, 0.0).astype(BF16)
    down = jnp.broadcast_to(own.astype(F32), (128, elements)).T
    for i in range(0, elements, 128):
        place = lax.broadcasted_iota(jnp.int32, (elements, 128), 1) + i
        pa[:, i : i + 128] = jnp.where(down == place.astype(F32), 1.0, 0.0).astype(BF16)

    def split(x):
        high = x.astype(BF16)
        return jnp.concatenate([high, (x - high.astype(F32)).astype(BF16)], axis=0)

    def joined(x):
        return x[:nodes] + x[nodes:]

    def across(src, dst, send, recv, side, back=0):
        return pltpu.make_async_remote_copy(
            src_ref=src, dst_ref=dst, send_sem=send, recv_sem=recv,
            device_id={"tm": t - back, "space": me - 1 if side == 0 else me + 1},
            device_id_type=pl.DeviceIdType.MESH,
        )

    def rim_copy(rnd, side, slot):
        return across(rim_out.at[rnd, side], rim_in.at[rnd, slot], rim_send.at[rnd, side], rim_recv.at[rnd, slot],
                      side, 1 if rnd == final else 0)

    def msg_copy(rnd, side, slot):
        return across(msg_out.at[rnd, side], msg_in.at[rnd, slot], msg_send.at[rnd, side], msg_recv.at[rnd, slot], side)

    def near_copy(side, slot):
        return across(near_out.at[side], near_in.at[slot], near_send.at[side], near_recv.at[slot], side)

    def at_side(side):
        return me > 0 if side == 0 else me < n_space - 1

    def start_both(copy):
        for side in (0, 1):
            @pl.when(at_side(side))
            def _():
                copy(side, 1 - side).start()

    def wait_both(copy):
        for side in (0, 1):
            @pl.when(at_side(side))
            def _():
                copy(side, side).wait()

    def send_msg(rnd, base, ahead):
        for side in (0, 1):
            msg_out[rnd, side, 0] = base(side).astype(BF16)
            msg_out[rnd, side, 1] = ahead(side).astype(BF16)
        start_both(functools.partial(msg_copy, rnd))

    def wait_final_rims():
        for side in (0, 1):
            @pl.when(at_side(side) & (t < n_tm - 1))
            def _():
                rim_copy(final, side, side).wait_recv()

            @pl.when(at_side(side) & (t > 0))
            def _():
                rim_copy(final, side, side).wait_send()

    depth = BLOCK * BLOCK
    place_k = lax.broadcasted_iota(jnp.int32, (BLOCK, depth), 1)
    place_r = lax.broadcasted_iota(jnp.int32, (BLOCK, depth), 0)
    sum_rows = jnp.where(place_k // BLOCK == place_r, 1.0, 0.0).astype(BF16)
    sum_groups = jnp.where(place_k % BLOCK == place_r, 1.0, 0.0).astype(BF16)
    sum_rows2 = jnp.concatenate([sum_rows, sum_rows], axis=1)

    def groups(n):
        place_c = lax.broadcasted_iota(jnp.int32, (BLOCK, n), 1) % BLOCK
        return jnp.where(place_c == lax.broadcasted_iota(jnp.int32, (BLOCK, n), 0), 1.0, 0.0).astype(BF16)

    def product(out, into, lanes, right):
        return (a_ref[out, into, lanes] * right[None]).reshape(depth, LAYER)

    def product_pair(out, into, lanes, right):
        (i0, i1), (r0, r1) = into, right
        return (a_ref[out, i0, lanes] * r0[None] + a_ref[out, i1, lanes] * r1[None]).reshape(depth, LAYER)

    def inner_blocks(side):
        return [b for b in blocks if b != edge_rows[side]]

    def apply_inner(side, outs, write):
        lanes = edge_lanes[side]
        b0, b1, b2 = inner_blocks(side)
        if side == 0:
            pair, single = (b0, b1), b2
        else:
            pair, single = (b1, b2), b0
        rp = (r_ref[pair[0], lanes], r_ref[pair[1], lanes])
        rs = r_ref[single, lanes]
        for out in outs:
            q = jnp.concatenate([product_pair(out, pair, lanes, rp), product(out, single, lanes, rs)], axis=0)
            write(out, lanes, dot(sum_rows2, q))

    def transposed(out, into, lanes):
        rows = [i for b in into for i in range(b.start, b.stop)]

        def term(i):
            row = jnp.broadcast_to(gf[i : i + 1, lanes], (BLOCK, LAYER)).astype(BF16)
            return a_ref[i, out, lanes] * row

        pieces = [term(rows[i]) + term(rows[i + 1]) for i in range(0, len(rows), 2)]
        return dot(groups(BLOCK * len(pieces)), jnp.concatenate(pieces, axis=0))

    def near_transposed(side):
        def term(i):
            row = jnp.broadcast_to(far_g[side, i : i + 1], (BLOCK, LAYER)).astype(BF16)
            return near_in[side, i] * row

        pieces = [term(i) + term(i + 1) for i in range(0, BLOCK, 2)]
        return dot(groups(BLOCK * len(pieces)), jnp.concatenate(pieces, axis=0))

    loads[1].wait()
    hist[0] = joined(dot(split(st[...]), pa[...]))
    for side in (0, 1):
        rim_out[0, side] = hist[0, edge_rows[side], edge_lanes[side]].astype(BF16)
    piece = depth // nodes

    def permute(part):
        for i in range(part * chunk, (part + 1) * chunk, piece):
            rows = a_raw[i : i + piece].reshape(depth, elements)
            a_ref[i : i + piece] = dot(rows, pa[...]).astype(BF16).reshape(piece, nodes, elements)

    a_loads[outer[0]].wait()
    permute(outer[0])
    pl.semaphore_wait(barrier, n_space - 1 + beside(1))
    start_both(functools.partial(rim_copy, 0))
    tell(1)
    near_out[0] = a_ref[edge_rows[0], edge_rows[0], edge_lanes[0]]
    a_loads[outer[1]].wait()
    corner = dot(a_raw[edge_rows[1], edge_rows[1]].reshape(depth, elements), pa[:, edge_lanes[1]])
    near_out[1] = corner.astype(BF16).reshape(BLOCK, BLOCK, LAYER)
    start_both(near_copy)

    loads[3].wait()
    for k in range(min(2, steps)):
        ctl[k] = dot(ctl_raw[k], pa[...]).astype(BF16)

    def arrange_later():
        for c in (loads[2], loads[4]):
            c.wait()
        goal[...] = dot(tgt_raw[...], pa[...])
        adj[...] = joined(dot(split(adj_raw[...]), pa[...]))
        for k in range(2, steps):
            ctl[k] = dot(ctl_raw[k], pa[...]).astype(BF16)

    def prepare(k):
        u = hist[k]
        c = ctl[k].astype(F32)
        base = u + TIME_STEP * (u - u * u * u) + TIME_STEP * PENALTY * jumps_inside(u) + TIME_STEP * c
        r_ref[...] = base.astype(BF16)
        for side in (0, 1):
            edge[side] = base[edge_rows[side], edge_lanes[side]]

    def keep(k):
        def write(rows, lanes, v):
            hist[k + 1, rows, lanes] = v

        return write

    def right_edges():
        return [(edge[side] + TIME_STEP * PENALTY * rim[side]).astype(BF16) for side in (0, 1)]

    def step_edges(k, right):
        for side, (rows, lanes) in enumerate(zip(edge_rows, edge_lanes)):
            hist[k + 1, rows, lanes] += dot(sum_rows, product(rows, rows, lanes, right[side]))

    def send_ahead(k):
        send_msg(k, lambda side: edge[side], lambda side: hist[k + 1, edge_rows[side], edge_lanes[side]])

    def far_rims(k):
        for side, (rows, lanes) in enumerate(zip(edge_rows, edge_lanes)):
            far = msg_in[k, side, 0].astype(F32) + TIME_STEP * PENALTY * hist[k, rows, lanes]
            q = (near_in[side] * far.astype(BF16)[None]).reshape(depth, LAYER)
            rim[side] = msg_in[k, side, 1].astype(F32) + dot(sum_rows, q)

    def step_rest(k, right):
        for side, (rows, lanes) in enumerate(zip(edge_rows, edge_lanes)):
            for out in inner_blocks(side):
                hist[k + 1, out, lanes] += dot(sum_rows, product(out, rows, lanes, right[side]))

    prepare(0)
    permute(outer[1])
    pass_on(1)
    for side in (0, 1):
        apply_inner(side, [edge_rows[side]], keep(0))
    if steps > 1:
        send_ahead(0)
    for part in inner:
        a_loads[part].wait()
        permute(part)
    pass_on(2)
    for side in (0, 1):
        apply_inner(side, inner_blocks(side), keep(0))
    wait_both(functools.partial(rim_copy, 0))
    for side in (0, 1):
        rim[side] = rim_in[0, side].astype(F32)
    first_right = right_edges()
    step_edges(0, first_right)
    step_rest(0, first_right)

    def forward(k, carry):
        prepare(k)
        for side in (0, 1):
            apply_inner(side, [edge_rows[side]], keep(k))
        pl.when(k < steps - 1)(functools.partial(send_ahead, k))
        for side in (0, 1):
            apply_inner(side, inner_blocks(side), keep(k))

        @pl.when(k == 1)
        def _():
            arrange_later()
            wait_both(near_copy)

        wait_both(functools.partial(msg_copy, k - 1))
        far_rims(k - 1)
        right = right_edges()
        step_edges(k, right)
        step_rest(k, right)
        for j in range(3, min(bits, steps + 2)):
            pl.when(k == j - 2)(functools.partial(pass_on, j))
        return carry

    lax.fori_loop(1, steps, forward, 0)

    w_end = weight(steps)
    u = hist[steps]
    gf[...] = w_end * (u - goal[...]) + adj[...]

    for side, (rows, lanes) in enumerate(zip(edge_rows, edge_lanes)):
        v = transposed(rows, blocks, lanes)
        pulled[rows, lanes] = v
        rim_out[turn, side] = v.astype(BF16)
    start_both(functools.partial(rim_copy, turn))

    st_out[...] = hist[steps].astype(BF16)

    def st_copy(dst):
        return pltpu.make_async_remote_copy(
            src_ref=st_out, dst_ref=st_in, send_sem=st_sem.at[0], recv_sem=st_sem.at[1],
            device_id={"tm": dst}, device_id_type=pl.DeviceIdType.MESH)

    def back_copy(i, dst):
        src, land = ((rate_out, rate_in), (adj_out, adj_in), (face_out, face_in))[i]
        return pltpu.make_async_remote_copy(
            src_ref=src, dst_ref=land, send_sem=adj_sem.at[0, i], recv_sem=adj_sem.at[1, i],
            device_id={"tm": dst}, device_id_type=pl.DeviceIdType.MESH)

    def send_back(i):
        @pl.when(t > 0)
        def _():
            back_copy(i, t - 1).start()


    def gather_copy(slots, send, recv, axis, index, count, d):
        return pltpu.make_async_remote_copy(
            src_ref=slots.at[index], dst_ref=slots.at[index], send_sem=send.at[d], recv_sem=recv.at[index],
            device_id={axis: lax.rem(index + d, count)}, device_id_type=pl.DeviceIdType.MESH)

    def gather_wait(slots, send, recv, axis, index, count, d):
        gather_copy(slots, send, recv, axis, index, count, d).wait_send()
        origin = lax.rem(index + d, count)
        pltpu.make_async_remote_copy(
            src_ref=slots.at[origin], dst_ref=slots.at[origin], send_sem=send.at[d], recv_sem=recv.at[origin],
            device_id={axis: origin}, device_id_type=pl.DeviceIdType.MESH).wait_recv()

    over_s = (slot_s, ss_send, ss_recv, "space", me, n_space)

    over_t = (slot_t, tt_send, tt_recv, "tm", t, n_tm)

    def gathered(slots, *rest):
        count = rest[-1]
        for d in range(1, count):
            gather_wait(slots, *rest, d)
        total = slots[0]
        for i in range(1, count):
            total = total + slots[i]
        return total

    def hand_round():
        for j in range(max(3, min(bits, steps + 2)), bits + 1):
            pass_on(j)
        slot_t[t] = gathered(*over_s)
        for d in range(1, n_tm):
            gather_copy(*over_t, d).start()

    def rate(k):
        before = hist[k]
        return 1.0 + TIME_STEP * (1.0 - 3.0 * before * before)


    @pl.when(t < n_tm - 1)
    def _():
        st_copy(t + 1).start()

    rate_out[...] = rate(0).astype(BF16)
    send_back(0)

    for side, lanes in enumerate(edge_lanes):
        for out in inner_blocks(side):
            pulled[out, lanes] = transposed(out, blocks, lanes)

    total = jnp.zeros((8, 128), F32)
    for k in range(steps):
        d = hist[k + 1] - goal[...]
        c = ctl[k].astype(F32)
        total += 0.5 * weight(k + 1) * fold(d * d) + 0.5 * REGULAR * fold(c * c)
    slot_s[me] = total
    for d in range(1, n_space):
        gather_copy(*over_s, d).start()

    def carry_back(factor, p):
        return factor * p + TIME_STEP * PENALTY * jumps_inside(p)

    def update(k, p):
        control = ctl[k].astype(F32)
        ctl[k] = (control - (TIME_STEP * p + REGULAR * control)).astype(BF16)

    def backward(i, carry):
        k = steps - 1 - i
        rnd = steps - 1 + i
        p = pulled[...]
        gf[...] = weight(k) * (hist[k] - goal[...]) + carry_back(rate(k), p)
        held[...] = p
        for side, (rows, lanes) in enumerate(zip(edge_rows, edge_lanes)):
            pulled[rows, lanes] = transposed(rows, inner_blocks(side), lanes)

        @pl.when(i < steps - 2)
        def _():
            send_msg(rnd, lambda side: gf[edge_rows[side], edge_lanes[side]],
                     lambda side: pulled[edge_rows[side], edge_lanes[side]])

        for side, lanes in enumerate(edge_lanes):
            for out in inner_blocks(side):
                pulled[out, lanes] = transposed(out, inner_blocks(side), lanes)

        @pl.when(i == steps - 2)
        def _():
            adj_out[...] = carry_back(rate(0), pulled[...]).astype(BF16)
            send_back(1)

        @pl.when(i == 0)
        def _():
            wait_both(functools.partial(rim_copy, turn))
            for side in (0, 1):
                rim[side] = rim_in[turn, side].astype(F32)

        @pl.when(i > 0)
        def _():
            wait_both(functools.partial(msg_copy, rnd - 1))
            for side in (0, 1):
                far_g[side] = msg_in[rnd - 1, side, 0].astype(F32) + TIME_STEP * PENALTY * prev[side]
            for side in (0, 1):
                rim[side] = msg_in[rnd - 1, side, 1].astype(F32) + near_transposed(side)

        for side, (rows, lanes) in enumerate(zip(edge_rows, edge_lanes)):
            g = gf[rows, lanes] + TIME_STEP * PENALTY * rim[side]
            gf[rows, lanes] = g
            face_out[side] = g.astype(BF16)

        @pl.when(i == steps - 2)
        def _():
            send_back(2)

        for side, (rows, lanes) in enumerate(zip(edge_rows, edge_lanes)):
            pulled[rows, lanes] += transposed(rows, [rows], lanes)

        @pl.when(i == steps - 2)
        def _():
            for side, (rows, lanes) in enumerate(zip(edge_rows, edge_lanes)):
                rim_out[final, side] = pulled[rows, lanes].astype(BF16)

                @pl.when(at_side(side) & (t > 0))
                def _():
                    rim_copy(final, side, 1 - side).start()

        for side, (rows, lanes) in enumerate(zip(edge_rows, edge_lanes)):
            for out in inner_blocks(side):
                pulled[out, lanes] += transposed(out, [rows], lanes)
        for side, (rows, lanes) in enumerate(zip(edge_rows, edge_lanes)):
            prev[side] = held[rows, lanes]
        update(k, held[...])
        pl.when(i == min(1, steps - 2))(hand_round)
        return carry

    lax.fori_loop(0, steps - 1, backward, 0)

    update(0, pulled[...])
    for k in range(steps):
        newc_ref[k] = dot(ctl[k], pt[...]).astype(BF16)

    @pl.when(t == 0)
    def _():
        nst_ref[0] = st[...]

    @pl.when(t > 0)
    def _():
        st_copy(t - 1).wait_recv()
        nst_ref[0] = dot(st_in[...], pt[...])

    @pl.when(t < n_tm - 1)
    def _():
        st_copy(t + 1).wait_send()

    total = gathered(*over_t)
    scaled = total * (1.0 / (total_steps * nodes * elements * n_space))
    obj_ref[...] = jnp.sum(jnp.sum(scaled, axis=0, keepdims=True), axis=1, keepdims=True)

    @pl.when(t == n_tm - 1)
    def _():
        nadj_ref[...] = jnp.zeros_like(nadj_ref)

    @pl.when(t < n_tm - 1)
    def _():
        for i in (0, 2):
            back_copy(i, t + 1).wait_recv()
        for side, (rows, lanes) in enumerate(zip(edge_rows, edge_lanes)):
            gf[rows, lanes] = face_in[side].astype(F32)
        for side, (rows, lanes) in enumerate(zip(edge_rows, edge_lanes)):
            for out in blocks:
                pulled[out, lanes] = transposed(out, [rows], lanes)
        gf[...] = carry_back(rate_in[...].astype(F32), pulled[...])
        back_copy(1, t + 1).wait_recv()

    wait_final_rims()

    @pl.when(t < n_tm - 1)
    def _():
        for side, (rows, lanes) in enumerate(zip(edge_rows, edge_lanes)):
            gf[rows, lanes] += TIME_STEP * PENALTY * rim_in[final, side].astype(F32)
        nadj_ref[0] = joined(dot(split(gf[...] + adj_in[...].astype(F32)), pt[...]))

    @pl.when(t > 0)
    def _():
        for i in range(3):
            back_copy(i, t - 1).wait_send()


def store_kernel(count, *refs):
    gives = [pltpu.make_async_copy(refs[i], refs[count + i], refs[-1].at[i]) for i in range(count)]
    for c in gives:
        c.start()
    for c in gives:
        c.wait()


def store(values):
    count = len(values)
    return pl.pallas_call(
        functools.partial(store_kernel, count),
        out_shape=tuple(jax.ShapeDtypeStruct(v.shape, v.dtype) for v in values),
        in_specs=[pl.BlockSpec(memory_space=pltpu.VMEM)] * count,
        out_specs=(pl.BlockSpec(memory_space=pltpu.HBM),) * count,
        scratch_shapes=[pltpu.SemaphoreType.DMA((count,))],
        compiler_params=pltpu.CompilerParams(vmem_limit_bytes=4194304),
    )(*values)


def solution(mesh):
    n_space, n_tm = mesh.shape["space"], mesh.shape["tm"]

    def per_device(controls, target, state_in, adjoint_in, block_inverse, numbering):
        steps, nodes, elements = controls.shape
        vm = pl.BlockSpec(memory_space=pltpu.VMEM)
        hbm = pl.BlockSpec(memory_space=pltpu.HBM)
        field = (nodes, elements)
        messages = max(2 * steps - 3, 1)
        bits = (n_tm - 1).bit_length()
        dma = pltpu.SemaphoreType.DMA
        new_controls, next_state, next_adjoint, objective = pl.pallas_call(
            functools.partial(kernel, n_space, n_tm),
            out_shape=(
                pltpu.VMEM(controls.shape, BF16),
                pltpu.VMEM(state_in.shape, F32),
                pltpu.VMEM(adjoint_in.shape, F32),
                pltpu.VMEM((1, 1), F32),
            ),
            in_specs=[hbm] * 6,
            out_specs=(vm, vm, vm, vm),
            scratch_shapes=[
                pltpu.VMEM(block_inverse.shape, BF16),
                pltpu.VMEM(block_inverse.shape, BF16),
                pltpu.VMEM(numbering.shape, jnp.int32),
                pltpu.VMEM(controls.shape, BF16),
                pltpu.VMEM(controls.shape, BF16),
                pltpu.VMEM(field, BF16),
                pltpu.VMEM(field, F32),
                pltpu.VMEM(field, F32),
                pltpu.VMEM(field, F32),
                pltpu.VMEM(field, F32),
                pltpu.VMEM((steps + 1,) + field, F32),
                pltpu.VMEM(field, BF16),
                pltpu.VMEM((2, BLOCK, LAYER), F32),
                pltpu.VMEM(field, F32),
                pltpu.VMEM(field, F32),
                pltpu.VMEM((elements, elements), BF16),
                pltpu.VMEM((elements, elements), BF16),
                pltpu.VMEM((3, 2, BLOCK, LAYER), BF16),
                pltpu.VMEM((3, 2, BLOCK, LAYER), BF16),
                pltpu.VMEM((messages, 2, 2, BLOCK, LAYER), BF16),
                pltpu.VMEM((messages, 2, 2, BLOCK, LAYER), BF16),
                pltpu.VMEM((2, BLOCK, BLOCK, LAYER), BF16),
                pltpu.VMEM((2, BLOCK, BLOCK, LAYER), BF16),
                pltpu.VMEM((2, BLOCK, LAYER), F32),
                pltpu.VMEM((2, BLOCK, LAYER), F32),
                pltpu.VMEM((2, BLOCK, LAYER), F32),
                pltpu.VMEM(field, F32),
                pltpu.VMEM(field, BF16),
                pltpu.VMEM(field, BF16),
                pltpu.VMEM(field, BF16),
                pltpu.VMEM(field, BF16),
                pltpu.VMEM(field, BF16),
                pltpu.VMEM(field, BF16),
                pltpu.VMEM((2, BLOCK, LAYER), BF16),
                pltpu.VMEM((2, BLOCK, LAYER), BF16),
                pltpu.VMEM((n_space, 8, 128), F32),
                pltpu.VMEM((n_tm, 8, 128), F32),
                dma((5,)),
                dma((4,)),
                dma((3, 2)),
                dma((3, 2)),
                dma((messages, 2)),
                dma((messages, 2)),
                dma((2,)),
                dma((2,)),
                dma((2,)),
                dma((2, 3)),
                dma((n_space,)),
                dma((n_space,)),
                dma((n_tm,)),
                dma((n_tm,)),
                pltpu.SemaphoreType.REGULAR((bits,)),
            ],
            compiler_params=pltpu.CompilerParams(
                collective_id=0, has_side_effects=True, vmem_limit_bytes=60000000
            ),
        )(numbering, controls, target, state_in, adjoint_in, block_inverse)
        out = store((new_controls, next_state, next_adjoint, objective))
        return out[:3] + (out[3].reshape(()),)

    return jax.shard_map(
        per_device,
        mesh=mesh,
        in_specs=(
            P("tm", None, "space"),
            P(None, "space"),
            P("tm", None, "space"),
            P("tm", None, "space"),
            P(None, None, "space"),
            P("space", None),
        ),
        out_specs=(P("tm", None, "space"), P("tm", None, "space"), P("tm", None, "space"), P()),
        check_vma=False,
    )
```

```python
import functools

import jax
import jax.numpy as jnp
from jax import lax
from jax.experimental import pallas as pl
from jax.experimental.pallas import tpu as pltpu
from jax.sharding import PartitionSpec as P

NSIDE = 4
EXY = 16
BLOCK = NSIDE * NSIDE
LAYER = EXY * EXY
TIME_STEP = 0.1
PENALTY = 0.5
REGULAR = 0.1
F32 = jnp.float32
BF16 = jnp.bfloat16


def dot(a, b):
    return jnp.dot(a, b, preferred_element_type=F32)


def fold(x):
    total = None
    for i in range(0, x.shape[0], 8):
        for j in range(0, x.shape[1], 128):
            piece = x[i : i + 8, j : j + 128]
            total = piece if total is None else total + piece
    return total


def lateral(x):
    nodes, elements = x.shape
    last = NSIDE - 1

    def by_layer(y, shift):
        return jnp.concatenate(
            [pltpu.roll(y[:, i : i + LAYER], shift, 1) for i in range(0, elements, LAYER)], axis=1
        )

    a = lax.broadcasted_iota(jnp.int32, x.shape, 0) % NSIDE
    y = jnp.where(a == last, by_layer(x, EXY), by_layer(x, LAYER - EXY)).reshape(nodes // 8, 8, elements)
    to_low = pltpu.roll(y, 8 - last, 1).reshape(nodes, elements)
    to_high = pltpu.roll(y, last, 1).reshape(nodes, elements)
    along_a = jnp.where(a == 0, to_low, jnp.where(a == last, to_high, 0.0))

    count = nodes // BLOCK
    tall = x.reshape(count, 2, 8, elements)
    low3 = lax.broadcasted_iota(jnp.int32, (count, 8, elements), 1) < NSIDE
    w = jnp.where(low3, tall[:, 0], tall[:, 1]).reshape(count * 8, elements)
    low2 = lax.broadcasted_iota(jnp.int32, w.shape, 0) % 8 < NSIDE
    row = lax.broadcasted_iota(jnp.int32, w.shape, 1) % EXY
    down = jnp.where(row == 0, pltpu.roll(w, elements - EXY + 1, 1), pltpu.roll(w, 1, 1))
    up = jnp.where(row == EXY - 1, pltpu.roll(w, EXY - 1, 1), pltpu.roll(w, elements - 1, 1))
    r = pltpu.roll(jnp.where(low2, up, down).reshape(count, 8, elements), NSIDE, 1)
    first, second = jnp.where(low3, r, 0.0), jnp.where(low3, 0.0, r)
    along_b = jnp.concatenate([v for i in range(count) for v in (first[i], second[i])], axis=0)
    return along_a + along_b


def face_count(shape):
    q = lax.broadcasted_iota(jnp.int32, shape, 0)
    count = jnp.zeros(shape, F32)
    for step in (1, NSIDE, BLOCK):
        at = (q // step) % NSIDE
        count += jnp.where((at == 0) | (at == NSIDE - 1), 1.0, 0.0)
    return count


def jumps_inside(x):
    nodes, elements = x.shape
    low, high = slice(0, BLOCK), slice(nodes - BLOCK, nodes)
    empty = jnp.zeros((BLOCK, LAYER), F32)
    below = jnp.concatenate([empty, x[high, : elements - LAYER]], axis=1)
    above = jnp.concatenate([x[low, LAYER:], empty], axis=1)
    middle = jnp.zeros((nodes - 2 * BLOCK, elements), F32)
    return lateral(x) + jnp.concatenate([below, middle, above], axis=0) - face_count(x.shape) * x


def kernel(
    n_space, n_tm,
    num_hbm, ctl_hbm, tgt_hbm, st_hbm, adj_hbm, a_hbm,
    newc_ref, nst_ref, nadj_ref, obj_ref,
    a_raw, a_ref, num, ctl_raw, ctl, tgt_raw, goal, adj_raw, adj, st, hist, r_ref, edge, gf, pulled, pa, pt,
    rim_out, rim_in, msg_out, msg_in, near_out, near_in, rim, prev, far_g, held, st_out, st_in, adj_out, adj_in, rate_out, rate_in, face_out, face_in, slot_s, slot_t,
    in_sem, a_sem, rim_send, rim_recv, msg_send, msg_recv, near_send, near_recv, st_sem, adj_sem,
    ss_send, ss_recv, tt_send, tt_recv, ready,
):
    steps, nodes, elements = ctl.shape
    me = lax.axis_index("space")
    t = lax.axis_index("tm")
    first = t * steps
    total_steps = steps * n_tm
    turn, final = 1, 2
    last_block = nodes - BLOCK
    blocks = [slice(s, s + BLOCK) for s in range(0, nodes, BLOCK)]
    edge_rows = (slice(0, BLOCK), slice(last_block, nodes))
    edge_lanes = (slice(0, LAYER), slice(elements - LAYER, elements))

    def weight(k):
        return lax.convert_element_type(first + k, F32) / total_steps

    loads = [
        pltpu.make_async_copy(src, dst, in_sem.at[i])
        for i, (src, dst) in enumerate(
            ((num_hbm, num), (st_hbm.at[0], st), (tgt_hbm, tgt_raw), (ctl_hbm, ctl_raw), (adj_hbm.at[0], adj_raw))
        )
    ]
    for c in loads[:2]:
        c.start()
    for landing in (rim_in, msg_in, near_in):
        landing[...] = jnp.zeros_like(landing)
    barrier = pltpu.get_barrier_semaphore()
    for d in range(1, n_space):
        pl.semaphore_signal(barrier, inc=1, device_id={"space": lax.rem(me + d, n_space)},
                            device_id_type=pl.DeviceIdType.MESH)
    bits = (n_tm - 1).bit_length()

    def beside(far):
        return jnp.where(t >= far, 1, 0) + jnp.where(t + far < n_tm, 1, 0)

    def greet(sem, far):
        @pl.when(t >= far)
        def _():
            pl.semaphore_signal(sem, inc=1, device_id={"tm": t - far}, device_id_type=pl.DeviceIdType.MESH)

        @pl.when(t + far < n_tm)
        def _():
            pl.semaphore_signal(sem, inc=1, device_id={"tm": t + far}, device_id_type=pl.DeviceIdType.MESH)

    greet(barrier, 1)

    def tell(j):
        if j <= bits:
            greet(ready.at[j - 1], 2 ** (j - 1))

    def hear(j):
        if j <= bits:
            pl.semaphore_wait(ready.at[j - 1], beside(2 ** (j - 1)))

    def pass_on(j):
        hear(j)
        tell(j + 1)

    parts = a_sem.shape[0]
    chunk = nodes // parts
    a_loads = [
        pltpu.make_async_copy(a_hbm.at[pl.ds(i * chunk, chunk)], a_raw.at[pl.ds(i * chunk, chunk)], a_sem.at[i])
        for i in range(parts)
    ]
    outer = [0, parts - 1]
    inner = list(range(1, parts - 1))
    for i in outer + inner:
        a_loads[i].start()
    for c in loads[2:]:
        c.start()

    loads[0].wait()
    stored = num[...]
    own = stored // LAYER * LAYER + stored % EXY * EXY + stored // EXY % EXY
    for i in range(0, elements, LAYER):
        place = lax.broadcasted_iota(jnp.int32, (LAYER, elements), 0) + i
        pt[i : i + LAYER, :] = jnp.where(own == place, 1.0, 0.0).astype(BF16)
    down = jnp.broadcast_to(own.astype(F32), (128, elements)).T
    for i in range(0, elements, 128):
        place = lax.broadcasted_iota(jnp.int32, (elements, 128), 1) + i
        pa[:, i : i + 128] = jnp.where(down == place.astype(F32), 1.0, 0.0).astype(BF16)

    def split(x):
        high = x.astype(BF16)
        return jnp.concatenate([high, (x - high.astype(F32)).astype(BF16)], axis=0)

    def joined(x):
        return x[:nodes] + x[nodes:]

    def across(src, dst, send, recv, side, back=0):
        return pltpu.make_async_remote_copy(
            src_ref=src, dst_ref=dst, send_sem=send, recv_sem=recv,
            device_id={"tm": t - back, "space": me - 1 if side == 0 else me + 1},
            device_id_type=pl.DeviceIdType.MESH,
        )

    def rim_copy(rnd, side, slot):
        return across(rim_out.at[rnd, side], rim_in.at[rnd, slot], rim_send.at[rnd, side], rim_recv.at[rnd, slot],
                      side, 1 if rnd == final else 0)

    def msg_copy(rnd, side, slot):
        return across(msg_out.at[rnd, side], msg_in.at[rnd, slot], msg_send.at[rnd, side], msg_recv.at[rnd, slot], side)

    def near_copy(side, slot):
        return across(near_out.at[side], near_in.at[slot], near_send.at[side], near_recv.at[slot], side)

    def at_side(side):
        return me > 0 if side == 0 else me < n_space - 1

    def start_both(copy):
        for side in (0, 1):
            @pl.when(at_side(side))
            def _():
                copy(side, 1 - side).start()

    def wait_both(copy):
        for side in (0, 1):
            @pl.when(at_side(side))
            def _():
                copy(side, side).wait()

    def send_msg(rnd, base, ahead):
        for side in (0, 1):
            msg_out[rnd, side, 0] = base(side).astype(BF16)
            msg_out[rnd, side, 1] = ahead(side).astype(BF16)
        start_both(functools.partial(msg_copy, rnd))

    def wait_final_rims():
        for side in (0, 1):
            @pl.when(at_side(side) & (t < n_tm - 1))
            def _():
                rim_copy(final, side, side).wait_recv()

            @pl.when(at_side(side) & (t > 0))
            def _():
                rim_copy(final, side, side).wait_send()

    depth = BLOCK * BLOCK
    place_k = lax.broadcasted_iota(jnp.int32, (BLOCK, depth), 1)
    place_r = lax.broadcasted_iota(jnp.int32, (BLOCK, depth), 0)
    sum_rows = jnp.where(place_k // BLOCK == place_r, 1.0, 0.0).astype(BF16)
    sum_groups = jnp.where(place_k % BLOCK == place_r, 1.0, 0.0).astype(BF16)
    sum_rows2 = jnp.concatenate([sum_rows, sum_rows], axis=1)

    def groups(n):
        place_c = lax.broadcasted_iota(jnp.int32, (BLOCK, n), 1) % BLOCK
        return jnp.where(place_c == lax.broadcasted_iota(jnp.int32, (BLOCK, n), 0), 1.0, 0.0).astype(BF16)

    def product(out, into, lanes, right):
        return (a_ref[out, into, lanes] * right[None]).reshape(depth, LAYER)

    def product_pair(out, into, lanes, right):
        (i0, i1), (r0, r1) = into, right
        return (a_ref[out, i0, lanes] * r0[None] + a_ref[out, i1, lanes] * r1[None]).reshape(depth, LAYER)

    def inner_blocks(side):
        return [b for b in blocks if b != edge_rows[side]]

    def apply_inner(side, outs, write):
        lanes = edge_lanes[side]
        b0, b1, b2 = inner_blocks(side)
        if side == 0:
            pair, single = (b0, b1), b2
        else:
            pair, single = (b1, b2), b0
        rp = (r_ref[pair[0], lanes], r_ref[pair[1], lanes])
        rs = r_ref[single, lanes]
        for out in outs:
            q = jnp.concatenate([product_pair(out, pair, lanes, rp), product(out, single, lanes, rs)], axis=0)
            write(out, lanes, dot(sum_rows2, q))

    def transposed(out, into, lanes):
        rows = [i for b in into for i in range(b.start, b.stop)]

        def term(i):
            row = jnp.broadcast_to(gf[i : i + 1, lanes], (BLOCK, LAYER)).astype(BF16)
            return a_ref[i, out, lanes] * row

        pieces = [term(rows[i]) + term(rows[i + 1]) for i in range(0, len(rows), 2)]
        return dot(groups(BLOCK * len(pieces)), jnp.concatenate(pieces, axis=0))

    def near_transposed(side):
        def term(i):
            row = jnp.broadcast_to(far_g[side, i : i + 1], (BLOCK, LAYER)).astype(BF16)
            return near_in[side, i] * row

        pieces = [term(i) + term(i + 1) for i in range(0, BLOCK, 2)]
        return dot(groups(BLOCK * len(pieces)), jnp.concatenate(pieces, axis=0))

    loads[1].wait()
    hist[0] = joined(dot(split(st[...]), pa[...]))
    for side in (0, 1):
        rim_out[0, side] = hist[0, edge_rows[side], edge_lanes[side]].astype(BF16)
    piece = depth // nodes

    def permute(part):
        for i in range(part * chunk, (part + 1) * chunk, piece):
            rows = a_raw[i : i + piece].reshape(depth, elements)
            a_ref[i : i + piece] = dot(rows, pa[...]).astype(BF16).reshape(piece, nodes, elements)

    a_loads[outer[0]].wait()
    permute(outer[0])
    pl.semaphore_wait(barrier, n_space - 1 + beside(1))
    start_both(functools.partial(rim_copy, 0))
    tell(1)
    near_out[0] = a_ref[edge_rows[0], edge_rows[0], edge_lanes[0]]
    a_loads[outer[1]].wait()
    corner = dot(a_raw[edge_rows[1], edge_rows[1]].reshape(depth, elements), pa[:, edge_lanes[1]])
    near_out[1] = corner.astype(BF16).reshape(BLOCK, BLOCK, LAYER)
    start_both(near_copy)

    loads[3].wait()
    for k in range(min(2, steps)):
        ctl[k] = dot(ctl_raw[k], pa[...]).astype(BF16)

    def arrange_later():
        for c in (loads[2], loads[4]):
            c.wait()
        goal[...] = dot(tgt_raw[...], pa[...])
        adj[...] = joined(dot(split(adj_raw[...]), pa[...]))
        for k in range(2, steps):
            ctl[k] = dot(ctl_raw[k], pa[...]).astype(BF16)

    def prepare(k):
        u = hist[k]
        c = ctl[k].astype(F32)
        base = u + TIME_STEP * (u - u * u * u) + TIME_STEP * PENALTY * jumps_inside(u) + TIME_STEP * c
        r_ref[...] = base.astype(BF16)
        for side in (0, 1):
            edge[side] = base[edge_rows[side], edge_lanes[side]]

    def keep(k):
        def write(rows, lanes, v):
            hist[k + 1, rows, lanes] = v

        return write

    def right_edges():
        return [(edge[side] + TIME_STEP * PENALTY * rim[side]).astype(BF16) for side in (0, 1)]

    def step_edges(k, right):
        for side, (rows, lanes) in enumerate(zip(edge_rows, edge_lanes)):
            hist[k + 1, rows, lanes] += dot(sum_rows, product(rows, rows, lanes, right[side]))

    def send_ahead(k):
        send_msg(k, lambda side: edge[side], lambda side: hist[k + 1, edge_rows[side], edge_lanes[side]])

    def far_rims(k):
        for side, (rows, lanes) in enumerate(zip(edge_rows, edge_lanes)):
            far = msg_in[k, side, 0].astype(F32) + TIME_STEP * PENALTY * hist[k, rows, lanes]
            q = (near_in[side] * far.astype(BF16)[None]).reshape(depth, LAYER)
            rim[side] = msg_in[k, side, 1].astype(F32) + dot(sum_rows, q)

    def step_rest(k, right):
        for side, (rows, lanes) in enumerate(zip(edge_rows, edge_lanes)):
            for out in inner_blocks(side):
                hist[k + 1, out, lanes] += dot(sum_rows, product(out, rows, lanes, right[side]))

    prepare(0)
    permute(outer[1])
    for side in (0, 1):
        apply_inner(side, [edge_rows[side]], keep(0))
    if steps > 1:
        send_ahead(0)
    for part in inner:
        a_loads[part].wait()
        permute(part)
    for side in (0, 1):
        apply_inner(side, inner_blocks(side), keep(0))
    wait_both(functools.partial(rim_copy, 0))
    for side in (0, 1):
        rim[side] = rim_in[0, side].astype(F32)
    first_right = right_edges()
    step_edges(0, first_right)
    step_rest(0, first_right)

    def forward(k, carry):
        prepare(k)
        for side in (0, 1):
            apply_inner(side, [edge_rows[side]], keep(k))
        pl.when(k < steps - 1)(functools.partial(send_ahead, k))
        for side in (0, 1):
            apply_inner(side, inner_blocks(side), keep(k))

        @pl.when(k == 1)
        def _():
            arrange_later()
            wait_both(near_copy)

        wait_both(functools.partial(msg_copy, k - 1))
        far_rims(k - 1)
        right = right_edges()
        step_edges(k, right)
        step_rest(k, right)
        pl.when(k == 1)(functools.partial(pass_on, 1))
        pl.when(k == steps - 1)(functools.partial(pass_on, 2))
        return carry

    lax.fori_loop(1, steps, forward, 0)

    w_end = weight(steps)
    u = hist[steps]
    gf[...] = w_end * (u - goal[...]) + adj[...]

    for side, (rows, lanes) in enumerate(zip(edge_rows, edge_lanes)):
        v = transposed(rows, blocks, lanes)
        pulled[rows, lanes] = v
        rim_out[turn, side] = v.astype(BF16)
    start_both(functools.partial(rim_copy, turn))

    st_out[...] = hist[steps].astype(BF16)

    def st_copy(dst):
        return pltpu.make_async_remote_copy(
            src_ref=st_out, dst_ref=st_in, send_sem=st_sem.at[0], recv_sem=st_sem.at[1],
            device_id={"tm": dst}, device_id_type=pl.DeviceIdType.MESH)

    def back_copy(i, dst):
        src, land = ((rate_out, rate_in), (adj_out, adj_in), (face_out, face_in))[i]
        return pltpu.make_async_remote_copy(
            src_ref=src, dst_ref=land, send_sem=adj_sem.at[0, i], recv_sem=adj_sem.at[1, i],
            device_id={"tm": dst}, device_id_type=pl.DeviceIdType.MESH)

    def send_back(i):
        @pl.when(t > 0)
        def _():
            back_copy(i, t - 1).start()


    def gather_copy(slots, send, recv, axis, index, count, d):
        return pltpu.make_async_remote_copy(
            src_ref=slots.at[index], dst_ref=slots.at[index], send_sem=send.at[d], recv_sem=recv.at[index],
            device_id={axis: lax.rem(index + d, count)}, device_id_type=pl.DeviceIdType.MESH)

    def gather_wait(slots, send, recv, axis, index, count, d):
        gather_copy(slots, send, recv, axis, index, count, d).wait_send()
        origin = lax.rem(index + d, count)
        pltpu.make_async_remote_copy(
            src_ref=slots.at[origin], dst_ref=slots.at[origin], send_sem=send.at[d], recv_sem=recv.at[origin],
            device_id={axis: origin}, device_id_type=pl.DeviceIdType.MESH).wait_recv()

    over_s = (slot_s, ss_send, ss_recv, "space", me, n_space)

    over_t = (slot_t, tt_send, tt_recv, "tm", t, n_tm)

    def gathered(slots, *rest):
        count = rest[-1]
        for d in range(1, count):
            gather_wait(slots, *rest, d)
        total = slots[0]
        for i in range(1, count):
            total = total + slots[i]
        return total

    def hand_round():
        for j in range(3, bits + 1):
            pass_on(j)
        slot_t[t] = gathered(*over_s)
        for d in range(1, n_tm):
            gather_copy(*over_t, d).start()

    def rate(k):
        before = hist[k]
        return 1.0 + TIME_STEP * (1.0 - 3.0 * before * before)


    @pl.when(t < n_tm - 1)
    def _():
        st_copy(t + 1).start()

    rate_out[...] = rate(0).astype(BF16)
    send_back(0)

    for side, lanes in enumerate(edge_lanes):
        for out in inner_blocks(side):
            pulled[out, lanes] = transposed(out, blocks, lanes)

    total = jnp.zeros((8, 128), F32)
    for k in range(steps):
        d = hist[k + 1] - goal[...]
        c = ctl[k].astype(F32)
        total += 0.5 * weight(k + 1) * fold(d * d) + 0.5 * REGULAR * fold(c * c)
    slot_s[me] = total
    for d in range(1, n_space):
        gather_copy(*over_s, d).start()

    def carry_back(factor, p):
        return factor * p + TIME_STEP * PENALTY * jumps_inside(p)

    def update(k, p):
        control = ctl[k].astype(F32)
        ctl[k] = (control - (TIME_STEP * p + REGULAR * control)).astype(BF16)

    def backward(i, carry):
        k = steps - 1 - i
        rnd = steps - 1 + i
        p = pulled[...]
        gf[...] = weight(k) * (hist[k] - goal[...]) + carry_back(rate(k), p)
        held[...] = p
        for side, (rows, lanes) in enumerate(zip(edge_rows, edge_lanes)):
            pulled[rows, lanes] = transposed(rows, inner_blocks(side), lanes)

        @pl.when(i < steps - 2)
        def _():
            send_msg(rnd, lambda side: gf[edge_rows[side], edge_lanes[side]],
                     lambda side: pulled[edge_rows[side], edge_lanes[side]])

        for side, lanes in enumerate(edge_lanes):
            for out in inner_blocks(side):
                pulled[out, lanes] = transposed(out, inner_blocks(side), lanes)

        @pl.when(i == steps - 2)
        def _():
            adj_out[...] = carry_back(rate(0), pulled[...]).astype(BF16)
            send_back(1)

        @pl.when(i == 0)
        def _():
            wait_both(functools.partial(rim_copy, turn))
            for side in (0, 1):
                rim[side] = rim_in[turn, side].astype(F32)

        @pl.when(i > 0)
        def _():
            wait_both(functools.partial(msg_copy, rnd - 1))
            for side in (0, 1):
                far_g[side] = msg_in[rnd - 1, side, 0].astype(F32) + TIME_STEP * PENALTY * prev[side]
            for side in (0, 1):
                rim[side] = msg_in[rnd - 1, side, 1].astype(F32) + near_transposed(side)

        for side, (rows, lanes) in enumerate(zip(edge_rows, edge_lanes)):
            g = gf[rows, lanes] + TIME_STEP * PENALTY * rim[side]
            gf[rows, lanes] = g
            face_out[side] = g.astype(BF16)

        @pl.when(i == steps - 2)
        def _():
            send_back(2)

        for side, (rows, lanes) in enumerate(zip(edge_rows, edge_lanes)):
            pulled[rows, lanes] += transposed(rows, [rows], lanes)

        @pl.when(i == steps - 2)
        def _():
            for side, (rows, lanes) in enumerate(zip(edge_rows, edge_lanes)):
                rim_out[final, side] = pulled[rows, lanes].astype(BF16)

                @pl.when(at_side(side) & (t > 0))
                def _():
                    rim_copy(final, side, 1 - side).start()

        for side, (rows, lanes) in enumerate(zip(edge_rows, edge_lanes)):
            for out in inner_blocks(side):
                pulled[out, lanes] += transposed(out, [rows], lanes)
        for side, (rows, lanes) in enumerate(zip(edge_rows, edge_lanes)):
            prev[side] = held[rows, lanes]
        update(k, held[...])
        pl.when(i == min(1, steps - 2))(hand_round)
        return carry

    lax.fori_loop(0, steps - 1, backward, 0)

    update(0, pulled[...])
    for k in range(steps):
        newc_ref[k] = dot(ctl[k], pt[...]).astype(BF16)

    @pl.when(t == 0)
    def _():
        nst_ref[0] = st[...]

    @pl.when(t > 0)
    def _():
        st_copy(t - 1).wait_recv()
        nst_ref[0] = dot(st_in[...], pt[...])

    @pl.when(t < n_tm - 1)
    def _():
        st_copy(t + 1).wait_send()

    total = gathered(*over_t)
    scaled = total * (1.0 / (total_steps * nodes * elements * n_space))
    obj_ref[...] = jnp.sum(jnp.sum(scaled, axis=0, keepdims=True), axis=1, keepdims=True)

    @pl.when(t == n_tm - 1)
    def _():
        nadj_ref[...] = jnp.zeros_like(nadj_ref)

    @pl.when(t < n_tm - 1)
    def _():
        for i in (0, 2):
            back_copy(i, t + 1).wait_recv()
        for side, (rows, lanes) in enumerate(zip(edge_rows, edge_lanes)):
            gf[rows, lanes] = face_in[side].astype(F32)
        for side, (rows, lanes) in enumerate(zip(edge_rows, edge_lanes)):
            for out in blocks:
                pulled[out, lanes] = transposed(out, [rows], lanes)
        gf[...] = carry_back(rate_in[...].astype(F32), pulled[...])
        back_copy(1, t + 1).wait_recv()

    wait_final_rims()

    @pl.when(t < n_tm - 1)
    def _():
        for side, (rows, lanes) in enumerate(zip(edge_rows, edge_lanes)):
            gf[rows, lanes] += TIME_STEP * PENALTY * rim_in[final, side].astype(F32)
        nadj_ref[0] = joined(dot(split(gf[...] + adj_in[...].astype(F32)), pt[...]))

    @pl.when(t > 0)
    def _():
        for i in range(3):
            back_copy(i, t - 1).wait_send()


def store_kernel(count, *refs):
    gives = [pltpu.make_async_copy(refs[i], refs[count + i], refs[-1].at[i]) for i in range(count)]
    for c in gives:
        c.start()
    for c in gives:
        c.wait()


def store(values):
    count = len(values)
    return pl.pallas_call(
        functools.partial(store_kernel, count),
        out_shape=tuple(jax.ShapeDtypeStruct(v.shape, v.dtype) for v in values),
        in_specs=[pl.BlockSpec(memory_space=pltpu.VMEM)] * count,
        out_specs=(pl.BlockSpec(memory_space=pltpu.HBM),) * count,
        scratch_shapes=[pltpu.SemaphoreType.DMA((count,))],
        compiler_params=pltpu.CompilerParams(vmem_limit_bytes=4194304),
    )(*values)


def solution(mesh):
    n_space, n_tm = mesh.shape["space"], mesh.shape["tm"]

    def per_device(controls, target, state_in, adjoint_in, block_inverse, numbering):
        steps, nodes, elements = controls.shape
        vm = pl.BlockSpec(memory_space=pltpu.VMEM)
        hbm = pl.BlockSpec(memory_space=pltpu.HBM)
        field = (nodes, elements)
        messages = max(2 * steps - 3, 1)
        bits = (n_tm - 1).bit_length()
        dma = pltpu.SemaphoreType.DMA
        new_controls, next_state, next_adjoint, objective = pl.pallas_call(
            functools.partial(kernel, n_space, n_tm),
            out_shape=(
                pltpu.VMEM(controls.shape, BF16),
                pltpu.VMEM(state_in.shape, F32),
                pltpu.VMEM(adjoint_in.shape, F32),
                pltpu.VMEM((1, 1), F32),
            ),
            in_specs=[hbm] * 6,
            out_specs=(vm, vm, vm, vm),
            scratch_shapes=[
                pltpu.VMEM(block_inverse.shape, BF16),
                pltpu.VMEM(block_inverse.shape, BF16),
                pltpu.VMEM(numbering.shape, jnp.int32),
                pltpu.VMEM(controls.shape, BF16),
                pltpu.VMEM(controls.shape, BF16),
                pltpu.VMEM(field, BF16),
                pltpu.VMEM(field, F32),
                pltpu.VMEM(field, F32),
                pltpu.VMEM(field, F32),
                pltpu.VMEM(field, F32),
                pltpu.VMEM((steps + 1,) + field, F32),
                pltpu.VMEM(field, BF16),
                pltpu.VMEM((2, BLOCK, LAYER), F32),
                pltpu.VMEM(field, F32),
                pltpu.VMEM(field, F32),
                pltpu.VMEM((elements, elements), BF16),
                pltpu.VMEM((elements, elements), BF16),
                pltpu.VMEM((3, 2, BLOCK, LAYER), BF16),
                pltpu.VMEM((3, 2, BLOCK, LAYER), BF16),
                pltpu.VMEM((messages, 2, 2, BLOCK, LAYER), BF16),
                pltpu.VMEM((messages, 2, 2, BLOCK, LAYER), BF16),
                pltpu.VMEM((2, BLOCK, BLOCK, LAYER), BF16),
                pltpu.VMEM((2, BLOCK, BLOCK, LAYER), BF16),
                pltpu.VMEM((2, BLOCK, LAYER), F32),
                pltpu.VMEM((2, BLOCK, LAYER), F32),
                pltpu.VMEM((2, BLOCK, LAYER), F32),
                pltpu.VMEM(field, F32),
                pltpu.VMEM(field, BF16),
                pltpu.VMEM(field, BF16),
                pltpu.VMEM(field, BF16),
                pltpu.VMEM(field, BF16),
                pltpu.VMEM(field, BF16),
                pltpu.VMEM(field, BF16),
                pltpu.VMEM((2, BLOCK, LAYER), BF16),
                pltpu.VMEM((2, BLOCK, LAYER), BF16),
                pltpu.VMEM((n_space, 8, 128), F32),
                pltpu.VMEM((n_tm, 8, 128), F32),
                dma((5,)),
                dma((4,)),
                dma((3, 2)),
                dma((3, 2)),
                dma((messages, 2)),
                dma((messages, 2)),
                dma((2,)),
                dma((2,)),
                dma((2,)),
                dma((2, 3)),
                dma((n_space,)),
                dma((n_space,)),
                dma((n_tm,)),
                dma((n_tm,)),
                pltpu.SemaphoreType.REGULAR((bits,)),
            ],
            compiler_params=pltpu.CompilerParams(
                collective_id=0, has_side_effects=True, vmem_limit_bytes=60000000
            ),
        )(numbering, controls, target, state_in, adjoint_in, block_inverse)
        out = store((new_controls, next_state, next_adjoint, objective))
        return out[:3] + (out[3].reshape(()),)

    return jax.shard_map(
        per_device,
        mesh=mesh,
        in_specs=(
            P("tm", None, "space"),
            P(None, "space"),
            P("tm", None, "space"),
            P("tm", None, "space"),
            P(None, None, "space"),
            P("space", None),
        ),
        out_specs=(P("tm", None, "space"), P("tm", None, "space"), P("tm", None, "space"), P()),
        check_vma=False,
    )
```

```python
import functools

import jax
import jax.numpy as jnp
from jax import lax
from jax.experimental import pallas as pl
from jax.experimental.pallas import tpu as pltpu
from jax.sharding import PartitionSpec as P

NSIDE = 4
EXY = 16
BLOCK = NSIDE * NSIDE
LAYER = EXY * EXY
TIME_STEP = 0.1
PENALTY = 0.5
REGULAR = 0.1
F32 = jnp.float32
BF16 = jnp.bfloat16


def dot(a, b):
    return jnp.dot(a, b, preferred_element_type=F32)


def fold(x):
    total = None
    for i in range(0, x.shape[0], 8):
        for j in range(0, x.shape[1], 128):
            piece = x[i : i + 8, j : j + 128]
            total = piece if total is None else total + piece
    return total


def lateral(x):
    nodes, elements = x.shape
    last = NSIDE - 1

    def by_layer(y, shift):
        return jnp.concatenate(
            [pltpu.roll(y[:, i : i + LAYER], shift, 1) for i in range(0, elements, LAYER)], axis=1
        )

    a = lax.broadcasted_iota(jnp.int32, x.shape, 0) % NSIDE
    y = jnp.where(a == last, by_layer(x, EXY), by_layer(x, LAYER - EXY)).reshape(nodes // 8, 8, elements)
    to_low = pltpu.roll(y, 8 - last, 1).reshape(nodes, elements)
    to_high = pltpu.roll(y, last, 1).reshape(nodes, elements)
    along_a = jnp.where(a == 0, to_low, jnp.where(a == last, to_high, 0.0))

    count = nodes // BLOCK
    tall = x.reshape(count, 2, 8, elements)
    low3 = lax.broadcasted_iota(jnp.int32, (count, 8, elements), 1) < NSIDE
    w = jnp.where(low3, tall[:, 0], tall[:, 1]).reshape(count * 8, elements)
    low2 = lax.broadcasted_iota(jnp.int32, w.shape, 0) % 8 < NSIDE
    row = lax.broadcasted_iota(jnp.int32, w.shape, 1) % EXY
    down = jnp.where(row == 0, pltpu.roll(w, elements - EXY + 1, 1), pltpu.roll(w, 1, 1))
    up = jnp.where(row == EXY - 1, pltpu.roll(w, EXY - 1, 1), pltpu.roll(w, elements - 1, 1))
    r = pltpu.roll(jnp.where(low2, up, down).reshape(count, 8, elements), NSIDE, 1)
    first, second = jnp.where(low3, r, 0.0), jnp.where(low3, 0.0, r)
    along_b = jnp.concatenate([v for i in range(count) for v in (first[i], second[i])], axis=0)
    return along_a + along_b


def face_count(shape):
    q = lax.broadcasted_iota(jnp.int32, shape, 0)
    count = jnp.zeros(shape, F32)
    for step in (1, NSIDE, BLOCK):
        at = (q // step) % NSIDE
        count += jnp.where((at == 0) | (at == NSIDE - 1), 1.0, 0.0)
    return count


def jumps_inside(x):
    nodes, elements = x.shape
    low, high = slice(0, BLOCK), slice(nodes - BLOCK, nodes)
    empty = jnp.zeros((BLOCK, LAYER), F32)
    below = jnp.concatenate([empty, x[high, : elements - LAYER]], axis=1)
    above = jnp.concatenate([x[low, LAYER:], empty], axis=1)
    middle = jnp.zeros((nodes - 2 * BLOCK, elements), F32)
    return lateral(x) + jnp.concatenate([below, middle, above], axis=0) - face_count(x.shape) * x


def kernel(
    n_space, n_tm,
    num_hbm, ctl_hbm, tgt_hbm, st_hbm, adj_hbm, a_hbm,
    newc_ref, nst_ref, nadj_ref, obj_ref,
    a_raw, a_ref, num, ctl_raw, ctl, tgt_raw, goal, adj_raw, adj, st, hist, r_ref, edge, gf, pulled, pa, pt,
    rim_out, rim_in, msg_out, msg_in, near_out, near_in, rim, prev, far_g, held, st_out, st_in, adj_out, adj_in, rate_out, rate_in, face_out, face_in, slot_s, slot_t,
    in_sem, a_sem, rim_send, rim_recv, msg_send, msg_recv, near_send, near_recv, st_sem, adj_sem,
    ss_send, ss_recv, tt_send, tt_recv, ready,
):
    steps, nodes, elements = ctl.shape
    me = lax.axis_index("space")
    t = lax.axis_index("tm")
    first = t * steps
    total_steps = steps * n_tm
    turn, final = 1, 2
    last_block = nodes - BLOCK
    blocks = [slice(s, s + BLOCK) for s in range(0, nodes, BLOCK)]
    edge_rows = (slice(0, BLOCK), slice(last_block, nodes))
    edge_lanes = (slice(0, LAYER), slice(elements - LAYER, elements))

    def weight(k):
        return lax.convert_element_type(first + k, F32) / total_steps

    loads = [
        pltpu.make_async_copy(src, dst, in_sem.at[i])
        for i, (src, dst) in enumerate(
            ((num_hbm, num), (st_hbm.at[0], st), (tgt_hbm, tgt_raw), (ctl_hbm, ctl_raw), (adj_hbm.at[0], adj_raw))
        )
    ]
    for c in loads[:2]:
        c.start()
    for landing in (rim_in, msg_in, near_in):
        landing[...] = jnp.zeros_like(landing)
    barrier = pltpu.get_barrier_semaphore()
    for d in range(1, n_space):
        pl.semaphore_signal(barrier, inc=1, device_id={"space": lax.rem(me + d, n_space)},
                            device_id_type=pl.DeviceIdType.MESH)
    bits = (n_tm - 1).bit_length()

    def beside(far):
        return jnp.where(t >= far, 1, 0) + jnp.where(t + far < n_tm, 1, 0)

    def greet(sem, far):
        @pl.when(t >= far)
        def _():
            pl.semaphore_signal(sem, inc=1, device_id={"tm": t - far}, device_id_type=pl.DeviceIdType.MESH)

        @pl.when(t + far < n_tm)
        def _():
            pl.semaphore_signal(sem, inc=1, device_id={"tm": t + far}, device_id_type=pl.DeviceIdType.MESH)

    greet(barrier, 1)

    def tell(j):
        if j <= bits:
            greet(ready.at[j - 1], 2 ** (j - 1))

    def hear(j):
        if j <= bits:
            pl.semaphore_wait(ready.at[j - 1], beside(2 ** (j - 1)))

    def pass_on(j):
        hear(j)
        tell(j + 1)

    parts = a_sem.shape[0]
    chunk = nodes // parts
    a_loads = [
        pltpu.make_async_copy(a_hbm.at[pl.ds(i * chunk, chunk)], a_raw.at[pl.ds(i * chunk, chunk)], a_sem.at[i])
        for i in range(parts)
    ]
    outer = [0, parts - 1]
    inner = list(range(1, parts - 1))
    for i in outer + inner:
        a_loads[i].start()
    for c in loads[2:]:
        c.start()

    loads[0].wait()
    stored = num[...]
    own = stored // LAYER * LAYER + stored % EXY * EXY + stored // EXY % EXY
    for i in range(0, elements, LAYER):
        place = lax.broadcasted_iota(jnp.int32, (LAYER, elements), 0) + i
        pt[i : i + LAYER, :] = jnp.where(own == place, 1.0, 0.0).astype(BF16)
    down = jnp.broadcast_to(own.astype(F32), (128, elements)).T
    for i in range(0, elements, 128):
        place = lax.broadcasted_iota(jnp.int32, (elements, 128), 1) + i
        pa[:, i : i + 128] = jnp.where(down == place.astype(F32), 1.0, 0.0).astype(BF16)

    def split(x):
        high = x.astype(BF16)
        return jnp.concatenate([high, (x - high.astype(F32)).astype(BF16)], axis=0)

    def joined(x):
        return x[:nodes] + x[nodes:]

    def across(src, dst, send, recv, side, back=0):
        return pltpu.make_async_remote_copy(
            src_ref=src, dst_ref=dst, send_sem=send, recv_sem=recv,
            device_id={"tm": t - back, "space": me - 1 if side == 0 else me + 1},
            device_id_type=pl.DeviceIdType.MESH,
        )

    def rim_copy(rnd, side, slot):
        return across(rim_out.at[rnd, side], rim_in.at[rnd, slot], rim_send.at[rnd, side], rim_recv.at[rnd, slot],
                      side, 1 if rnd == final else 0)

    def msg_copy(rnd, side, slot):
        return across(msg_out.at[rnd, side], msg_in.at[rnd, slot], msg_send.at[rnd, side], msg_recv.at[rnd, slot], side)

    def near_copy(side, slot):
        return across(near_out.at[side], near_in.at[slot], near_send.at[side], near_recv.at[slot], side)

    def at_side(side):
        return me > 0 if side == 0 else me < n_space - 1

    def start_both(copy):
        for side in (0, 1):
            @pl.when(at_side(side))
            def _():
                copy(side, 1 - side).start()

    def wait_both(copy):
        for side in (0, 1):
            @pl.when(at_side(side))
            def _():
                copy(side, side).wait()

    def send_msg(rnd, base, ahead):
        for side in (0, 1):
            msg_out[rnd, side, 0] = base(side).astype(BF16)
            msg_out[rnd, side, 1] = ahead(side).astype(BF16)
        start_both(functools.partial(msg_copy, rnd))

    def wait_final_rims():
        for side in (0, 1):
            @pl.when(at_side(side) & (t < n_tm - 1))
            def _():
                rim_copy(final, side, side).wait_recv()

            @pl.when(at_side(side) & (t > 0))
            def _():
                rim_copy(final, side, side).wait_send()

    depth = BLOCK * BLOCK
    place_k = lax.broadcasted_iota(jnp.int32, (BLOCK, depth), 1)
    place_r = lax.broadcasted_iota(jnp.int32, (BLOCK, depth), 0)
    sum_rows = jnp.where(place_k // BLOCK == place_r, 1.0, 0.0).astype(BF16)
    sum_groups = jnp.where(place_k % BLOCK == place_r, 1.0, 0.0).astype(BF16)
    sum_rows2 = jnp.concatenate([sum_rows, sum_rows], axis=1)

    def groups(n):
        place_c = lax.broadcasted_iota(jnp.int32, (BLOCK, n), 1) % BLOCK
        return jnp.where(place_c == lax.broadcasted_iota(jnp.int32, (BLOCK, n), 0), 1.0, 0.0).astype(BF16)

    def product(out, into, lanes, right):
        return (a_ref[out, into, lanes] * right[None]).reshape(depth, LAYER)

    def product_pair(out, into, lanes, right):
        (i0, i1), (r0, r1) = into, right
        return (a_ref[out, i0, lanes] * r0[None] + a_ref[out, i1, lanes] * r1[None]).reshape(depth, LAYER)

    def inner_blocks(side):
        return [b for b in blocks if b != edge_rows[side]]

    def apply_inner(side, outs, write):
        lanes = edge_lanes[side]
        b0, b1, b2 = inner_blocks(side)
        if side == 0:
            pair, single = (b0, b1), b2
        else:
            pair, single = (b1, b2), b0
        rp = (r_ref[pair[0], lanes], r_ref[pair[1], lanes])
        rs = r_ref[single, lanes]
        for out in outs:
            q = jnp.concatenate([product_pair(out, pair, lanes, rp), product(out, single, lanes, rs)], axis=0)
            write(out, lanes, dot(sum_rows2, q))

    def transposed(out, into, lanes):
        rows = [i for b in into for i in range(b.start, b.stop)]

        def term(i):
            row = jnp.broadcast_to(gf[i : i + 1, lanes], (BLOCK, LAYER)).astype(BF16)
            return a_ref[i, out, lanes] * row

        pieces = [term(rows[i]) + term(rows[i + 1]) for i in range(0, len(rows), 2)]
        return dot(groups(BLOCK * len(pieces)), jnp.concatenate(pieces, axis=0))

    def near_transposed(side):
        def term(i):
            row = jnp.broadcast_to(far_g[side, i : i + 1], (BLOCK, LAYER)).astype(BF16)
            return near_in[side, i] * row

        pieces = [term(i) + term(i + 1) for i in range(0, BLOCK, 2)]
        return dot(groups(BLOCK * len(pieces)), jnp.concatenate(pieces, axis=0))

    loads[1].wait()
    hist[0] = joined(dot(split(st[...]), pa[...]))
    for side in (0, 1):
        rim_out[0, side] = hist[0, edge_rows[side], edge_lanes[side]].astype(BF16)
    piece = depth // nodes

    def permute(part):
        for i in range(part * chunk, (part + 1) * chunk, piece):
            rows = a_raw[i : i + piece].reshape(depth, elements)
            a_ref[i : i + piece] = dot(rows, pa[...]).astype(BF16).reshape(piece, nodes, elements)

    a_loads[outer[0]].wait()
    permute(outer[0])
    pl.semaphore_wait(barrier, n_space - 1 + beside(1))
    start_both(functools.partial(rim_copy, 0))
    tell(1)
    near_out[0] = a_ref[edge_rows[0], edge_rows[0], edge_lanes[0]]
    a_loads[outer[1]].wait()
    corner = dot(a_raw[edge_rows[1], edge_rows[1]].reshape(depth, elements), pa[:, edge_lanes[1]])
    near_out[1] = corner.astype(BF16).reshape(BLOCK, BLOCK, LAYER)
    start_both(near_copy)

    loads[3].wait()
    for k in range(min(2, steps)):
        ctl[k] = dot(ctl_raw[k], pa[...]).astype(BF16)

    def arrange_later():
        for c in (loads[2], loads[4]):
            c.wait()
        goal[...] = dot(tgt_raw[...], pa[...])
        adj[...] = joined(dot(split(adj_raw[...]), pa[...]))
        for k in range(2, steps):
            ctl[k] = dot(ctl_raw[k], pa[...]).astype(BF16)

    def prepare(k):
        u = hist[k]
        c = ctl[k].astype(F32)
        base = u + TIME_STEP * (u - u * u * u) + TIME_STEP * PENALTY * jumps_inside(u) + TIME_STEP * c
        r_ref[...] = base.astype(BF16)
        for side in (0, 1):
            edge[side] = base[edge_rows[side], edge_lanes[side]]

    def keep(k):
        def write(rows, lanes, v):
            hist[k + 1, rows, lanes] = v

        return write

    def right_edges():
        return [(edge[side] + TIME_STEP * PENALTY * rim[side]).astype(BF16) for side in (0, 1)]

    def step_edges(k, right):
        for side, (rows, lanes) in enumerate(zip(edge_rows, edge_lanes)):
            hist[k + 1, rows, lanes] += dot(sum_rows, product(rows, rows, lanes, right[side]))

    def send_ahead(k):
        send_msg(k, lambda side: edge[side], lambda side: hist[k + 1, edge_rows[side], edge_lanes[side]])

    def far_rims(k):
        for side, (rows, lanes) in enumerate(zip(edge_rows, edge_lanes)):
            far = msg_in[k, side, 0].astype(F32) + TIME_STEP * PENALTY * hist[k, rows, lanes]
            q = (near_in[side] * far.astype(BF16)[None]).reshape(depth, LAYER)
            rim[side] = msg_in[k, side, 1].astype(F32) + dot(sum_rows, q)

    def step_rest(k, right):
        for side, (rows, lanes) in enumerate(zip(edge_rows, edge_lanes)):
            for out in inner_blocks(side):
                hist[k + 1, out, lanes] += dot(sum_rows, product(out, rows, lanes, right[side]))

    prepare(0)
    permute(outer[1])
    for side in (0, 1):
        apply_inner(side, [edge_rows[side]], keep(0))
    if steps > 1:
        send_ahead(0)
    for part in inner:
        a_loads[part].wait()
        permute(part)
    for side in (0, 1):
        apply_inner(side, inner_blocks(side), keep(0))
    wait_both(functools.partial(rim_copy, 0))
    for side in (0, 1):
        rim[side] = rim_in[0, side].astype(F32)
    first_right = right_edges()
    step_edges(0, first_right)
    step_rest(0, first_right)

    def forward(k, carry):
        prepare(k)
        for side in (0, 1):
            apply_inner(side, [edge_rows[side]], keep(k))
        pl.when(k < steps - 1)(functools.partial(send_ahead, k))
        for side in (0, 1):
            apply_inner(side, inner_blocks(side), keep(k))

        @pl.when(k == 1)
        def _():
            arrange_later()
            wait_both(near_copy)

        wait_both(functools.partial(msg_copy, k - 1))
        far_rims(k - 1)
        right = right_edges()
        step_edges(k, right)
        step_rest(k, right)
        pl.when(k == 1)(functools.partial(pass_on, 1))
        pl.when(k == steps - 1)(functools.partial(pass_on, 2))
        return carry

    lax.fori_loop(1, steps, forward, 0)

    w_end = weight(steps)
    u = hist[steps]
    gf[...] = w_end * (u - goal[...]) + adj[...]

    for side, (rows, lanes) in enumerate(zip(edge_rows, edge_lanes)):
        v = transposed(rows, blocks, lanes)
        pulled[rows, lanes] = v
        rim_out[turn, side] = v.astype(BF16)
    start_both(functools.partial(rim_copy, turn))

    def st_copy(dst):
        return pltpu.make_async_remote_copy(
            src_ref=st_out, dst_ref=st_in, send_sem=st_sem.at[0], recv_sem=st_sem.at[1],
            device_id={"tm": dst}, device_id_type=pl.DeviceIdType.MESH)

    def back_copy(i, dst):
        src, land = ((rate_out, rate_in), (adj_out, adj_in), (face_out, face_in))[i]
        return pltpu.make_async_remote_copy(
            src_ref=src, dst_ref=land, send_sem=adj_sem.at[0, i], recv_sem=adj_sem.at[1, i],
            device_id={"tm": dst}, device_id_type=pl.DeviceIdType.MESH)

    def send_back(i):
        @pl.when(t > 0)
        def _():
            back_copy(i, t - 1).start()


    def gather_copy(slots, send, recv, axis, index, count, d):
        return pltpu.make_async_remote_copy(
            src_ref=slots.at[index], dst_ref=slots.at[index], send_sem=send.at[d], recv_sem=recv.at[index],
            device_id={axis: lax.rem(index + d, count)}, device_id_type=pl.DeviceIdType.MESH)

    def gather_wait(slots, send, recv, axis, index, count, d):
        gather_copy(slots, send, recv, axis, index, count, d).wait_send()
        origin = lax.rem(index + d, count)
        pltpu.make_async_remote_copy(
            src_ref=slots.at[origin], dst_ref=slots.at[origin], send_sem=send.at[d], recv_sem=recv.at[origin],
            device_id={axis: origin}, device_id_type=pl.DeviceIdType.MESH).wait_recv()

    over_s = (slot_s, ss_send, ss_recv, "space", me, n_space)

    over_t = (slot_t, tt_send, tt_recv, "tm", t, n_tm)

    def gathered(slots, *rest):
        count = rest[-1]
        for d in range(1, count):
            gather_wait(slots, *rest, d)
        total = slots[0]
        for i in range(1, count):
            total = total + slots[i]
        return total

    def hand_round():
        for j in range(3, bits + 1):
            pass_on(j)
        slot_t[t] = gathered(*over_s)
        for d in range(1, n_tm):
            gather_copy(*over_t, d).start()

    def rate(k):
        before = hist[k]
        return 1.0 + TIME_STEP * (1.0 - 3.0 * before * before)


    for side, lanes in enumerate(edge_lanes):
        for out in inner_blocks(side):
            pulled[out, lanes] = transposed(out, blocks, lanes)

    def carry_back(factor, p):
        return factor * p + TIME_STEP * PENALTY * jumps_inside(p)

    def update(k, p):
        control = ctl[k].astype(F32)
        ctl[k] = (control - (TIME_STEP * p + REGULAR * control)).astype(BF16)

    def turn_chores():
        st_out[...] = hist[steps].astype(BF16)

        @pl.when(t < n_tm - 1)
        def _():
            st_copy(t + 1).start()

        rate_out[...] = rate(0).astype(BF16)
        send_back(0)

        total = jnp.zeros((8, 128), F32)
        for k in range(steps):
            d = hist[k + 1] - goal[...]
            c = ctl[k].astype(F32)
            total += 0.5 * weight(k + 1) * fold(d * d) + 0.5 * REGULAR * fold(c * c)
        slot_s[me] = total
        for d in range(1, n_space):
            gather_copy(*over_s, d).start()

    def backward(i, carry):
        k = steps - 1 - i
        rnd = steps - 1 + i
        p = pulled[...]
        gf[...] = weight(k) * (hist[k] - goal[...]) + carry_back(rate(k), p)
        held[...] = p
        for side, (rows, lanes) in enumerate(zip(edge_rows, edge_lanes)):
            pulled[rows, lanes] = transposed(rows, inner_blocks(side), lanes)

        @pl.when(i < steps - 2)
        def _():
            send_msg(rnd, lambda side: gf[edge_rows[side], edge_lanes[side]],
                     lambda side: pulled[edge_rows[side], edge_lanes[side]])

        pl.when(i == 0)(turn_chores)
        for side, lanes in enumerate(edge_lanes):
            for out in inner_blocks(side):
                pulled[out, lanes] = transposed(out, inner_blocks(side), lanes)

        @pl.when(i == steps - 2)
        def _():
            adj_out[...] = carry_back(rate(0), pulled[...]).astype(BF16)
            send_back(1)

        @pl.when(i == 0)
        def _():
            wait_both(functools.partial(rim_copy, turn))
            for side in (0, 1):
                rim[side] = rim_in[turn, side].astype(F32)

        @pl.when(i > 0)
        def _():
            wait_both(functools.partial(msg_copy, rnd - 1))
            for side in (0, 1):
                far_g[side] = msg_in[rnd - 1, side, 0].astype(F32) + TIME_STEP * PENALTY * prev[side]
            for side in (0, 1):
                rim[side] = msg_in[rnd - 1, side, 1].astype(F32) + near_transposed(side)

        for side, (rows, lanes) in enumerate(zip(edge_rows, edge_lanes)):
            g = gf[rows, lanes] + TIME_STEP * PENALTY * rim[side]
            gf[rows, lanes] = g
            face_out[side] = g.astype(BF16)

        @pl.when(i == steps - 2)
        def _():
            send_back(2)

        for side, (rows, lanes) in enumerate(zip(edge_rows, edge_lanes)):
            pulled[rows, lanes] += transposed(rows, [rows], lanes)

        @pl.when(i == steps - 2)
        def _():
            for side, (rows, lanes) in enumerate(zip(edge_rows, edge_lanes)):
                rim_out[final, side] = pulled[rows, lanes].astype(BF16)

                @pl.when(at_side(side) & (t > 0))
                def _():
                    rim_copy(final, side, 1 - side).start()

        for side, (rows, lanes) in enumerate(zip(edge_rows, edge_lanes)):
            for out in inner_blocks(side):
                pulled[out, lanes] += transposed(out, [rows], lanes)
        for side, (rows, lanes) in enumerate(zip(edge_rows, edge_lanes)):
            prev[side] = held[rows, lanes]
        update(k, held[...])
        pl.when(i == min(1, steps - 2))(hand_round)
        return carry

    lax.fori_loop(0, steps - 1, backward, 0)

    update(0, pulled[...])
    for k in range(steps):
        newc_ref[k] = dot(ctl[k], pt[...]).astype(BF16)

    @pl.when(t == 0)
    def _():
        nst_ref[0] = st[...]

    @pl.when(t > 0)
    def _():
        st_copy(t - 1).wait_recv()
        nst_ref[0] = dot(st_in[...], pt[...])

    @pl.when(t < n_tm - 1)
    def _():
        st_copy(t + 1).wait_send()

    total = gathered(*over_t)
    scaled = total * (1.0 / (total_steps * nodes * elements * n_space))
    obj_ref[...] = jnp.sum(jnp.sum(scaled, axis=0, keepdims=True), axis=1, keepdims=True)

    @pl.when(t == n_tm - 1)
    def _():
        nadj_ref[...] = jnp.zeros_like(nadj_ref)

    @pl.when(t < n_tm - 1)
    def _():
        for i in (0, 2):
            back_copy(i, t + 1).wait_recv()
        for side, (rows, lanes) in enumerate(zip(edge_rows, edge_lanes)):
            gf[rows, lanes] = face_in[side].astype(F32)
        for side, (rows, lanes) in enumerate(zip(edge_rows, edge_lanes)):
            for out in blocks:
                pulled[out, lanes] = transposed(out, [rows], lanes)
        gf[...] = carry_back(rate_in[...].astype(F32), pulled[...])
        back_copy(1, t + 1).wait_recv()

    wait_final_rims()

    @pl.when(t < n_tm - 1)
    def _():
        for side, (rows, lanes) in enumerate(zip(edge_rows, edge_lanes)):
            gf[rows, lanes] += TIME_STEP * PENALTY * rim_in[final, side].astype(F32)
        nadj_ref[0] = joined(dot(split(gf[...] + adj_in[...].astype(F32)), pt[...]))

    @pl.when(t > 0)
    def _():
        for i in range(3):
            back_copy(i, t - 1).wait_send()


def store_kernel(count, *refs):
    gives = [pltpu.make_async_copy(refs[i], refs[count + i], refs[-1].at[i]) for i in range(count)]
    for c in gives:
        c.start()
    for c in gives:
        c.wait()


def store(values):
    count = len(values)
    return pl.pallas_call(
        functools.partial(store_kernel, count),
        out_shape=tuple(jax.ShapeDtypeStruct(v.shape, v.dtype) for v in values),
        in_specs=[pl.BlockSpec(memory_space=pltpu.VMEM)] * count,
        out_specs=(pl.BlockSpec(memory_space=pltpu.HBM),) * count,
        scratch_shapes=[pltpu.SemaphoreType.DMA((count,))],
        compiler_params=pltpu.CompilerParams(vmem_limit_bytes=4194304),
    )(*values)


def solution(mesh):
    n_space, n_tm = mesh.shape["space"], mesh.shape["tm"]

    def per_device(controls, target, state_in, adjoint_in, block_inverse, numbering):
        steps, nodes, elements = controls.shape
        vm = pl.BlockSpec(memory_space=pltpu.VMEM)
        hbm = pl.BlockSpec(memory_space=pltpu.HBM)
        field = (nodes, elements)
        messages = max(2 * steps - 3, 1)
        bits = (n_tm - 1).bit_length()
        dma = pltpu.SemaphoreType.DMA
        new_controls, next_state, next_adjoint, objective = pl.pallas_call(
            functools.partial(kernel, n_space, n_tm),
            out_shape=(
                pltpu.VMEM(controls.shape, BF16),
                pltpu.VMEM(state_in.shape, F32),
                pltpu.VMEM(adjoint_in.shape, F32),
                pltpu.VMEM((1, 1), F32),
            ),
            in_specs=[hbm] * 6,
            out_specs=(vm, vm, vm, vm),
            scratch_shapes=[
                pltpu.VMEM(block_inverse.shape, BF16),
                pltpu.VMEM(block_inverse.shape, BF16),
                pltpu.VMEM(numbering.shape, jnp.int32),
                pltpu.VMEM(controls.shape, BF16),
                pltpu.VMEM(controls.shape, BF16),
                pltpu.VMEM(field, BF16),
                pltpu.VMEM(field, F32),
                pltpu.VMEM(field, F32),
                pltpu.VMEM(field, F32),
                pltpu.VMEM(field, F32),
                pltpu.VMEM((steps + 1,) + field, F32),
                pltpu.VMEM(field, BF16),
                pltpu.VMEM((2, BLOCK, LAYER), F32),
                pltpu.VMEM(field, F32),
                pltpu.VMEM(field, F32),
                pltpu.VMEM((elements, elements), BF16),
                pltpu.VMEM((elements, elements), BF16),
                pltpu.VMEM((3, 2, BLOCK, LAYER), BF16),
                pltpu.VMEM((3, 2, BLOCK, LAYER), BF16),
                pltpu.VMEM((messages, 2, 2, BLOCK, LAYER), BF16),
                pltpu.VMEM((messages, 2, 2, BLOCK, LAYER), BF16),
                pltpu.VMEM((2, BLOCK, BLOCK, LAYER), BF16),
                pltpu.VMEM((2, BLOCK, BLOCK, LAYER), BF16),
                pltpu.VMEM((2, BLOCK, LAYER), F32),
                pltpu.VMEM((2, BLOCK, LAYER), F32),
                pltpu.VMEM((2, BLOCK, LAYER), F32),
                pltpu.VMEM(field, F32),
                pltpu.VMEM(field, BF16),
                pltpu.VMEM(field, BF16),
                pltpu.VMEM(field, BF16),
                pltpu.VMEM(field, BF16),
                pltpu.VMEM(field, BF16),
                pltpu.VMEM(field, BF16),
                pltpu.VMEM((2, BLOCK, LAYER), BF16),
                pltpu.VMEM((2, BLOCK, LAYER), BF16),
                pltpu.VMEM((n_space, 8, 128), F32),
                pltpu.VMEM((n_tm, 8, 128), F32),
                dma((5,)),
                dma((4,)),
                dma((3, 2)),
                dma((3, 2)),
                dma((messages, 2)),
                dma((messages, 2)),
                dma((2,)),
                dma((2,)),
                dma((2,)),
                dma((2, 3)),
                dma((n_space,)),
                dma((n_space,)),
                dma((n_tm,)),
                dma((n_tm,)),
                pltpu.SemaphoreType.REGULAR((bits,)),
            ],
            compiler_params=pltpu.CompilerParams(
                collective_id=0, has_side_effects=True, vmem_limit_bytes=60000000
            ),
        )(numbering, controls, target, state_in, adjoint_in, block_inverse)
        out = store((new_controls, next_state, next_adjoint, objective))
        return out[:3] + (out[3].reshape(()),)

    return jax.shard_map(
        per_device,
        mesh=mesh,
        in_specs=(
            P("tm", None, "space"),
            P(None, "space"),
            P("tm", None, "space"),
            P("tm", None, "space"),
            P(None, None, "space"),
            P("space", None),
        ),
        out_specs=(P("tm", None, "space"), P("tm", None, "space"), P("tm", None, "space"), P()),
        check_vma=False,
    )
```

```python
import functools

import jax
import jax.numpy as jnp
from jax import lax
from jax.experimental import pallas as pl
from jax.experimental.pallas import tpu as pltpu
from jax.sharding import PartitionSpec as P

NSIDE = 4
EXY = 16
BLOCK = NSIDE * NSIDE
LAYER = EXY * EXY
TIME_STEP = 0.1
PENALTY = 0.5
REGULAR = 0.1
F32 = jnp.float32
BF16 = jnp.bfloat16


def dot(a, b):
    return jnp.dot(a, b, preferred_element_type=F32)


def fold(x):
    total = None
    for i in range(0, x.shape[0], 8):
        for j in range(0, x.shape[1], 128):
            piece = x[i : i + 8, j : j + 128]
            total = piece if total is None else total + piece
    return total


def lateral(x):
    nodes, elements = x.shape
    last = NSIDE - 1

    def by_layer(y, shift):
        return jnp.concatenate(
            [pltpu.roll(y[:, i : i + LAYER], shift, 1) for i in range(0, elements, LAYER)], axis=1
        )

    a = lax.broadcasted_iota(jnp.int32, x.shape, 0) % NSIDE
    y = jnp.where(a == last, by_layer(x, EXY), by_layer(x, LAYER - EXY)).reshape(nodes // 8, 8, elements)
    to_low = pltpu.roll(y, 8 - last, 1).reshape(nodes, elements)
    to_high = pltpu.roll(y, last, 1).reshape(nodes, elements)
    along_a = jnp.where(a == 0, to_low, jnp.where(a == last, to_high, 0.0))

    count = nodes // BLOCK
    tall = x.reshape(count, 2, 8, elements)
    low3 = lax.broadcasted_iota(jnp.int32, (count, 8, elements), 1) < NSIDE
    w = jnp.where(low3, tall[:, 0], tall[:, 1]).reshape(count * 8, elements)
    low2 = lax.broadcasted_iota(jnp.int32, w.shape, 0) % 8 < NSIDE
    row = lax.broadcasted_iota(jnp.int32, w.shape, 1) % EXY
    down = jnp.where(row == 0, pltpu.roll(w, elements - EXY + 1, 1), pltpu.roll(w, 1, 1))
    up = jnp.where(row == EXY - 1, pltpu.roll(w, EXY - 1, 1), pltpu.roll(w, elements - 1, 1))
    r = pltpu.roll(jnp.where(low2, up, down).reshape(count, 8, elements), NSIDE, 1)
    first, second = jnp.where(low3, r, 0.0), jnp.where(low3, 0.0, r)
    along_b = jnp.concatenate([v for i in range(count) for v in (first[i], second[i])], axis=0)
    return along_a + along_b


def face_count(shape):
    q = lax.broadcasted_iota(jnp.int32, shape, 0)
    count = jnp.zeros(shape, F32)
    for step in (1, NSIDE, BLOCK):
        at = (q // step) % NSIDE
        count += jnp.where((at == 0) | (at == NSIDE - 1), 1.0, 0.0)
    return count


def jumps_inside(x):
    nodes, elements = x.shape
    low, high = slice(0, BLOCK), slice(nodes - BLOCK, nodes)
    empty = jnp.zeros((BLOCK, LAYER), F32)
    below = jnp.concatenate([empty, x[high, : elements - LAYER]], axis=1)
    above = jnp.concatenate([x[low, LAYER:], empty], axis=1)
    middle = jnp.zeros((nodes - 2 * BLOCK, elements), F32)
    return lateral(x) + jnp.concatenate([below, middle, above], axis=0) - face_count(x.shape) * x


def kernel(
    n_space, n_tm,
    num_hbm, ctl_hbm, tgt_hbm, st_hbm, adj_hbm, a_hbm,
    newc_ref, nst_ref, nadj_ref, obj_ref,
    a_raw, a_ref, num, ctl_raw, ctl, tgt_raw, goal, adj_raw, adj, st, hist, r_ref, edge, gf, pulled, pa, pt,
    rim_out, rim_in, msg_out, msg_in, near_out, near_in, rim, prev, far_g, held, st_out, st_in, adj_out, adj_in, rate_out, rate_in, face_out, face_in, slot_s, slot_t,
    in_sem, a_sem, rim_send, rim_recv, msg_send, msg_recv, near_send, near_recv, st_sem, adj_sem,
    ss_send, ss_recv, tt_send, tt_recv, ready,
):
    steps, nodes, elements = ctl.shape
    me = lax.axis_index("space")
    t = lax.axis_index("tm")
    first = t * steps
    total_steps = steps * n_tm
    turn, final = 1, 2
    last_block = nodes - BLOCK
    blocks = [slice(s, s + BLOCK) for s in range(0, nodes, BLOCK)]
    edge_rows = (slice(0, BLOCK), slice(last_block, nodes))
    edge_lanes = (slice(0, LAYER), slice(elements - LAYER, elements))

    def weight(k):
        return lax.convert_element_type(first + k, F32) / total_steps

    loads = [
        pltpu.make_async_copy(src, dst, in_sem.at[i])
        for i, (src, dst) in enumerate(
            ((num_hbm, num), (st_hbm.at[0], st), (tgt_hbm, tgt_raw), (ctl_hbm, ctl_raw), (adj_hbm.at[0], adj_raw))
        )
    ]
    for c in loads[:2]:
        c.start()
    parts = a_sem.shape[0]
    chunk = nodes // parts
    a_loads = [
        pltpu.make_async_copy(a_hbm.at[pl.ds(i * chunk, chunk)], a_raw.at[pl.ds(i * chunk, chunk)], a_sem.at[i])
        for i in range(parts)
    ]
    outer = [0, parts - 1]
    inner = list(range(1, parts - 1))
    for i in outer + inner:
        a_loads[i].start()
    for c in loads[2:]:
        c.start()
    for landing in (rim_in, msg_in, near_in):
        landing[...] = jnp.zeros_like(landing)
    barrier = pltpu.get_barrier_semaphore()
    for d in range(1, n_space):
        pl.semaphore_signal(barrier, inc=1, device_id={"space": lax.rem(me + d, n_space)},
                            device_id_type=pl.DeviceIdType.MESH)
    bits = (n_tm - 1).bit_length()

    def beside(far):
        return jnp.where(t >= far, 1, 0) + jnp.where(t + far < n_tm, 1, 0)

    def greet(sem, far):
        @pl.when(t >= far)
        def _():
            pl.semaphore_signal(sem, inc=1, device_id={"tm": t - far}, device_id_type=pl.DeviceIdType.MESH)

        @pl.when(t + far < n_tm)
        def _():
            pl.semaphore_signal(sem, inc=1, device_id={"tm": t + far}, device_id_type=pl.DeviceIdType.MESH)

    greet(barrier, 1)

    def tell(j):
        if j <= bits:
            greet(ready.at[j - 1], 2 ** (j - 1))

    def hear(j):
        if j <= bits:
            pl.semaphore_wait(ready.at[j - 1], beside(2 ** (j - 1)))

    def pass_on(j):
        hear(j)
        tell(j + 1)


    loads[0].wait()
    stored = num[...]
    own = stored // LAYER * LAYER + stored % EXY * EXY + stored // EXY % EXY
    for i in range(0, elements, LAYER):
        place = lax.broadcasted_iota(jnp.int32, (LAYER, elements), 0) + i
        pt[i : i + LAYER, :] = jnp.where(own == place, 1.0, 0.0).astype(BF16)
    down = jnp.broadcast_to(own.astype(F32), (128, elements)).T
    for i in range(0, elements, 128):
        place = lax.broadcasted_iota(jnp.int32, (elements, 128), 1) + i
        pa[:, i : i + 128] = jnp.where(down == place.astype(F32), 1.0, 0.0).astype(BF16)

    def split(x):
        high = x.astype(BF16)
        return jnp.concatenate([high, (x - high.astype(F32)).astype(BF16)], axis=0)

    def joined(x):
        return x[:nodes] + x[nodes:]

    def across(src, dst, send, recv, side, back=0):
        return pltpu.make_async_remote_copy(
            src_ref=src, dst_ref=dst, send_sem=send, recv_sem=recv,
            device_id={"tm": t - back, "space": me - 1 if side == 0 else me + 1},
            device_id_type=pl.DeviceIdType.MESH,
        )

    def rim_copy(rnd, side, slot):
        return across(rim_out.at[rnd, side], rim_in.at[rnd, slot], rim_send.at[rnd, side], rim_recv.at[rnd, slot],
                      side, 1 if rnd == final else 0)

    def msg_copy(rnd, side, slot):
        return across(msg_out.at[rnd, side], msg_in.at[rnd, slot], msg_send.at[rnd, side], msg_recv.at[rnd, slot], side)

    def near_copy(side, slot):
        return across(near_out.at[side], near_in.at[slot], near_send.at[side], near_recv.at[slot], side)

    def at_side(side):
        return me > 0 if side == 0 else me < n_space - 1

    def start_both(copy):
        for side in (0, 1):
            @pl.when(at_side(side))
            def _():
                copy(side, 1 - side).start()

    def wait_both(copy):
        for side in (0, 1):
            @pl.when(at_side(side))
            def _():
                copy(side, side).wait()

    def send_msg(rnd, base, ahead):
        for side in (0, 1):
            msg_out[rnd, side, 0] = base(side).astype(BF16)
            msg_out[rnd, side, 1] = ahead(side).astype(BF16)
        start_both(functools.partial(msg_copy, rnd))

    def wait_final_rims():
        for side in (0, 1):
            @pl.when(at_side(side) & (t < n_tm - 1))
            def _():
                rim_copy(final, side, side).wait_recv()

            @pl.when(at_side(side) & (t > 0))
            def _():
                rim_copy(final, side, side).wait_send()

    depth = BLOCK * BLOCK
    place_k = lax.broadcasted_iota(jnp.int32, (BLOCK, depth), 1)
    place_r = lax.broadcasted_iota(jnp.int32, (BLOCK, depth), 0)
    sum_rows = jnp.where(place_k // BLOCK == place_r, 1.0, 0.0).astype(BF16)
    sum_groups = jnp.where(place_k % BLOCK == place_r, 1.0, 0.0).astype(BF16)
    sum_rows2 = jnp.concatenate([sum_rows, sum_rows], axis=1)

    def groups(n):
        place_c = lax.broadcasted_iota(jnp.int32, (BLOCK, n), 1) % BLOCK
        return jnp.where(place_c == lax.broadcasted_iota(jnp.int32, (BLOCK, n), 0), 1.0, 0.0).astype(BF16)

    def product(out, into, lanes, right):
        return (a_ref[out, into, lanes] * right[None]).reshape(depth, LAYER)

    def product_pair(out, into, lanes, right):
        (i0, i1), (r0, r1) = into, right
        return (a_ref[out, i0, lanes] * r0[None] + a_ref[out, i1, lanes] * r1[None]).reshape(depth, LAYER)

    def inner_blocks(side):
        return [b for b in blocks if b != edge_rows[side]]

    def apply_inner(side, outs, write):
        lanes = edge_lanes[side]
        b0, b1, b2 = inner_blocks(side)
        if side == 0:
            pair, single = (b0, b1), b2
        else:
            pair, single = (b1, b2), b0
        rp = (r_ref[pair[0], lanes], r_ref[pair[1], lanes])
        rs = r_ref[single, lanes]
        for out in outs:
            q = jnp.concatenate([product_pair(out, pair, lanes, rp), product(out, single, lanes, rs)], axis=0)
            write(out, lanes, dot(sum_rows2, q))

    def transposed(out, into, lanes):
        rows = [i for b in into for i in range(b.start, b.stop)]

        def term(i):
            row = jnp.broadcast_to(gf[i : i + 1, lanes], (BLOCK, LAYER)).astype(BF16)
            return a_ref[i, out, lanes] * row

        pieces = [term(rows[i]) + term(rows[i + 1]) for i in range(0, len(rows), 2)]
        return dot(groups(BLOCK * len(pieces)), jnp.concatenate(pieces, axis=0))

    def near_transposed(side):
        def term(i):
            row = jnp.broadcast_to(far_g[side, i : i + 1], (BLOCK, LAYER)).astype(BF16)
            return near_in[side, i] * row

        pieces = [term(i) + term(i + 1) for i in range(0, BLOCK, 2)]
        return dot(groups(BLOCK * len(pieces)), jnp.concatenate(pieces, axis=0))

    loads[1].wait()
    hist[0] = joined(dot(split(st[...]), pa[...]))
    for side in (0, 1):
        rim_out[0, side] = hist[0, edge_rows[side], edge_lanes[side]].astype(BF16)
    piece = depth // nodes

    def permute(part):
        for i in range(part * chunk, (part + 1) * chunk, piece):
            rows = a_raw[i : i + piece].reshape(depth, elements)
            a_ref[i : i + piece] = dot(rows, pa[...]).astype(BF16).reshape(piece, nodes, elements)

    a_loads[outer[0]].wait()
    permute(outer[0])
    pl.semaphore_wait(barrier, n_space - 1 + beside(1))
    start_both(functools.partial(rim_copy, 0))
    tell(1)
    near_out[0] = a_ref[edge_rows[0], edge_rows[0], edge_lanes[0]]
    a_loads[outer[1]].wait()
    corner = dot(a_raw[edge_rows[1], edge_rows[1]].reshape(depth, elements), pa[:, edge_lanes[1]])
    near_out[1] = corner.astype(BF16).reshape(BLOCK, BLOCK, LAYER)
    start_both(near_copy)

    loads[3].wait()
    for k in range(min(2, steps)):
        ctl[k] = dot(ctl_raw[k], pa[...]).astype(BF16)

    def arrange_later():
        for c in (loads[2], loads[4]):
            c.wait()
        goal[...] = dot(tgt_raw[...], pa[...])
        adj[...] = joined(dot(split(adj_raw[...]), pa[...]))
        for k in range(2, steps):
            ctl[k] = dot(ctl_raw[k], pa[...]).astype(BF16)

    def prepare(k):
        u = hist[k]
        c = ctl[k].astype(F32)
        base = u + TIME_STEP * (u - u * u * u) + TIME_STEP * PENALTY * jumps_inside(u) + TIME_STEP * c
        r_ref[...] = base.astype(BF16)
        for side in (0, 1):
            edge[side] = base[edge_rows[side], edge_lanes[side]]

    def keep(k):
        def write(rows, lanes, v):
            hist[k + 1, rows, lanes] = v

        return write

    def right_edges():
        return [(edge[side] + TIME_STEP * PENALTY * rim[side]).astype(BF16) for side in (0, 1)]

    def step_edges(k, right):
        for side, (rows, lanes) in enumerate(zip(edge_rows, edge_lanes)):
            hist[k + 1, rows, lanes] += dot(sum_rows, product(rows, rows, lanes, right[side]))

    def send_ahead(k):
        send_msg(k, lambda side: edge[side], lambda side: hist[k + 1, edge_rows[side], edge_lanes[side]])

    def far_rims(k):
        for side, (rows, lanes) in enumerate(zip(edge_rows, edge_lanes)):
            far = msg_in[k, side, 0].astype(F32) + TIME_STEP * PENALTY * hist[k, rows, lanes]
            q = (near_in[side] * far.astype(BF16)[None]).reshape(depth, LAYER)
            rim[side] = msg_in[k, side, 1].astype(F32) + dot(sum_rows, q)

    def step_rest(k, right):
        for side, (rows, lanes) in enumerate(zip(edge_rows, edge_lanes)):
            for out in inner_blocks(side):
                hist[k + 1, out, lanes] += dot(sum_rows, product(out, rows, lanes, right[side]))

    prepare(0)
    permute(outer[1])
    for side in (0, 1):
        apply_inner(side, [edge_rows[side]], keep(0))
    if steps > 1:
        send_ahead(0)
    for part in inner:
        a_loads[part].wait()
        permute(part)
    for side in (0, 1):
        apply_inner(side, inner_blocks(side), keep(0))
    wait_both(functools.partial(rim_copy, 0))
    for side in (0, 1):
        rim[side] = rim_in[0, side].astype(F32)
    first_right = right_edges()
    step_edges(0, first_right)
    step_rest(0, first_right)

    def forward(k, carry):
        prepare(k)
        for side in (0, 1):
            apply_inner(side, [edge_rows[side]], keep(k))
        pl.when(k < steps - 1)(functools.partial(send_ahead, k))
        for side in (0, 1):
            apply_inner(side, inner_blocks(side), keep(k))

        @pl.when(k == 1)
        def _():
            arrange_later()
            wait_both(near_copy)

        wait_both(functools.partial(msg_copy, k - 1))
        far_rims(k - 1)
        right = right_edges()
        step_edges(k, right)
        step_rest(k, right)
        pl.when(k == 1)(functools.partial(pass_on, 1))
        pl.when(k == steps - 1)(functools.partial(pass_on, 2))
        return carry

    lax.fori_loop(1, steps, forward, 0)

    w_end = weight(steps)
    u = hist[steps]
    gf[...] = w_end * (u - goal[...]) + adj[...]

    for side, (rows, lanes) in enumerate(zip(edge_rows, edge_lanes)):
        v = transposed(rows, blocks, lanes)
        pulled[rows, lanes] = v
        rim_out[turn, side] = v.astype(BF16)
    start_both(functools.partial(rim_copy, turn))

    st_out[...] = hist[steps].astype(BF16)

    def st_copy(dst):
        return pltpu.make_async_remote_copy(
            src_ref=st_out, dst_ref=st_in, send_sem=st_sem.at[0], recv_sem=st_sem.at[1],
            device_id={"tm": dst}, device_id_type=pl.DeviceIdType.MESH)

    def back_copy(i, dst):
        src, land = ((rate_out, rate_in), (adj_out, adj_in), (face_out, face_in))[i]
        return pltpu.make_async_remote_copy(
            src_ref=src, dst_ref=land, send_sem=adj_sem.at[0, i], recv_sem=adj_sem.at[1, i],
            device_id={"tm": dst}, device_id_type=pl.DeviceIdType.MESH)

    def send_back(i):
        @pl.when(t > 0)
        def _():
            back_copy(i, t - 1).start()


    def gather_copy(slots, send, recv, axis, index, count, d):
        return pltpu.make_async_remote_copy(
            src_ref=slots.at[index], dst_ref=slots.at[index], send_sem=send.at[d], recv_sem=recv.at[index],
            device_id={axis: lax.rem(index + d, count)}, device_id_type=pl.DeviceIdType.MESH)

    def gather_wait(slots, send, recv, axis, index, count, d):
        gather_copy(slots, send, recv, axis, index, count, d).wait_send()
        origin = lax.rem(index + d, count)
        pltpu.make_async_remote_copy(
            src_ref=slots.at[origin], dst_ref=slots.at[origin], send_sem=send.at[d], recv_sem=recv.at[origin],
            device_id={axis: origin}, device_id_type=pl.DeviceIdType.MESH).wait_recv()

    over_s = (slot_s, ss_send, ss_recv, "space", me, n_space)

    over_t = (slot_t, tt_send, tt_recv, "tm", t, n_tm)

    def gathered(slots, *rest):
        count = rest[-1]
        for d in range(1, count):
            gather_wait(slots, *rest, d)
        total = slots[0]
        for i in range(1, count):
            total = total + slots[i]
        return total

    def hand_round():
        for j in range(3, bits + 1):
            pass_on(j)
        slot_t[t] = gathered(*over_s)
        for d in range(1, n_tm):
            gather_copy(*over_t, d).start()

    def rate(k):
        before = hist[k]
        return 1.0 + TIME_STEP * (1.0 - 3.0 * before * before)


    @pl.when(t < n_tm - 1)
    def _():
        st_copy(t + 1).start()

    rate_out[...] = rate(0).astype(BF16)
    send_back(0)

    for side, lanes in enumerate(edge_lanes):
        for out in inner_blocks(side):
            pulled[out, lanes] = transposed(out, blocks, lanes)

    total = jnp.zeros((8, 128), F32)
    for k in range(steps):
        d = hist[k + 1] - goal[...]
        c = ctl[k].astype(F32)
        total += 0.5 * weight(k + 1) * fold(d * d) + 0.5 * REGULAR * fold(c * c)
    slot_s[me] = total
    for d in range(1, n_space):
        gather_copy(*over_s, d).start()

    def carry_back(factor, p):
        return factor * p + TIME_STEP * PENALTY * jumps_inside(p)

    def update(k, p):
        control = ctl[k].astype(F32)
        ctl[k] = (control - (TIME_STEP * p + REGULAR * control)).astype(BF16)

    def backward(i, carry):
        k = steps - 1 - i
        rnd = steps - 1 + i
        p = pulled[...]
        gf[...] = weight(k) * (hist[k] - goal[...]) + carry_back(rate(k), p)
        held[...] = p
        for side, (rows, lanes) in enumerate(zip(edge_rows, edge_lanes)):
            pulled[rows, lanes] = transposed(rows, inner_blocks(side), lanes)

        @pl.when(i < steps - 2)
        def _():
            send_msg(rnd, lambda side: gf[edge_rows[side], edge_lanes[side]],
                     lambda side: pulled[edge_rows[side], edge_lanes[side]])

        for side, lanes in enumerate(edge_lanes):
            for out in inner_blocks(side):
                pulled[out, lanes] = transposed(out, inner_blocks(side), lanes)

        @pl.when(i == steps - 2)
        def _():
            adj_out[...] = carry_back(rate(0), pulled[...]).astype(BF16)
            send_back(1)

        @pl.when(i == 0)
        def _():
            wait_both(functools.partial(rim_copy, turn))
            for side in (0, 1):
                rim[side] = rim_in[turn, side].astype(F32)

        @pl.when(i > 0)
        def _():
            wait_both(functools.partial(msg_copy, rnd - 1))
            for side in (0, 1):
                far_g[side] = msg_in[rnd - 1, side, 0].astype(F32) + TIME_STEP * PENALTY * prev[side]
            for side in (0, 1):
                rim[side] = msg_in[rnd - 1, side, 1].astype(F32) + near_transposed(side)

        for side, (rows, lanes) in enumerate(zip(edge_rows, edge_lanes)):
            g = gf[rows, lanes] + TIME_STEP * PENALTY * rim[side]
            gf[rows, lanes] = g
            face_out[side] = g.astype(BF16)

        @pl.when(i == steps - 2)
        def _():
            send_back(2)

        for side, (rows, lanes) in enumerate(zip(edge_rows, edge_lanes)):
            pulled[rows, lanes] += transposed(rows, [rows], lanes)

        @pl.when(i == steps - 2)
        def _():
            for side, (rows, lanes) in enumerate(zip(edge_rows, edge_lanes)):
                rim_out[final, side] = pulled[rows, lanes].astype(BF16)

                @pl.when(at_side(side) & (t > 0))
                def _():
                    rim_copy(final, side, 1 - side).start()

        for side, (rows, lanes) in enumerate(zip(edge_rows, edge_lanes)):
            for out in inner_blocks(side):
                pulled[out, lanes] += transposed(out, [rows], lanes)
        for side, (rows, lanes) in enumerate(zip(edge_rows, edge_lanes)):
            prev[side] = held[rows, lanes]
        update(k, held[...])
        pl.when(i == min(1, steps - 2))(hand_round)
        return carry

    lax.fori_loop(0, steps - 1, backward, 0)

    update(0, pulled[...])
    for k in range(steps):
        newc_ref[k] = dot(ctl[k], pt[...]).astype(BF16)

    @pl.when(t == 0)
    def _():
        nst_ref[0] = st[...]

    @pl.when(t > 0)
    def _():
        st_copy(t - 1).wait_recv()
        nst_ref[0] = dot(st_in[...], pt[...])

    @pl.when(t < n_tm - 1)
    def _():
        st_copy(t + 1).wait_send()

    total = gathered(*over_t)
    scaled = total * (1.0 / (total_steps * nodes * elements * n_space))
    obj_ref[...] = jnp.sum(jnp.sum(scaled, axis=0, keepdims=True), axis=1, keepdims=True)

    @pl.when(t == n_tm - 1)
    def _():
        nadj_ref[...] = jnp.zeros_like(nadj_ref)

    @pl.when(t < n_tm - 1)
    def _():
        for i in (0, 2):
            back_copy(i, t + 1).wait_recv()
        for side, (rows, lanes) in enumerate(zip(edge_rows, edge_lanes)):
            gf[rows, lanes] = face_in[side].astype(F32)
        for side, (rows, lanes) in enumerate(zip(edge_rows, edge_lanes)):
            for out in blocks:
                pulled[out, lanes] = transposed(out, [rows], lanes)
        gf[...] = carry_back(rate_in[...].astype(F32), pulled[...])
        back_copy(1, t + 1).wait_recv()

    wait_final_rims()

    @pl.when(t < n_tm - 1)
    def _():
        for side, (rows, lanes) in enumerate(zip(edge_rows, edge_lanes)):
            gf[rows, lanes] += TIME_STEP * PENALTY * rim_in[final, side].astype(F32)
        nadj_ref[0] = joined(dot(split(gf[...] + adj_in[...].astype(F32)), pt[...]))

    @pl.when(t > 0)
    def _():
        for i in range(3):
            back_copy(i, t - 1).wait_send()


def store_kernel(count, *refs):
    gives = [pltpu.make_async_copy(refs[i], refs[count + i], refs[-1].at[i]) for i in range(count)]
    for c in gives:
        c.start()
    for c in gives:
        c.wait()


def store(values):
    count = len(values)
    return pl.pallas_call(
        functools.partial(store_kernel, count),
        out_shape=tuple(jax.ShapeDtypeStruct(v.shape, v.dtype) for v in values),
        in_specs=[pl.BlockSpec(memory_space=pltpu.VMEM)] * count,
        out_specs=(pl.BlockSpec(memory_space=pltpu.HBM),) * count,
        scratch_shapes=[pltpu.SemaphoreType.DMA((count,))],
        compiler_params=pltpu.CompilerParams(vmem_limit_bytes=4194304),
    )(*values)


def solution(mesh):
    n_space, n_tm = mesh.shape["space"], mesh.shape["tm"]

    def per_device(controls, target, state_in, adjoint_in, block_inverse, numbering):
        steps, nodes, elements = controls.shape
        vm = pl.BlockSpec(memory_space=pltpu.VMEM)
        hbm = pl.BlockSpec(memory_space=pltpu.HBM)
        field = (nodes, elements)
        messages = max(2 * steps - 3, 1)
        bits = (n_tm - 1).bit_length()
        dma = pltpu.SemaphoreType.DMA
        new_controls, next_state, next_adjoint, objective = pl.pallas_call(
            functools.partial(kernel, n_space, n_tm),
            out_shape=(
                pltpu.VMEM(controls.shape, BF16),
                pltpu.VMEM(state_in.shape, F32),
                pltpu.VMEM(adjoint_in.shape, F32),
                pltpu.VMEM((1, 1), F32),
            ),
            in_specs=[hbm] * 6,
            out_specs=(vm, vm, vm, vm),
            scratch_shapes=[
                pltpu.VMEM(block_inverse.shape, BF16),
                pltpu.VMEM(block_inverse.shape, BF16),
                pltpu.VMEM(numbering.shape, jnp.int32),
                pltpu.VMEM(controls.shape, BF16),
                pltpu.VMEM(controls.shape, BF16),
                pltpu.VMEM(field, BF16),
                pltpu.VMEM(field, F32),
                pltpu.VMEM(field, F32),
                pltpu.VMEM(field, F32),
                pltpu.VMEM(field, F32),
                pltpu.VMEM((steps + 1,) + field, F32),
                pltpu.VMEM(field, BF16),
                pltpu.VMEM((2, BLOCK, LAYER), F32),
                pltpu.VMEM(field, F32),
                pltpu.VMEM(field, F32),
                pltpu.VMEM((elements, elements), BF16),
                pltpu.VMEM((elements, elements), BF16),
                pltpu.VMEM((3, 2, BLOCK, LAYER), BF16),
                pltpu.VMEM((3, 2, BLOCK, LAYER), BF16),
                pltpu.VMEM((messages, 2, 2, BLOCK, LAYER), BF16),
                pltpu.VMEM((messages, 2, 2, BLOCK, LAYER), BF16),
                pltpu.VMEM((2, BLOCK, BLOCK, LAYER), BF16),
                pltpu.VMEM((2, BLOCK, BLOCK, LAYER), BF16),
                pltpu.VMEM((2, BLOCK, LAYER), F32),
                pltpu.VMEM((2, BLOCK, LAYER), F32),
                pltpu.VMEM((2, BLOCK, LAYER), F32),
                pltpu.VMEM(field, F32),
                pltpu.VMEM(field, BF16),
                pltpu.VMEM(field, BF16),
                pltpu.VMEM(field, BF16),
                pltpu.VMEM(field, BF16),
                pltpu.VMEM(field, BF16),
                pltpu.VMEM(field, BF16),
                pltpu.VMEM((2, BLOCK, LAYER), BF16),
                pltpu.VMEM((2, BLOCK, LAYER), BF16),
                pltpu.VMEM((n_space, 8, 128), F32),
                pltpu.VMEM((n_tm, 8, 128), F32),
                dma((5,)),
                dma((4,)),
                dma((3, 2)),
                dma((3, 2)),
                dma((messages, 2)),
                dma((messages, 2)),
                dma((2,)),
                dma((2,)),
                dma((2,)),
                dma((2, 3)),
                dma((n_space,)),
                dma((n_space,)),
                dma((n_tm,)),
                dma((n_tm,)),
                pltpu.SemaphoreType.REGULAR((bits,)),
            ],
            compiler_params=pltpu.CompilerParams(
                collective_id=0, has_side_effects=True, vmem_limit_bytes=60000000
            ),
        )(numbering, controls, target, state_in, adjoint_in, block_inverse)
        out = store((new_controls, next_state, next_adjoint, objective))
        return out[:3] + (out[3].reshape(()),)

    return jax.shard_map(
        per_device,
        mesh=mesh,
        in_specs=(
            P("tm", None, "space"),
            P(None, "space"),
            P("tm", None, "space"),
            P("tm", None, "space"),
            P(None, None, "space"),
            P("space", None),
        ),
        out_specs=(P("tm", None, "space"), P("tm", None, "space"), P("tm", None, "space"), P()),
        check_vma=False,
    )
```
